32 devices in a mesh: dp: 16 (over z, y, core), tensor: 2 (over x).
Axes of the slice: x: 2, y: 2, z: 4, core: 2. Of those that a mesh axis runs over, the one named last changes fastest.
Arguments:
- inputs: bfloat16 [8192, 2048], P(('dp', 'tensor')), may hold values from -6 to 6
- ln_gain: bfloat16 [2048], P('dp'), may hold values from 0.5 to 1.5
- ln_bias: bfloat16 [2048], P('dp'), may hold values from -3 to 3
- qkv_weight: bfloat16 [3, 2048, 2048], P(None, 'dp', 'tensor'), may hold values from -0.125 to 0.125
- out_weight: bfloat16 [2048, 2048], P('dp', 'tensor'), may hold values from -0.75 to 0.75
- fc1_weight: bfloat16 [2048, 8192], P('dp', 'tensor'), may hold values from -0.125 to 0.125
- fc2_weight: bfloat16 [2048, 8192], P('dp', 'tensor'), may hold values from -0.0625 to 0.0625
- cotangent: bfloat16 [8192, 2048], P(('dp', 'tensor')), may hold values from -6 to 6
- m_gain: float32 [2048], P('dp'), may hold values from -78 to 78
- v_gain: float32 [2048], P('dp'), may hold values from 250 to 2500
- m_bias: float32 [2048], P('dp'), may hold values from -78 to 78
- v_bias: float32 [2048], P('dp'), may hold values from 250 to 2500
- m_qkv: float32 [3, 2048, 2048], P(None, 'dp', 'tensor'), may hold values from -9 to 9
- v_qkv: float32 [3, 2048, 2048], P(None, 'dp', 'tensor'), may hold values from 3 to 30
- m_out: float32 [2048, 2048], P('dp', 'tensor'), may hold values from -18 to 18
- v_out: float32 [2048, 2048], P('dp', 'tensor'), may hold values from 10 to 100
- m_fc1: float32 [2048, 8192], P('dp', 'tensor'), may hold values from -24 to 24
- v_fc1: float32 [2048, 8192], P('dp', 'tensor'), may hold values from 25 to 250
- m_fc2: float32 [2048, 8192], P('dp', 'tensor'), may hold values from -48 to 48
- v_fc2: float32 [2048, 8192], P('dp', 'tensor'), may hold values from 80 to 800
Outputs:
- output: bfloat16 [8192, 2048], P(('dp', 'tensor'))
- input_grad: float32 [8192, 2048], P(('dp', 'tensor'))
- gain_grad: float32 [2048], P('dp')
- gain_update: float32 [2048], P('dp')
- gain_m: float32 [2048], P('dp')
- gain_v: float32 [2048], P('dp')
- bias_grad: float32 [2048], P('dp')
- bias_update: float32 [2048], P('dp')
- bias_m: float32 [2048], P('dp')
- bias_v: float32 [2048], P('dp')
- qkv_grad: float32 [3, 2048, 2048], P(None, 'dp', 'tensor')
- qkv_update: float32 [3, 2048, 2048], P(None, 'dp', 'tensor')
- qkv_m: float32 [3, 2048, 2048], P(None, 'dp', 'tensor')
- qkv_v: float32 [3, 2048, 2048], P(None, 'dp', 'tensor')
- out_grad: float32 [2048, 2048], P('dp', 'tensor')
- out_update: float32 [2048, 2048], P('dp', 'tensor')
- out_m: float32 [2048, 2048], P('dp', 'tensor')
- out_v: float32 [2048, 2048], P('dp', 'tensor')
- fc1_grad: float32 [2048, 8192], P('dp', 'tensor')
- fc1_update: float32 [2048, 8192], P('dp', 'tensor')
- fc1_m: float32 [2048, 8192], P('dp', 'tensor')
- fc1_v: float32 [2048, 8192], P('dp', 'tensor')
- fc2_grad: float32 [2048, 8192], P('dp', 'tensor')
- fc2_update: float32 [2048, 8192], P('dp', 'tensor')
- fc2_m: float32 [2048, 8192], P('dp', 'tensor')
- fc2_v: float32 [2048, 8192], P('dp', 'tensor')
The draws below stay inside these ranges and needn't reach their ends.
All inputs are finite; a program needn't handle non-finite values.
Results may differ from the reference program's by a relative error of at most 0.0085.
The reference program's roundings to bfloat16 on the way count: a program that leaves them out, or rounds other values in their place, can miss the bound.
Values may be sent and summed in bfloat16 or wider, within the bound.
No kernel may reach another device: no remote copies, remote signals or barrier semaphores. Data moves between devices by JAX's collectives and lax.ppermute only.
A program may use at most 320 MiB of HBM per device.

```python
import math
import jax
import jax.numpy as jnp
from jax import lax

D = 2048
HEADS = 32
HEAD = 64
ROT = 32
FF = 8192
TOK_DP = 512
TOKENS = 8192
N_DP = 16


def block_levels(key, extent, pieces, low, largest):
    loudness, own = 1.0, jax.random.fold_in(key, 6)
    for dim, shards_of in pieces:
        heights = jnp.exp(jax.random.uniform(jax.random.fold_in(own, dim), (shards_of,), jnp.float32, low / len(pieces), largest / len(pieces)))
        loudness = loudness * jnp.repeat(heights, extent[dim] // shards_of).reshape([-1 if axis == dim else 1 for axis in range(len(extent))])
    return loudness


def gaussian(key, extent, scale, bound, pieces=(), held_as=jnp.bfloat16):
    array = jax.random.normal(key, extent, jnp.float32) * scale
    if len(pieces) > 0:
        array = block_levels(key, extent, pieces, -0.22, 0.18) * array
    return jnp.clip(array, min=-bound, max=bound).astype(held_as)


def setup_inputs(seed: int = 0) -> dict:
    seeds = jax.random.split(jax.random.key(seed), 21)
    inputs = gaussian(seeds[0], (TOKENS, D), 1.0, 6.0, ((0, 32),))
    ln_gain = jnp.clip(1.0 + 0.1 * jax.random.normal(seeds[1], (D,), jnp.float32), 0.5, 1.5).astype(jnp.bfloat16)
    ln_bias = gaussian(seeds[2], (D,), 0.5, 3.0, ((0, 16),))
    qkv_weight = gaussian(seeds[3], (3, D, D), D ** -0.5, 0.125, ((1, 16), (2, 2)))
    out_weight = gaussian(seeds[4], (D, D), (D // 32) ** -0.5, 0.75, ((0, 16), (1, 2)))
    fc1_weight = gaussian(seeds[5], (D, FF), D ** -0.5, 0.125, ((0, 16), (1, 2)))
    fc2_weight = gaussian(seeds[6], (D, FF), FF ** -0.5, 0.0625, ((0, 16), (1, 2)))
    cotangent = gaussian(seeds[7], (TOKENS, D), 1.0, 6.0, ((0, 32),))
    m_gain = gaussian(seeds[8], (D,), 13.0, 78.0, ((0, 16),), jnp.float32)
    v_gain = jnp.clip(jnp.exp(math.log(2500.0) - 2.3025851 * jax.random.uniform(seeds[9], (D,), jnp.float32) ** block_levels(seeds[9], (D,), ((0, 16),), -0.2, 0.2)), 250.0, 2500.0)
    m_bias = gaussian(seeds[10], (D,), 13.0, 78.0, ((0, 16),), jnp.float32)
    v_bias = jnp.clip(jnp.exp(math.log(2500.0) - 2.3025851 * jax.random.uniform(seeds[11], (D,), jnp.float32) ** block_levels(seeds[11], (D,), ((0, 16),), -0.2, 0.2)), 250.0, 2500.0)
    m_qkv = gaussian(seeds[12], (3, D, D), 1.5, 9.0, ((1, 16), (2, 2)), jnp.float32)
    v_qkv = jnp.clip(jnp.exp(math.log(30.0) - 2.3025851 * jax.random.uniform(seeds[13], (3, D, D), jnp.float32) ** block_levels(seeds[13], (3, D, D), ((1, 16), (2, 2)), -0.2, 0.2)), 3.0, 30.0)
    m_out = gaussian(seeds[14], (D, D), 3.0, 18.0, ((0, 16), (1, 2)), jnp.float32)
    v_out = jnp.clip(jnp.exp(math.log(100.0) - 2.3025851 * jax.random.uniform(seeds[15], (D, D), jnp.float32) ** block_levels(seeds[15], (D, D), ((0, 16), (1, 2)), -0.2, 0.2)), 10.0, 100.0)
    m_fc1 = gaussian(seeds[16], (D, FF), 4.0, 24.0, ((0, 16), (1, 2)), jnp.float32)
    v_fc1 = jnp.clip(jnp.exp(math.log(250.0) - 2.3025851 * jax.random.uniform(seeds[17], (D, FF), jnp.float32) ** block_levels(seeds[17], (D, FF), ((0, 16), (1, 2)), -0.2, 0.2)), 25.0, 250.0)
    m_fc2 = gaussian(seeds[18], (D, FF), 8.0, 48.0, ((0, 16), (1, 2)), jnp.float32)
    v_fc2 = jnp.clip(jnp.exp(math.log(800.0) - 2.3025851 * jax.random.uniform(seeds[19], (D, FF), jnp.float32) ** block_levels(seeds[19], (D, FF), ((0, 16), (1, 2)), -0.2, 0.2)), 80.0, 800.0)
    return dict(inputs=inputs, ln_gain=ln_gain, ln_bias=ln_bias, qkv_weight=qkv_weight, out_weight=out_weight, fc1_weight=fc1_weight, fc2_weight=fc2_weight, cotangent=cotangent, m_gain=m_gain, v_gain=v_gain, m_bias=m_bias, v_bias=v_bias, m_qkv=m_qkv, v_qkv=v_qkv, m_out=m_out, v_out=v_out, m_fc1=m_fc1, v_fc1=v_fc1, m_fc2=m_fc2, v_fc2=v_fc2)


HIGHEST = lax.Precision.HIGHEST
EPS_NORM = 1e-05
MASK_FILL = -1e+30
BETA_ONE = 0.9
BETA_TWO = 0.95
ADAM_EPS = 1e-08
RATE = 0.02
DECAY = 0.1
STEP_COUNT = 10

@jax.custom_vjp
def low(v):
    return lax.optimization_barrier(v.astype(jnp.bfloat16)).astype(jnp.float32)

@jax.custom_vjp
def low_back(v):
    return v

def low_keep(v):
    return (low(v), None)

def low_pass(kept, grad):
    return (grad,)

def back_keep(v):
    return (v, None)

def back_low(kept, grad):
    return (low(grad),)
low.defvjp(low_keep, low_pass)
low_back.defvjp(back_keep, back_low)

def rope_angles(length):
    position = jnp.arange(length, dtype=jnp.float32)[:, None]
    inverse = 10000.0 ** (-(jnp.arange(ROT // 2, dtype=jnp.float32) * 2.0 / ROT))
    angles = position * inverse[None, :]
    return (jnp.cos(angles), jnp.sin(angles))

def rotate(tensor_in, cosine, sine_table):
    half_rot = ROT // 2
    first_half = tensor_in[..., :half_rot]
    second_half = tensor_in[..., half_rot:ROT]
    cos_wide = cosine[:, None, :]
    sin_wide = sine_table[:, None, :]
    return jnp.concatenate([first_half * cos_wide - second_half * sin_wide, second_half * cos_wide + first_half * sin_wide, tensor_in[..., ROT:]], axis=-1)

def layer(inputs_group, gain, bias, qkv_w, out_w, fc1_w, fc2_w):
    groups, length = (inputs_group.shape[0], inputs_group.shape[1])
    centred = inputs_group - lax.optimization_barrier(jnp.mean(inputs_group, axis=-1, keepdims=True))
    inv_std = lax.rsqrt(lax.optimization_barrier(jnp.mean(centred * centred, axis=-1, keepdims=True)) + EPS_NORM)
    hidden = low(centred * inv_std * gain + bias)
    proj = jnp.einsum('gld,cde->cgle', hidden, qkv_w, precision=HIGHEST)
    proj = proj.reshape(3, groups, length, HEADS, HEAD)
    cosine, sine_table = rope_angles(length)
    query = low(rotate(low_back(proj[0]), cosine, sine_table))
    keys = low(rotate(low_back(proj[1]), cosine, sine_table))
    values = low(low_back(proj[2]))
    scores = jnp.einsum('gqhd,gkhd->ghqk', query, keys, precision=HIGHEST) * HEAD ** (-0.5)
    scores = low_back(scores)
    rows = jnp.arange(length)[:, None]
    cols = jnp.arange(length)[None, :]
    scores = jnp.where((cols <= rows)[None, None], scores, MASK_FILL)
    probs = low(jax.nn.softmax(scores, axis=-1))
    context = jnp.einsum('ghqk,gkhd->gqhd', probs, values, precision=HIGHEST)
    context = low(low_back(context.reshape(groups, length, D)))
    attn_out = jnp.einsum('gle,de->gld', context, out_w, precision=HIGHEST)
    pre = low_back(jnp.einsum('gld,df->glf', hidden, fc1_w, precision=HIGHEST))
    act = low(jax.nn.gelu(pre, approximate=True))
    mlp_out = jnp.einsum('glf,df->gld', act, fc2_w, precision=HIGHEST)
    return inputs_group + (attn_out + mlp_out)

def adamw(weight, gradient, moment, second):
    new_m = BETA_ONE * moment + (1.0 - BETA_ONE) * gradient
    new_v = BETA_TWO * second + (1.0 - BETA_TWO) * gradient * gradient
    m_hat = new_m / (1.0 - BETA_ONE ** STEP_COUNT)
    v_hat = new_v / (1.0 - BETA_TWO ** STEP_COUNT)
    update = -RATE * (m_hat / (jnp.sqrt(v_hat) + ADAM_EPS) + DECAY * weight.astype(jnp.float32))
    return (gradient, update, new_m, new_v)

def reference(inputs, ln_gain, ln_bias, qkv_weight, out_weight, fc1_weight, fc2_weight, cotangent, m_gain, v_gain, m_bias, v_bias, m_qkv, v_qkv, m_out, v_out, m_fc1, v_fc1, m_fc2, v_fc2):
    group_size = math.gcd(N_DP, max(1, 2048 // TOK_DP))
    group_count = N_DP // group_size
    inputs_all = inputs.astype(jnp.float32).reshape(group_count, group_size, TOK_DP, D)
    cotan_all = cotangent.astype(jnp.float32).reshape(group_count, group_size, TOK_DP, D)
    params = (ln_gain.astype(jnp.float32), ln_bias.astype(jnp.float32), qkv_weight.astype(jnp.float32), out_weight.astype(jnp.float32), fc1_weight.astype(jnp.float32), fc2_weight.astype(jnp.float32))

    def accumulate(running, sequences):
        inputs_group, cotan_group = sequences
        result, pull_back = jax.vjp(layer, inputs_group, *params)
        grads = pull_back(cotan_group)
        running = tuple((total + extra for total, extra in zip(running, grads[1:])))
        return (running, (result.astype(jnp.bfloat16), grads[0]))
    zeros = tuple((jnp.zeros_like(item) for item in params))
    totals, (outputs, input_grads) = lax.scan(accumulate, zeros, (inputs_all, cotan_all))
    output = outputs.reshape(TOKENS, D)
    input_grad = input_grads.reshape(TOKENS, D)
    gain_res = adamw(ln_gain, totals[0], m_gain, v_gain)
    bias_res = adamw(ln_bias, totals[1], m_bias, v_bias)
    qkv_res = adamw(qkv_weight, totals[2], m_qkv, v_qkv)
    out_res = adamw(out_weight, totals[3], m_out, v_out)
    fc1_res = adamw(fc1_weight, totals[4], m_fc1, v_fc1)
    fc2_res = adamw(fc2_weight, totals[5], m_fc2, v_fc2)
    return (output, input_grad, gain_res[0], gain_res[1], gain_res[2], gain_res[3], bias_res[0], bias_res[1], bias_res[2], bias_res[3], qkv_res[0], qkv_res[1], qkv_res[2], qkv_res[3], out_res[0], out_res[1], out_res[2], out_res[3], fc1_res[0], fc1_res[1], fc1_res[2], fc1_res[3], fc2_res[0], fc2_res[1], fc2_res[2], fc2_res[3])
```

```python
import jax
import jax.numpy as jnp
import numpy as np
from jax import lax
from jax.experimental import pallas as pl
from jax.experimental.pallas import tpu as pltpu
from jax.sharding import Mesh
from jax.sharding import PartitionSpec as P

HEAD = 64
ROT = 32
PAIR = 2 * HEAD
SCALE = HEAD ** (-0.5)

EPS_NORM = 1e-05
MASK_FILL = -1e30
BETA_ONE = 0.9
BETA_TWO = 0.95
ADAM_EPS = 1e-08
RATE = 0.02
DECAY = 0.1
STEP_COUNT = 10

BF16 = jnp.bfloat16
F32 = jnp.float32


def swap(value, axis):
    return lax.ppermute(value, axis, [(0, 1), (1, 0)])


def swap_inner(value, flip):
    return lax.ppermute(value, ("y", "c"), [(i, i ^ flip) for i in range(4)])


def inner_index():
    return 2 * lax.axis_index("y") + lax.axis_index("c")


def spread_columns(weight):
    r = inner_index()
    rows, width = weight.shape[0], weight.shape[1] // 4
    out = jnp.zeros((4 * rows, width), weight.dtype)
    for flip in range(4):
        piece = lax.dynamic_slice(weight, (0, (r ^ flip) * width), (rows, width))
        if flip:
            piece = swap_inner(piece, flip)
        out = lax.dynamic_update_slice(out, piece, ((r ^ flip) * rows, 0))
    return out


def spread_qkv(weight):
    r = inner_index()
    rows, width = weight.shape[1], weight.shape[2] // 4
    out = jnp.zeros((4 * rows, 3 * width), weight.dtype)
    for flip in range(4):
        piece = lax.dynamic_slice(weight, (0, 0, (r ^ flip) * width), (3, rows, width))
        piece = jnp.concatenate([piece[0], piece[1], piece[2]], axis=1)
        if flip:
            piece = swap_inner(piece, flip)
        out = lax.dynamic_update_slice(out, piece, ((r ^ flip) * rows, 0))
    return out


def collect_columns(part):
    r = inner_index()
    rows = part.shape[0] // 4
    pieces = []
    for flip in range(4):
        piece = lax.dynamic_slice(part, ((r ^ flip) * rows, 0), (rows, part.shape[1]))
        if flip:
            piece = swap_inner(piece.astype(BF16), flip).astype(F32)
        pieces.append(piece)
    return r, pieces


def join_columns(part):
    r, pieces = collect_columns(part)
    rows, width = pieces[0].shape
    out = jnp.zeros((rows, 4 * width), F32)
    for flip, piece in enumerate(pieces):
        out = lax.dynamic_update_slice(out, piece, (0, (r ^ flip) * width))
    return out


def join_qkv(part):
    r, pieces = collect_columns(part)
    rows, width = pieces[0].shape[0], pieces[0].shape[1] // 3
    out = jnp.zeros((3, rows, 4 * width), F32)
    for flip, piece in enumerate(pieces):
        piece = jnp.stack([piece[:, i * width : (i + 1) * width] for i in range(3)])
        out = lax.dynamic_update_slice(out, piece, (0, 0, (r ^ flip) * width))
    return out


def gather_outer(value):
    return lax.all_gather(value, "o", axis=0, tiled=True)


def reduce_outer(part):
    n = lax.axis_size("o")
    z = lax.axis_index("o")
    rows = part.shape[0] // n

    def block(i):
        return lax.dynamic_slice(part, (i * rows, 0), (rows, part.shape[1]))

    up = down = None
    for s in range(n - 1, 0, -1):
        to_up = block(jnp.minimum(z + s, n - 1))
        to_down = block(jnp.maximum(z - s, 0))
        if up is not None:
            to_up = to_up + up
            to_down = to_down + down
        up = lax.ppermute(to_up, "o", [(i, i + 1) for i in range(0, n - s)])
        down = lax.ppermute(to_down, "o", [(i + 1, i) for i in range(s - 1, n - 1)])
    return block(z).astype(F32) + up.astype(F32) + down.astype(F32)


def order_halves(own, other):
    first = lax.axis_index("t") == 0
    return jnp.concatenate([jnp.where(first, own, other), jnp.where(first, other, own)])


def gather_plane(own):
    mid = own.shape[0] // 2
    by_t = swap(own, "t")
    by_y = swap(own, "y")
    corner = jnp.concatenate([swap(by_t[:mid], "y"), swap(by_y[mid:], "t")])
    core = jnp.concatenate([order_halves(own, by_t), order_halves(by_y, corner)])
    return jnp.concatenate([core, swap(core, "c")])


def scatter_plane(part):
    rows = part.shape[0] // 8
    mid = rows // 2
    core = part[: 4 * rows] + swap(part[4 * rows :], "c")
    t = lax.axis_index("t")

    def block(sequence, half):
        return lax.dynamic_slice(core, ((2 * sequence + half) * rows, 0), (rows, part.shape[1]))

    own, by_t, by_y, corner = block(0, t), block(0, 1 - t), block(1, t), block(1, 1 - t)
    by_t = jnp.concatenate([by_t[:mid] + swap(corner[:mid], "y"), by_t[mid:]])
    by_y = jnp.concatenate([by_y[:mid], by_y[mid:] + swap(corner[mid:], "t")])
    return own.astype(F32) + swap(by_t, "t").astype(F32) + swap(by_y, "y").astype(F32)


def flips_outer(value):
    n = lax.axis_size("o")
    bit = 1
    while bit < n:
        value = value + lax.ppermute(value, "o", [(i, i ^ bit) for i in range(n)])
        bit *= 2
    return value


def gather_vectors(pair):
    count = 4 * lax.axis_size("o")
    index = 4 * lax.axis_index("o") + inner_index()
    out = jnp.zeros((2, count * pair.shape[1]), pair.dtype)
    out = lax.dynamic_update_slice(out, pair, (0, index * pair.shape[1]))
    out = out + swap(out, "c")
    out = out + swap(out, "y")
    return flips_outer(out)


def sum_vectors(pair):
    pair = pair + swap(pair, "c")
    pair = pair + swap(pair, "t")
    pair = pair + swap(pair, "y")
    pair = flips_outer(pair)
    count = 4 * lax.axis_size("o")
    index = 4 * lax.axis_index("o") + inner_index()
    width = pair.shape[1] // count
    return lax.dynamic_slice(pair, (0, index * width), (2, width))


def lane_tables(length):
    position = np.arange(length, dtype=np.float32)[:, None]
    inverse = 10000.0 ** (-(np.arange(ROT // 2, dtype=np.float32) * 2.0 / ROT))
    angles = (position * inverse.astype(np.float32)[None, :]).astype(np.float64)
    cosine = jnp.asarray(np.cos(angles).astype(np.float32))
    sine = jnp.asarray(np.sin(angles).astype(np.float32))
    none = jnp.zeros_like(sine)
    rest = jnp.zeros((length, HEAD - ROT), F32)
    tables = (
        jnp.concatenate([cosine, cosine, rest + 1.0], axis=1),
        jnp.concatenate([sine, none, rest], axis=1),
        jnp.concatenate([none, sine, rest], axis=1),
    )
    return tuple(jnp.concatenate([table, table], axis=1) for table in tables)


def attention_body(proj_ref, grad_ref, cos_ref, low_ref, high_ref, context_ref, d_proj_ref):
    length, width = grad_ref.shape
    half = length // 2
    cosine, low, high = cos_ref[...], low_ref[...], high_ref[...]
    first = lax.broadcasted_iota(jnp.int32, (length, PAIR), 1) < HEAD
    row = lax.broadcasted_iota(jnp.int32, (half, half), 0)
    col = lax.broadcasted_iota(jnp.int32, (half, half), 1)
    keep = row <= col

    def turn(value, sign):
        ahead = pltpu.roll(value, PAIR - ROT // 2, 1)
        behind = pltpu.roll(value, ROT // 2, 1)
        return value * cosine - sign * ahead * low + sign * behind * high

    def rows_by_rows(a, b):
        return lax.dot_general(a, b, (((1,), (1,)), ((), ())), preferred_element_type=F32)

    def turned(a, b):
        return lax.dot_general(a, b, (((0,), (0,)), ((), ())), preferred_element_type=F32)

    def plain(a, b):
        return lax.dot_general(a, b, (((1,), (0,)), ((), ())), preferred_element_type=F32)

    def over_keys(function, value):
        return function(value, axis=0, keepdims=True)

    for pair in range(width // PAIR):
        lanes = pl.ds(pair * PAIR, PAIR)
        key_lanes = pl.ds(width + pair * PAIR, PAIR)
        value_lanes = pl.ds(2 * width + pair * PAIR, PAIR)
        query = (turn(proj_ref[:, lanes], 1.0).astype(BF16).astype(F32) * SCALE).astype(BF16)
        keys = turn(proj_ref[:, key_lanes], 1.0).astype(BF16)
        values = proj_ref[:, value_lanes].astype(BF16)
        grad = grad_ref[:, lanes]
        context = jnp.zeros((length, PAIR), F32)
        d_query = context
        d_keys_a = d_keys_b = d_values_a = d_values_b = jnp.zeros((half, PAIR), F32)
        for head in range(2):
            mine = first if head == 0 else jnp.logical_not(first)
            q, k, v, g = (
                jnp.where(mine, item, jnp.zeros_like(item)) for item in (query, keys, values, grad)
            )
            qa, qb, ga, gb = q[:half], q[half:], g[:half], g[half:]
            s_aa = jnp.where(keep, rows_by_rows(keys[:half], qa), MASK_FILL)
            s_ab = rows_by_rows(keys[:half], qb)
            s_bb = jnp.where(keep, rows_by_rows(keys[half:], qb), MASK_FILL)
            max_a = over_keys(jnp.max, s_aa)
            max_b = jnp.maximum(over_keys(jnp.max, s_ab), over_keys(jnp.max, s_bb))
            e_aa, e_ab, e_bb = jnp.exp(s_aa - max_a), jnp.exp(s_ab - max_b), jnp.exp(s_bb - max_b)
            inv_a = 1.0 / over_keys(jnp.sum, e_aa)
            inv_b = 1.0 / (over_keys(jnp.sum, e_ab) + over_keys(jnp.sum, e_bb))
            p_aa, p_ab, p_bb = e_aa * inv_a, e_ab * inv_b, e_bb * inv_b
            r_aa, r_ab, r_bb = p_aa.astype(BF16), p_ab.astype(BF16), p_bb.astype(BF16)
            d_aa = rows_by_rows(values[:half], ga)
            d_ab = rows_by_rows(values[:half], gb)
            d_bb = rows_by_rows(values[half:], gb)
            centre_a = over_keys(jnp.sum, d_aa * p_aa)
            centre_b = over_keys(jnp.sum, d_ab * p_ab) + over_keys(jnp.sum, d_bb * p_bb)
            t_aa = (p_aa * (d_aa - centre_a)).astype(BF16)
            t_ab = (p_ab * (d_ab - centre_b)).astype(BF16)
            t_bb = (p_bb * (d_bb - centre_b)).astype(BF16)
            context += jnp.concatenate(
                [turned(r_aa, v[:half]), turned(r_ab, v[:half]) + turned(r_bb, v[half:])]
            )
            d_query += jnp.concatenate(
                [turned(t_aa, k[:half]), turned(t_ab, k[:half]) + turned(t_bb, k[half:])]
            )
            d_keys_a += plain(t_aa, qa) + plain(t_ab, qb)
            d_keys_b += plain(t_bb, qb)
            d_values_a += plain(r_aa, ga) + plain(r_ab, gb)
            d_values_b += plain(r_bb, gb)
        context_ref[:, lanes] = context.astype(BF16)
        d_proj_ref[:, lanes] = turn(d_query * SCALE, -1.0).astype(BF16)
        d_keys = jnp.concatenate([d_keys_a, d_keys_b])
        d_proj_ref[:, key_lanes] = turn(d_keys, -1.0).astype(BF16)
        d_proj_ref[:, value_lanes] = jnp.concatenate([d_values_a, d_values_b]).astype(BF16)


def attention(proj, d_context, length):
    tokens, width = d_context.shape
    table = pl.BlockSpec((length, PAIR), lambda s: (0, 0))
    one = pl.BlockSpec((length, width), lambda s: (s, 0))
    three = pl.BlockSpec((length, 3 * width), lambda s: (s, 0))
    return pl.pallas_call(
        attention_body,
        out_shape=(
            jax.ShapeDtypeStruct((tokens, width), BF16),
            jax.ShapeDtypeStruct((tokens, 3 * width), BF16),
        ),
        grid=(tokens // length,),
        in_specs=[three, one, table, table, table],
        out_specs=(one, three),
        compiler_params=pltpu.CompilerParams(vmem_limit_bytes=48 << 20),
        name="attention",
    )(proj, d_context, *lane_tables(length))


def gelu_tanh(values_in):
    return jax.nn.gelu(values_in, approximate=True)


def adamw(weight, gradient, moment, second):
    new_m = BETA_ONE * moment + (1.0 - BETA_ONE) * gradient
    new_v = BETA_TWO * second + (1.0 - BETA_TWO) * gradient * gradient
    m_hat = new_m / (1.0 - BETA_ONE**STEP_COUNT)
    v_hat = new_v / (1.0 - BETA_TWO**STEP_COUNT)
    update = -RATE * (m_hat / (jnp.sqrt(v_hat) + ADAM_EPS) + DECAY * weight.astype(F32))
    return (gradient, update, new_m, new_v)


def dot_nn(a, b):
    return lax.dot_general(a, b, (((1,), (0,)), ((), ())), preferred_element_type=F32)


def dot_nt(a, b):
    return lax.dot_general(a, b, (((1,), (1,)), ((), ())), preferred_element_type=F32)


def dot_tn(a, b):
    return lax.dot_general(a, b, (((0,), (0,)), ((), ())), preferred_element_type=F32)


def shards(
    inputs,
    ln_gain,
    ln_bias,
    qkv_weight,
    out_weight,
    fc1_weight,
    fc2_weight,
    cotangent,
    m_gain,
    v_gain,
    m_bias,
    v_bias,
    m_qkv,
    v_qkv,
    m_out,
    v_out,
    m_fc1,
    v_fc1,
    m_fc2,
    v_fc2,
):
    length = 2 * inputs.shape[0]
    qkv_cols = gather_outer(spread_qkv(qkv_weight))
    out_cols = gather_outer(spread_columns(out_weight))
    fc1_cols = gather_outer(spread_columns(fc1_weight))
    fc2_cols = gather_outer(spread_columns(fc2_weight))

    vectors = gather_vectors(jnp.stack([ln_gain, ln_bias])).astype(F32)
    gain_wide, bias_wide = vectors[0], vectors[1]
    own_rows = inputs.astype(F32)
    centred = own_rows - jnp.mean(own_rows, axis=1, keepdims=True)
    inv_std = lax.rsqrt(jnp.mean(centred * centred, axis=1, keepdims=True) + EPS_NORM)
    normed = centred * inv_std
    hidden_own = (normed * gain_wide + bias_wide).astype(BF16)
    hidden = gather_plane(hidden_own)
    cotan = gather_plane(cotangent)

    proj = dot_nn(hidden, qkv_cols)
    d_context = dot_nn(cotan, out_cols).astype(BF16)
    context, d_proj = attention(proj, d_context, length)
    qkv_sum = reduce_outer(dot_tn(hidden, d_proj).astype(BF16))
    out_sum = reduce_outer(dot_tn(cotan, context).astype(BF16))

    pre_act = dot_nn(hidden, fc1_cols)
    activated = gelu_tanh(pre_act).astype(BF16)
    fc2_sum = reduce_outer(dot_tn(cotan, activated).astype(BF16))
    d_act = dot_nn(cotan, fc2_cols)
    ignored, pull_back = jax.vjp(gelu_tanh, pre_act)
    d_pre = pull_back(d_act)[0].astype(BF16)
    fc1_sum = reduce_outer(dot_tn(hidden, d_pre).astype(BF16))

    branch = dot_nt(context, out_cols) + dot_nt(activated, fc2_cols)
    output = (own_rows + scatter_plane(branch.astype(BF16))).astype(BF16)
    d_hidden = scatter_plane((dot_nt(d_proj, qkv_cols) + dot_nt(d_pre, fc1_cols)).astype(BF16))

    vector_parts = jnp.stack([jnp.sum(d_hidden * normed, axis=0), jnp.sum(d_hidden, axis=0)])
    vector_grads = sum_vectors(vector_parts)
    scaled_grad = d_hidden * gain_wide
    input_grad = cotangent.astype(F32) + inv_std * (
        scaled_grad
        - jnp.mean(scaled_grad, axis=1, keepdims=True)
        - normed * jnp.mean(scaled_grad * normed, axis=1, keepdims=True)
    )
    gain_res = adamw(ln_gain, vector_grads[0], m_gain, v_gain)
    bias_res = adamw(ln_bias, vector_grads[1], m_bias, v_bias)
    qkv_res = adamw(qkv_weight, join_qkv(qkv_sum), m_qkv, v_qkv)
    out_res = adamw(out_weight, join_columns(out_sum), m_out, v_out)
    fc1_res = adamw(fc1_weight, join_columns(fc1_sum), m_fc1, v_fc1)
    fc2_res = adamw(fc2_weight, join_columns(fc2_sum), m_fc2, v_fc2)
    return (
        output,
        input_grad,
        *gain_res,
        *bias_res,
        *qkv_res,
        *out_res,
        *fc1_res,
        *fc2_res,
    )


def solution(mesh):
    dp, tensor = mesh.devices.shape
    inner = Mesh(mesh.devices.reshape(dp // 4, 2, 2, tensor), ("o", "y", "c", "t"))
    rows = P(("o", "y", "c", "t"), None)
    vector = P(("o", "y", "c"))
    stack = P(None, ("o", "y", "c"), "t")
    matrix = P(("o", "y", "c"), "t")
    return jax.shard_map(
        shards,
        mesh=inner,
        in_specs=(rows, vector, vector, stack, matrix, matrix, matrix, rows)
        + (vector,) * 4
        + (stack,) * 2
        + (matrix,) * 6,
        out_specs=(rows, rows) + (vector,) * 8 + (stack,) * 4 + (matrix,) * 12,
        check_vma=False,
    )
```

```python
import functools
import math

import jax
import jax.numpy as jnp
import numpy as np
from jax import lax
from jax.experimental import pallas as pl
from jax.experimental.pallas import tpu as pltpu
from jax.sharding import Mesh
from jax.sharding import PartitionSpec as P

HEAD = 64
ROT = 32
PAIR = 2 * HEAD
SCALE = HEAD ** (-0.5)

EPS_NORM = 1e-05
MASK_FILL = -1e30
BETA_ONE = 0.9
BETA_TWO = 0.95
ADAM_EPS = 1e-08
RATE = 0.02
DECAY = 0.1
STEP_COUNT = 10
GELU_ROOT = math.sqrt(2.0 / math.pi)
GELU_CUBE = 0.044715

BF16 = jnp.bfloat16
F32 = jnp.float32


def swap(value, axis):
    return lax.ppermute(value, axis, [(0, 1), (1, 0)])


def swap_inner(value, flip):
    return lax.ppermute(value, ("w", "c"), [(i, i ^ flip) for i in range(4)])


def ring(value):
    n = lax.axis_size("h")
    return lax.ppermute(value, "h", [(i, (i + 1) % n) for i in range(n)])


def inner_index():
    return 2 * lax.axis_index("w") + lax.axis_index("c")


def dp_index():
    outer = 2 * lax.axis_index("h") + lax.axis_index("w")
    return 4 * outer + 2 * lax.axis_index("y") + lax.axis_index("c")


def feature_table():
    n = lax.axis_size("h")
    h, w, y, c = (lax.axis_index(axis) for axis in "hwyc")
    entries = [lax.axis_index("t")]
    for flip_y in range(2):
        for back in range(n):
            for flip in range(4):
                outer = 2 * lax.rem(h + n - back, n) + (w ^ (flip >> 1))
                entries.append(4 * outer + 2 * (y ^ flip_y) + (c ^ (flip & 1)))
    return jnp.stack(entries).astype(jnp.int32)


def column_block(weight, j):
    width = weight.shape[-1] // 4
    return lax.dynamic_slice_in_dim(weight, j * width, width, weight.ndim - 1)


def attention_block(qkv_weight, out_weight, j):
    qkv = column_block(qkv_weight, j)
    return jnp.concatenate([qkv[0], qkv[1], qkv[2], column_block(out_weight, j)], axis=1)


def spread(piece_of):
    r = inner_index()
    pieces = [swap_inner(piece_of(r ^ flip), flip) for flip in range(1, 4)]
    return jnp.concatenate([piece_of(r), *pieces])


def collect(total):
    r = inner_index()
    rows = total.shape[0] // 4
    pieces = [(r, total[:rows])]
    for flip in range(1, 4):
        pieces.append((r ^ flip, swap_inner(total[flip * rows : (flip + 1) * rows], flip)))
    return pieces


def join_columns(pieces):
    rows, width = pieces[0][1].shape
    out = jnp.zeros((rows, 4 * width), BF16)
    for j, piece in pieces:
        out = lax.dynamic_update_slice(out, piece, (0, j * width))
    return out.astype(F32)


def join_attention(pieces):
    rows, width = pieces[0][1].shape[0], pieces[0][1].shape[1] // 4
    parts = []
    for i in range(4):
        parts.append(join_columns([(j, piece[:, i * width : (i + 1) * width]) for j, piece in pieces]))
    return jnp.stack(parts[:3]), parts[3]


class Gather:
    def __init__(self, own):
        self.beside = [own]
        self.far = []

    def over_h(self):
        for _ in range(lax.axis_size("h") - 1):
            self.beside.append(ring(self.beside[-1]))

    def over_y_first(self):
        self.far.append(swap(self.beside[0], "y"))

    def over_y_rest(self):
        self.far += [swap(piece, "y") for piece in self.beside[1:]]

    def pieces(self):
        return self.beside + self.far


class Reduce:
    def __init__(self, parts):
        n = len(parts) // 2
        self.own, self.beside, self.own_far, self.far = parts[0], parts[1:n], parts[n], parts[n + 1 :]

    def over_y_rest(self):
        self.beside = [near + swap(far, "y") for near, far in zip(self.beside, self.far)]
        self.far = []

    def over_h(self):
        moving = None
        for near in self.beside:
            moving = ring(near if moving is None else near + moving)
        self.beside = [] if moving is None else [moving]

    def over_y_first(self):
        self.own_far = swap(self.own_far, "y")

    def total(self):
        total = self.own.astype(F32) + self.own_far.astype(F32)
        return sum((near.astype(F32) for near in self.beside), total).astype(BF16)


class GroupSum:
    def __init__(self, parts):
        self.mine, self.other = parts

    def over_c(self):
        self.other = swap(self.other, "c")

    def block(self, sequence, half):
        rows = self.mine.shape[0] // 4
        start = ((2 * sequence + half) * rows, 0)
        size = (rows, self.mine.shape[1])
        return lax.dynamic_slice(self.mine, start, size) + lax.dynamic_slice(self.other, start, size)

    def corner(self):
        self.moving = swap(self.block(1, 1 - lax.axis_index("t")), "t")

    def edges(self):
        t = lax.axis_index("t")
        self.turning = swap(self.block(1, t) + self.moving, "w")
        self.moving = swap(self.block(0, 1 - t), "t")

    def total(self):
        own = self.block(0, lax.axis_index("t"))
        return own.astype(F32) + self.moving.astype(F32) + self.turning.astype(F32)


def close(*items):
    holders = [vars(item) if isinstance(item, (Gather, Reduce, GroupSum)) else item for item in items]
    held = lax.optimization_barrier(holders)
    out = []
    for item, value in zip(items, held):
        if isinstance(item, (Gather, Reduce, GroupSum)):
            vars(item).update(value)
        else:
            out.append(value)
    return out


def flips_outer(value):
    n = lax.axis_size("h")
    bit = 1
    while bit < n:
        value = value + lax.ppermute(value, "h", [(i, i ^ bit) for i in range(n)])
        bit *= 2
    return value


def gather_vectors(pair):
    count = 8 * lax.axis_size("h")
    out = jnp.zeros((2, count * pair.shape[1]), pair.dtype)
    out = lax.dynamic_update_slice(out, pair, (0, dp_index() * pair.shape[1]))
    for axis in "wyc":
        out = out + swap(out, axis)
    return flips_outer(out)


def sum_vectors(pair):
    for axis in "ctyw":
        pair = pair + swap(pair, axis)
    pair = flips_outer(pair)
    width = pair.shape[1] // (8 * lax.axis_size("h"))
    return lax.dynamic_slice(pair, (0, dp_index() * width), (2, width))


def lane_tables(length):
    position = np.arange(length, dtype=np.float32)[:, None]
    inverse = 10000.0 ** (-(np.arange(ROT // 2, dtype=np.float32) * 2.0 / ROT))
    angles = (position * inverse.astype(np.float32)[None, :]).astype(np.float64)
    cosine = jnp.asarray(np.cos(angles).astype(np.float32))
    sine = jnp.asarray(np.sin(angles).astype(np.float32))
    none = jnp.zeros_like(sine)
    rest = jnp.zeros((length, HEAD - ROT), F32)
    tables = (
        jnp.concatenate([cosine, cosine, rest + 1.0], axis=1),
        jnp.concatenate([sine, none, rest], axis=1),
        jnp.concatenate([none, sine, rest], axis=1),
    )
    return tuple(jnp.concatenate([table, table], axis=1) for table in tables)


def attention_body(proj_ref, grad_ref, cos_ref, low_ref, high_ref, context_ref, d_proj_ref):
    length, width = grad_ref.shape
    half = length // 2
    cosine, low, high = cos_ref[...], low_ref[...], high_ref[...]
    first = lax.broadcasted_iota(jnp.int32, (length, PAIR), 1) < HEAD
    row = lax.broadcasted_iota(jnp.int32, (half, half), 0)
    col = lax.broadcasted_iota(jnp.int32, (half, half), 1)
    keep = row <= col

    def turn(value, sign):
        ahead = pltpu.roll(value, PAIR - ROT // 2, 1)
        behind = pltpu.roll(value, ROT // 2, 1)
        return value * cosine - sign * ahead * low + sign * behind * high

    def rows_by_rows(a, b):
        return lax.dot_general(a, b, (((1,), (1,)), ((), ())), preferred_element_type=F32)

    def turned(a, b):
        return lax.dot_general(a, b, (((0,), (0,)), ((), ())), preferred_element_type=F32)

    def plain(a, b):
        return lax.dot_general(a, b, (((1,), (0,)), ((), ())), preferred_element_type=F32)

    def over_keys(function, value):
        return function(value, axis=0, keepdims=True)

    for pair in range(width // PAIR):
        lanes = pl.ds(pair * PAIR, PAIR)
        key_lanes = pl.ds(width + pair * PAIR, PAIR)
        value_lanes = pl.ds(2 * width + pair * PAIR, PAIR)
        query = (turn(proj_ref[:, lanes], 1.0).astype(BF16).astype(F32) * SCALE).astype(BF16)
        keys = turn(proj_ref[:, key_lanes], 1.0).astype(BF16)
        values = proj_ref[:, value_lanes].astype(BF16)
        grad = grad_ref[:, lanes]
        context = jnp.zeros((length, PAIR), F32)
        d_query = context
        d_keys_a = d_keys_b = d_values_a = d_values_b = jnp.zeros((half, PAIR), F32)
        for head in range(2):
            mine = first if head == 0 else jnp.logical_not(first)
            q, k, v, g = (
                jnp.where(mine, item, jnp.zeros_like(item)) for item in (query, keys, values, grad)
            )
            qa, qb, ga, gb = q[:half], q[half:], g[:half], g[half:]
            s_aa = jnp.where(keep, rows_by_rows(keys[:half], qa), MASK_FILL)
            s_ab = rows_by_rows(keys[:half], qb)
            s_bb = jnp.where(keep, rows_by_rows(keys[half:], qb), MASK_FILL)
            max_a = over_keys(jnp.max, s_aa)
            max_b = jnp.maximum(over_keys(jnp.max, s_ab), over_keys(jnp.max, s_bb))
            e_aa, e_ab, e_bb = jnp.exp(s_aa - max_a), jnp.exp(s_ab - max_b), jnp.exp(s_bb - max_b)
            inv_a = 1.0 / over_keys(jnp.sum, e_aa)
            inv_b = 1.0 / (over_keys(jnp.sum, e_ab) + over_keys(jnp.sum, e_bb))
            p_aa, p_ab, p_bb = e_aa * inv_a, e_ab * inv_b, e_bb * inv_b
            r_aa, r_ab, r_bb = p_aa.astype(BF16), p_ab.astype(BF16), p_bb.astype(BF16)
            d_aa = rows_by_rows(values[:half], ga)
            d_ab = rows_by_rows(values[:half], gb)
            d_bb = rows_by_rows(values[half:], gb)
            centre_a = over_keys(jnp.sum, d_aa * p_aa)
            centre_b = over_keys(jnp.sum, d_ab * p_ab) + over_keys(jnp.sum, d_bb * p_bb)
            t_aa = (p_aa * (d_aa - centre_a)).astype(BF16)
            t_ab = (p_ab * (d_ab - centre_b)).astype(BF16)
            t_bb = (p_bb * (d_bb - centre_b)).astype(BF16)
            context += jnp.concatenate(
                [turned(r_aa, v[:half]), turned(r_ab, v[:half]) + turned(r_bb, v[half:])]
            )
            d_query += jnp.concatenate(
                [turned(t_aa, k[:half]), turned(t_ab, k[:half]) + turned(t_bb, k[half:])]
            )
            d_keys_a += plain(t_aa, qa) + plain(t_ab, qb)
            d_keys_b += plain(t_bb, qb)
            d_values_a += plain(r_aa, ga) + plain(r_ab, gb)
            d_values_b += plain(r_bb, gb)
        context_ref[:, lanes] = context.astype(BF16)
        d_proj_ref[:, lanes] = turn(d_query * SCALE, -1.0).astype(BF16)
        d_keys = jnp.concatenate([d_keys_a, d_keys_b])
        d_proj_ref[:, key_lanes] = turn(d_keys, -1.0).astype(BF16)
        d_proj_ref[:, value_lanes] = jnp.concatenate([d_values_a, d_values_b]).astype(BF16)


def dot_nn(a, b):
    return lax.dot_general(a, b, (((1,), (0,)), ((), ())), preferred_element_type=F32)


def dot_nt(a, b):
    return lax.dot_general(a, b, (((1,), (1,)), ((), ())), preferred_element_type=F32)


def dot_tn(a, b):
    return lax.dot_general(a, b, (((0,), (0,)), ((), ())), preferred_element_type=F32)


def rows_of(block, width):
    return pl.BlockSpec((block, width), lambda s: (s, 0))


def whole(shape):
    return pl.BlockSpec(shape, lambda s: (0, 0), pipeline_mode=pl.Buffered(1))


ANYWHERE = pl.BlockSpec(memory_space=pl.ANY)
PARAMS = pltpu.CompilerParams(vmem_limit_bytes=58 << 20)


def fetch(piece_refs, into_ref, sem_ref, start=0):
    width = into_ref.shape[1]

    @pl.when(pl.program_id(0) == 0)
    def _():
        copies = []
        for i, piece in enumerate(piece_refs):
            rows = piece.shape[0]
            copies.append(
                pltpu.make_async_copy(
                    piece.at[:, pl.ds(start, width)],
                    into_ref.at[pl.ds(i * rows, rows), :],
                    sem_ref.at[i],
                )
            )
        for copy in copies:
            copy.start()
        for copy in copies:
            copy.wait()


def join_step(table_ref, *refs, norm, permute):
    pieces, (gain_ref, bias_ref, out_ref, buffer, sems) = refs[:8], refs[8:]
    step = pl.program_id(0)
    features = out_ref.shape[1]
    blocks = table_ref.shape[0] - 1 if permute else 1
    size = features // blocks

    def copy(i, slot):
        return pltpu.make_async_copy(pieces[i], buffer.at[slot], sems.at[slot])

    for i in range(8):
        pl.when(step == max(i - 1, 0))(lambda i=i: copy(i, i % 2).start())
    slot = lax.rem(step, 2)
    copy(0, slot).wait()
    chunk = min(128, out_ref.shape[0])

    def emit(i, carry):
        at = pl.ds(pl.multiple_of(i * chunk, chunk), chunk)
        if norm:
            rows = buffer[slot, at, :].astype(F32)
            mean = jnp.mean(rows, axis=1, keepdims=True)
            centred = rows - mean
            inv_std = lax.rsqrt(jnp.mean(centred * centred, axis=1, keepdims=True) + EPS_NORM)
        for j in range(blocks):
            lanes = pl.ds(pl.multiple_of(table_ref[1 + j] * size, size), size) if permute else slice(None)
            value = buffer[slot, at, lanes]
            if norm:
                normed = (value.astype(F32) - mean) * inv_std
                value = (normed * gain_ref[:, lanes] + bias_ref[:, lanes]).astype(BF16)
            out_ref[at, j * size : (j + 1) * size] = value
        return carry

    lax.fori_loop(0, out_ref.shape[0] // chunk, emit, 0)


def join(table, pieces, gain, bias, norm):
    block, features = pieces[0].shape
    blocks = table.shape[0] - 1
    permute = features // blocks % 128 == 0
    vector = pl.BlockSpec((1, features), lambda s, h: (0, 0))
    out = pl.pallas_call(
        functools.partial(join_step, norm=norm, permute=permute),
        grid_spec=pltpu.PrefetchScalarGridSpec(
            num_scalar_prefetch=1,
            grid=(8,),
            in_specs=[ANYWHERE] * 8 + [vector, vector],
            out_specs=pl.BlockSpec((block, features), lambda s, h: (s - s % 2 + (s + h[0]) % 2, 0)),
            scratch_shapes=[
                pltpu.VMEM((2, block, features), BF16),
                pltpu.SemaphoreType.DMA((2,)),
            ],
        ),
        out_shape=jax.ShapeDtypeStruct((8 * block, features), BF16),
        compiler_params=PARAMS,
        name="join",
    )(table, *pieces, gain, bias)
    if not permute:
        cut = out.reshape(8 * block, blocks, features // blocks)
        out = jnp.take(cut, table[1:], axis=1).reshape(8 * block, features)
    return out


def add_and_flush(total_ref, part_refs, addends):
    step = pl.program_id(0)

    @pl.when(step == 0)
    def _():
        total_ref[...] = jnp.zeros_like(total_ref)

    for lanes, addend in addends:
        total_ref[:, lanes] += addend()

    @pl.when(step == pl.num_programs(0) - 1)
    def _():
        rows = part_refs[0].shape[0]
        for i, part_ref in enumerate(part_refs):
            part_ref[...] = total_ref[i * rows : (i + 1) * rows, :].astype(BF16)


def attention_step(hidden_ref, cotan_ref, cos_ref, low_ref, high_ref, *refs):
    pieces, (context_ref, d_proj_ref, cols_ref, proj_ref, grad_ref, sems) = refs[:-6], refs[-6:]
    fetch(pieces, cols_ref, sems)
    width = grad_ref.shape[1]
    proj_ref[...] = dot_nn(hidden_ref[...], cols_ref[:, : 3 * width])
    grad_ref[...] = dot_nn(cotan_ref[...], cols_ref[:, 3 * width :]).astype(BF16)
    attention_body(proj_ref, grad_ref, cos_ref, low_ref, high_ref, context_ref, d_proj_ref)


def attention(hidden, cotan, pieces, length):
    tokens, features = hidden.shape
    width = pieces[0].shape[1] // 4
    return pl.pallas_call(
        attention_step,
        grid=(tokens // length,),
        in_specs=[rows_of(length, features)] * 2
        + [whole((length, PAIR))] * 3
        + [ANYWHERE] * len(pieces),
        out_specs=(rows_of(length, width), rows_of(length, 3 * width)),
        out_shape=(
            jax.ShapeDtypeStruct((tokens, width), BF16),
            jax.ShapeDtypeStruct((tokens, 3 * width), BF16),
        ),
        scratch_shapes=[
            pltpu.VMEM((features, 4 * width), BF16),
            pltpu.VMEM((length, 3 * width), F32),
            pltpu.VMEM((length, width), BF16),
            pltpu.SemaphoreType.DMA((len(pieces),)),
        ],
        compiler_params=PARAMS,
        name="attention",
    )(hidden, cotan, *lane_tables(length), *pieces)


def parts_of(count, features, width):
    rows = features // count
    shapes = [jax.ShapeDtypeStruct((rows, width), BF16)] * count
    return [whole((rows, width))] * count, shapes, [pltpu.VMEM((features, width), F32)]


def attention_grads_step(hidden_ref, cotan_ref, d_proj_ref, context_ref, *refs):
    wide = d_proj_ref.shape[1]
    add_and_flush(
        refs[-1],
        refs[:-1],
        [
            (pl.ds(0, wide), lambda: dot_tn(hidden_ref[...], d_proj_ref[...])),
            (pl.ds(wide, wide // 3), lambda: dot_tn(cotan_ref[...], context_ref[...])),
        ],
    )


def attention_grads(hidden, cotan, d_proj, context, block, count):
    tokens, features = hidden.shape
    width = context.shape[1]
    specs, shapes, scratch = parts_of(count, features, 4 * width)
    return pl.pallas_call(
        attention_grads_step,
        grid=(tokens // block,),
        in_specs=[rows_of(block, features)] * 2 + [rows_of(block, 3 * width), rows_of(block, width)],
        out_specs=specs,
        out_shape=shapes,
        scratch_shapes=scratch,
        compiler_params=PARAMS,
        name="attention_grads",
    )(hidden, cotan, d_proj, context)


def fc1_step(hidden_ref, cotan_ref, *refs, count):
    pieces, (act_ref, slope_ref), parts = refs[:count], refs[count : count + 2], refs[count + 2 : -3]
    cols_ref, total_ref, sems = refs[-3:]
    fetch(pieces, cols_ref, sems)
    pre = dot_nn(hidden_ref[...], cols_ref[...])
    square = pre * pre
    tanh = jnp.tanh(GELU_ROOT * (pre + GELU_CUBE * (pre * square)))
    half = 0.5 * (1.0 + tanh)
    slope = 0.5 * GELU_ROOT * pre * (1.0 - tanh * tanh) * (1.0 + 3.0 * GELU_CUBE * square)
    act_ref[...] = (pre * half).astype(BF16)
    slope_ref[...] = half + slope
    every = pl.ds(0, total_ref.shape[1])
    add_and_flush(total_ref, parts, [(every, lambda: dot_tn(cotan_ref[...], act_ref[...]))])


def fc1_pass(hidden, cotan, pieces, block):
    tokens, features = hidden.shape
    count, width = len(pieces), pieces[0].shape[1]
    specs, shapes, scratch = parts_of(count, features, width)
    act, slope, *parts = pl.pallas_call(
        functools.partial(fc1_step, count=count),
        grid=(tokens // block,),
        in_specs=[rows_of(block, features)] * 2 + [ANYWHERE] * count,
        out_specs=[rows_of(block, width)] * 2 + specs,
        out_shape=[
            jax.ShapeDtypeStruct((tokens, width), BF16),
            jax.ShapeDtypeStruct((tokens, width), F32),
            *shapes,
        ],
        scratch_shapes=[
            pltpu.VMEM((features, width), BF16),
            *scratch,
            pltpu.SemaphoreType.DMA((count,)),
        ],
        compiler_params=PARAMS,
        name="fc1_pass",
    )(hidden, cotan, *pieces)
    return act, slope, parts


def fc2_step(hidden_ref, cotan_ref, slope_ref, *refs, count):
    pieces, d_pre_ref, parts = refs[:count], refs[count], refs[count + 1 : -3]
    cols_ref, total_ref, sems = refs[-3:]
    fetch(pieces, cols_ref, sems)
    d_pre_ref[...] = (dot_nn(cotan_ref[...], cols_ref[...]) * slope_ref[...]).astype(BF16)
    every = pl.ds(0, total_ref.shape[1])
    add_and_flush(total_ref, parts, [(every, lambda: dot_tn(hidden_ref[...], d_pre_ref[...]))])


def fc2_pass(hidden, cotan, pieces, slope, block):
    tokens, features = hidden.shape
    count, width = len(pieces), pieces[0].shape[1]
    specs, shapes, scratch = parts_of(count, features, width)
    d_pre, *parts = pl.pallas_call(
        functools.partial(fc2_step, count=count),
        grid=(tokens // block,),
        in_specs=[rows_of(block, features)] * 2 + [rows_of(block, width)] + [ANYWHERE] * count,
        out_specs=[rows_of(block, width)] + specs,
        out_shape=[jax.ShapeDtypeStruct((tokens, width), BF16), *shapes],
        scratch_shapes=[
            pltpu.VMEM((features, width), BF16),
            *scratch,
            pltpu.SemaphoreType.DMA((count,)),
        ],
        compiler_params=PARAMS,
        name="fc2_pass",
    )(hidden, cotan, slope, *pieces)
    return d_pre, parts


def back_step(table_ref, first_ref, second_ref, *refs, count, start, permute):
    attn_pieces, fc_pieces, (mine_ref, other_ref) = refs[:count], refs[count:-6], refs[-6:-4]
    attn_ref, fc_ref, attn_sems, fc_sems = refs[-4:]
    fetch(attn_pieces, attn_ref, attn_sems, start)
    fetch(fc_pieces, fc_ref, fc_sems)
    out = dot_nt(first_ref[...], attn_ref[...]) + dot_nt(second_ref[...], fc_ref[...])
    out = out.astype(BF16)
    middle = pl.num_programs(0) // 2
    blocks = table_ref.shape[0] - 1
    size = out.shape[1] // blocks

    def store(out_ref):
        if not permute:
            out_ref[...] = out
            return
        for j in range(blocks):
            lanes = pl.ds(pl.multiple_of(table_ref[1 + j] * size, size), size)
            out_ref[:, lanes] = out[:, j * size : (j + 1) * size]

    pl.when(pl.program_id(0) < middle)(lambda: store(mine_ref))
    pl.when(pl.program_id(0) >= middle)(lambda: store(other_ref))


def back_product(table, first, second, attn_pieces, fc_pieces, start, block):
    (tokens, size), width = first.shape, second.shape[1]
    count = len(attn_pieces)
    features = count * attn_pieces[0].shape[0]
    blocks = table.shape[0] - 1
    permute = features // blocks % 128 == 0
    middle = tokens // block // 2
    outs = pl.pallas_call(
        functools.partial(back_step, count=count, start=start, permute=permute),
        grid_spec=pltpu.PrefetchScalarGridSpec(
            num_scalar_prefetch=1,
            grid=(tokens // block,),
            in_specs=[
                pl.BlockSpec((block, size), lambda s, h: (s, 0)),
                pl.BlockSpec((block, width), lambda s, h: (s, 0)),
            ]
            + [ANYWHERE] * (2 * count),
            out_specs=(
                pl.BlockSpec((block, features), lambda s, h: (jnp.minimum(s, middle - 1), 0)),
                pl.BlockSpec((block, features), lambda s, h: (jnp.maximum(s - middle, 0), 0)),
            ),
            scratch_shapes=[
                pltpu.VMEM((features, size), BF16),
                pltpu.VMEM((features, width), BF16),
                pltpu.SemaphoreType.DMA((count,)),
                pltpu.SemaphoreType.DMA((count,)),
            ],
        ),
        out_shape=(jax.ShapeDtypeStruct((tokens // 2, features), BF16),) * 2,
        compiler_params=PARAMS,
        name="back_product",
    )(table, first, second, *attn_pieces, *fc_pieces)
    if not permute:
        order = jnp.argsort(table[1:])
        cut = [out.reshape(tokens // 2, blocks, features // blocks) for out in outs]
        outs = [jnp.take(out, order, axis=1).reshape(tokens // 2, features) for out in cut]
    return outs


def adamw(weight, gradient, moment, second):
    new_m = BETA_ONE * moment + (1.0 - BETA_ONE) * gradient
    new_v = BETA_TWO * second + (1.0 - BETA_TWO) * gradient * gradient
    m_hat = new_m / (1.0 - BETA_ONE**STEP_COUNT)
    v_hat = new_v / (1.0 - BETA_TWO**STEP_COUNT)
    update = -RATE * (m_hat / (jnp.sqrt(v_hat) + ADAM_EPS) + DECAY * weight.astype(F32))
    return (gradient, update, new_m, new_v)


def shards(
    inputs,
    ln_gain,
    ln_bias,
    qkv_weight,
    out_weight,
    fc1_weight,
    fc2_weight,
    cotangent,
    m_gain,
    v_gain,
    m_bias,
    v_bias,
    m_qkv,
    v_qkv,
    m_out,
    v_out,
    m_fc1,
    v_fc1,
    m_fc2,
    v_fc2,
):
    length = 2 * inputs.shape[0]
    block = length // 2
    count = 2 * lax.axis_size("h")
    table = feature_table()

    attn = Gather(spread(functools.partial(attention_block, qkv_weight, out_weight)))
    x, g = [inputs, swap(inputs, "t"), swap(inputs, "w")], [cotangent]
    x_other, g_other = [swap(inputs, "c")], [swap(cotangent, "c")]
    vectors = gather_vectors(jnp.stack([ln_gain, ln_bias]))
    x, g, x_other, g_other, vectors, fc1_late, fc2_late = close(attn, x, g, x_other, g_other, vectors, fc1_weight, fc2_weight)
    attn.over_h()
    attn.over_y_first()
    g += [swap(g[0], "t"), swap(g[0], "w")]
    x.append(swap(x[2], "t"))
    x_other += [swap(x[1], "c"), swap(x[2], "c"), swap(x[3], "c")]
    fc1 = Gather(spread(functools.partial(column_block, fc1_late)))
    x, g, x_other, g_other, vectors, fc2_late = close(attn, fc1, x, g, x_other, g_other, vectors, fc2_late)
    fc1.over_h()
    fc1.over_y_first()
    attn.over_y_rest()
    g.append(swap(g[2], "t"))
    g_other += [swap(g[1], "c"), swap(g[2], "c"), swap(g[3], "c")]
    gain_wide, bias_wide = vectors[:1].astype(F32), vectors[1:].astype(F32)
    fc2 = Gather(spread(functools.partial(column_block, fc2_late)))
    hidden = join(table, x + x_other, gain_wide, bias_wide, True)
    g, g_other, hidden = close(fc1, attn, fc2, g, g_other, hidden)
    fc2.over_h()
    fc2.over_y_first()
    fc1.over_y_rest()
    cotan = join(table, g + g_other, gain_wide, bias_wide, False)
    context, d_proj = attention(hidden, cotan, attn.pieces(), length)
    attn_parts = attention_grads(hidden, cotan, d_proj, context, block, count)
    hidden, cotan, context, d_proj, attn_parts = close(attn, fc1, fc2, hidden, cotan, context, d_proj, attn_parts)
    fc2.over_y_rest()
    attn_sum = Reduce(attn_parts)
    attn_sum.over_y_rest()
    act, slope, fc2_parts = fc1_pass(hidden, cotan, fc1.pieces(), block)
    hidden, cotan, context, d_proj, act, slope, fc2_parts = close(attn, fc1, fc2, attn_sum, hidden, cotan, context, d_proj, act, slope, fc2_parts)
    attn_sum.over_h()
    attn_sum.over_y_first()
    fc2_sum = Reduce(fc2_parts)
    fc2_sum.over_y_rest()
    start = d_proj.shape[1]
    d_pre, fc1_parts = fc2_pass(hidden, cotan, fc2.pieces(), slope, block)
    d_hidden = GroupSum(back_product(table, d_proj, d_pre, attn.pieces(), fc1.pieces(), 0, block))
    context, act, fc1_parts = close(attn, fc2, attn_sum, fc2_sum, d_hidden, context, act, fc1_parts)
    fc2_sum.over_h()
    fc2_sum.over_y_first()
    fc1_sum = Reduce(fc1_parts)
    fc1_sum.over_y_rest()
    d_hidden.over_c()
    d_hidden.corner()
    branch = GroupSum(back_product(table, context, act, attn.pieces(), fc2.pieces(), start, block))
    attn_pieces = collect(attn_sum.total())
    (attn_pieces,) = close(fc1_sum, fc2_sum, d_hidden, branch, attn_pieces)
    fc1_sum.over_h()
    fc1_sum.over_y_first()
    d_hidden.edges()
    branch.over_c()
    branch.corner()
    qkv_grad, out_grad = join_attention(attn_pieces)
    qkv_res = adamw(qkv_weight, qkv_grad, m_qkv, v_qkv)
    out_res = adamw(out_weight, out_grad, m_out, v_out)
    fc2_pieces = collect(fc2_sum.total())
    (fc2_pieces,) = close(fc1_sum, d_hidden, branch, fc2_pieces)
    branch.edges()
    fc1_res = adamw(fc1_weight, join_columns(collect(fc1_sum.total())), m_fc1, v_fc1)
    fc2_res = adamw(fc2_weight, join_columns(fc2_pieces), m_fc2, v_fc2)
    d_hidden = d_hidden.total()
    own_rows = inputs.astype(F32)
    output = (own_rows + branch.total()).astype(BF16)

    centred = own_rows - jnp.mean(own_rows, axis=1, keepdims=True)
    inv_std = lax.rsqrt(jnp.mean(centred * centred, axis=1, keepdims=True) + EPS_NORM)
    normed = centred * inv_std
    vector_parts = jnp.stack([jnp.sum(d_hidden * normed, axis=0), jnp.sum(d_hidden, axis=0)])
    vector_grads = sum_vectors(vector_parts)
    scaled_grad = d_hidden * vectors[:1].astype(F32)
    input_grad = cotangent.astype(F32) + inv_std * (
        scaled_grad
        - jnp.mean(scaled_grad, axis=1, keepdims=True)
        - normed * jnp.mean(scaled_grad * normed, axis=1, keepdims=True)
    )
    gain_res = adamw(ln_gain, vector_grads[0], m_gain, v_gain)
    bias_res = adamw(ln_bias, vector_grads[1], m_bias, v_bias)
    return (
        output,
        input_grad,
        *gain_res,
        *bias_res,
        *qkv_res,
        *out_res,
        *fc1_res,
        *fc2_res,
    )


def solution(mesh):
    dp, tensor = mesh.devices.shape
    inner = Mesh(mesh.devices.reshape(dp // 8, 2, 2, 2, tensor), ("h", "w", "y", "c", "t"))
    rows = P(("h", "w", "y", "c", "t"), None)
    vector = P(("h", "w", "y", "c"))
    stack = P(None, ("h", "w", "y", "c"), "t")
    matrix = P(("h", "w", "y", "c"), "t")
    return jax.shard_map(
        shards,
        mesh=inner,
        in_specs=(rows, vector, vector, stack, matrix, matrix, matrix, rows)
        + (vector,) * 4
        + (stack,) * 2
        + (matrix,) * 6,
        out_specs=(rows, rows) + (vector,) * 8 + (stack,) * 4 + (matrix,) * 12,
        check_vma=False,
    )
```

```python
import functools
import math

import jax
import jax.numpy as jnp
import numpy as np
from jax import lax
from jax.experimental import pallas as pl
from jax.experimental.pallas import tpu as pltpu
from jax.sharding import Mesh
from jax.sharding import PartitionSpec as P

HEAD = 64
ROT = 32
PAIR = 2 * HEAD
SCALE = HEAD ** (-0.5)

EPS_NORM = 1e-05
MASK_FILL = -1e30
BETA_ONE = 0.9
BETA_TWO = 0.95
ADAM_EPS = 1e-08
RATE = 0.02
DECAY = 0.1
STEP_COUNT = 10
GELU_ROOT = math.sqrt(2.0 / math.pi)
GELU_CUBE = 0.044715

BF16 = jnp.bfloat16
F32 = jnp.float32


def swap(value, axis):
    return lax.ppermute(value, axis, [(0, 1), (1, 0)])


def swap_inner(value, flip):
    return lax.ppermute(value, ("w", "c"), [(i, i ^ flip) for i in range(4)])


def ring(value):
    n = lax.axis_size("h")
    return lax.ppermute(value, "h", [(i, (i + 1) % n) for i in range(n)])


def inner_index():
    return 2 * lax.axis_index("w") + lax.axis_index("c")


def dp_index():
    outer = 2 * lax.axis_index("h") + lax.axis_index("w")
    return 4 * outer + 2 * lax.axis_index("y") + lax.axis_index("c")


def feature_table():
    n = lax.axis_size("h")
    h, w, y, c = (lax.axis_index(axis) for axis in "hwyc")
    entries = [lax.axis_index("t")]
    for flip_y in range(2):
        for back in range(n):
            for flip in range(4):
                outer = 2 * lax.rem(h + n - back, n) + (w ^ (flip >> 1))
                entries.append(4 * outer + 2 * (y ^ flip_y) + (c ^ (flip & 1)))
    return jnp.stack(entries).astype(jnp.int32)


def column_block(weight, j):
    width = weight.shape[-1] // 4
    return lax.dynamic_slice_in_dim(weight, j * width, width, weight.ndim - 1)


def attention_block(qkv_weight, out_weight, j):
    qkv = column_block(qkv_weight, j)
    return jnp.concatenate([qkv[0], qkv[1], qkv[2], column_block(out_weight, j)], axis=1)


def cut(piece_of):
    r = inner_index()
    return [piece_of(r ^ flip) for flip in range(4)]


def exchange(pieces):
    return [pieces[0]] + [swap_inner(piece, flip) for flip, piece in enumerate(pieces[1:], 1)]


def collect(total):
    r = inner_index()
    rows = total.shape[0] // 4
    pieces = [(r, total[:rows])]
    for flip in range(1, 4):
        pieces.append((r ^ flip, swap_inner(total[flip * rows : (flip + 1) * rows], flip)))
    return pieces


def join_columns(pieces):
    rows, width = pieces[0][1].shape
    out = jnp.zeros((rows, 4 * width), BF16)
    for j, piece in pieces:
        out = lax.dynamic_update_slice(out, piece, (0, j * width))
    return out.astype(F32)


def join_attention(pieces):
    rows, width = pieces[0][1].shape[0], pieces[0][1].shape[1] // 4
    parts = []
    for i in range(4):
        parts.append(join_columns([(j, piece[:, i * width : (i + 1) * width]) for j, piece in pieces]))
    return jnp.stack(parts[:3]), parts[3]


class Gather:
    def __init__(self, own):
        self.beside = [own]
        self.far = []

    def over_h(self):
        for _ in range(lax.axis_size("h") - 1):
            self.beside.append(ring(self.beside[-1]))

    def over_y_first(self):
        self.far.append(swap(self.beside[0], "y"))

    def over_y_rest(self):
        self.far += [swap(piece, "y") for piece in self.beside[1:]]

    def pieces(self):
        return self.beside + self.far


class Reduce:
    def __init__(self, parts):
        n = len(parts) // 2
        self.own, self.beside, self.own_far, self.far = parts[0], parts[1:n], parts[n], parts[n + 1 :]

    def over_y_rest(self):
        self.beside = [near + swap(far, "y") for near, far in zip(self.beside, self.far)]
        self.far = []

    def over_h(self):
        moving = None
        for near in self.beside:
            moving = ring(near if moving is None else near + moving)
        self.beside = [] if moving is None else [moving]

    def over_y_first(self):
        self.own_far = swap(self.own_far, "y")

    def total(self):
        total = self.own.astype(F32) + self.own_far.astype(F32)
        return sum((near.astype(F32) for near in self.beside), total).astype(BF16)


class GroupSum:
    def __init__(self, parts):
        self.mine, self.other = parts

    def over_c(self):
        self.other = swap(self.other, "c")

    def block(self, sequence, half):
        rows = self.mine.shape[0] // 4
        start = ((2 * sequence + half) * rows, 0)
        size = (rows, self.mine.shape[1])
        return lax.dynamic_slice(self.mine, start, size) + lax.dynamic_slice(self.other, start, size)

    def corner(self):
        self.moving = swap(self.block(1, 1 - lax.axis_index("t")), "t")

    def edges(self):
        t = lax.axis_index("t")
        self.turning = swap(self.block(1, t) + self.moving, "w")
        self.moving = swap(self.block(0, 1 - t), "t")

    def total(self):
        own = self.block(0, lax.axis_index("t"))
        return own.astype(F32) + self.moving.astype(F32) + self.turning.astype(F32)


def close(*items):
    holders = [vars(item) if isinstance(item, (Gather, Reduce, GroupSum)) else item for item in items]
    held = lax.optimization_barrier(holders)
    out = []
    for item, value in zip(items, held):
        if isinstance(item, (Gather, Reduce, GroupSum)):
            vars(item).update(value)
        else:
            out.append(value)
    return out


def shifted(value):
    n = 2 * lax.axis_size("h")
    return [
        lax.ppermute(value, ("h", "w"), [(i, (i + k) % n) for i in range(n)]) for k in range(1, n)
    ]


def place_vectors(pair):
    out = jnp.zeros((2, 8 * lax.axis_size("h") * pair.shape[1]), pair.dtype)
    return lax.dynamic_update_slice(out, pair, (0, dp_index() * pair.shape[1]))


def relative(vectors, table):
    rows, features = vectors.shape
    blocks = table.shape[0] - 1
    parts = jnp.take(vectors.reshape(rows, blocks, features // blocks), table[1:], axis=1)
    return parts.reshape(rows, features)


def own_part(sums):
    width = sums.shape[1] // (8 * lax.axis_size("h"))
    return lax.dynamic_slice(sums, (0, dp_index() * width), (2, width))


def lane_tables(length):
    position = np.arange(length, dtype=np.float32)[:, None]
    inverse = 10000.0 ** (-(np.arange(ROT // 2, dtype=np.float32) * 2.0 / ROT))
    angles = (position * inverse.astype(np.float32)[None, :]).astype(np.float64)
    cosine = jnp.asarray(np.cos(angles).astype(np.float32))
    sine = jnp.asarray(np.sin(angles).astype(np.float32))
    none = jnp.zeros_like(sine)
    rest = jnp.zeros((length, HEAD - ROT), F32)
    tables = (
        jnp.concatenate([cosine, cosine, rest + 1.0], axis=1),
        jnp.concatenate([sine, none, rest], axis=1),
        jnp.concatenate([none, sine, rest], axis=1),
    )
    return tuple(jnp.concatenate([table, table], axis=1) for table in tables)


def attention_body(proj_ref, grad_ref, cos_ref, low_ref, high_ref, context_ref, d_proj_ref):
    length, width = grad_ref.shape
    half = length // 2
    cosine, low, high = cos_ref[...], low_ref[...], high_ref[...]
    first = lax.broadcasted_iota(jnp.int32, (length, PAIR), 1) < HEAD
    row = lax.broadcasted_iota(jnp.int32, (half, half), 0)
    col = lax.broadcasted_iota(jnp.int32, (half, half), 1)
    keep = row <= col

    def turn(value, sign):
        ahead = pltpu.roll(value, PAIR - ROT // 2, 1)
        behind = pltpu.roll(value, ROT // 2, 1)
        return value * cosine - sign * ahead * low + sign * behind * high

    def rows_by_rows(a, b):
        return lax.dot_general(a, b, (((1,), (1,)), ((), ())), preferred_element_type=F32)

    def turned(a, b):
        return lax.dot_general(a, b, (((0,), (0,)), ((), ())), preferred_element_type=F32)

    def plain(a, b):
        return lax.dot_general(a, b, (((1,), (0,)), ((), ())), preferred_element_type=F32)

    def over_keys(function, value):
        return function(value, axis=0, keepdims=True)

    for pair in range(width // PAIR):
        lanes = pl.ds(pair * PAIR, PAIR)
        key_lanes = pl.ds(width + pair * PAIR, PAIR)
        value_lanes = pl.ds(2 * width + pair * PAIR, PAIR)
        query = (turn(proj_ref[:, lanes], 1.0).astype(BF16).astype(F32) * SCALE).astype(BF16)
        keys = turn(proj_ref[:, key_lanes], 1.0).astype(BF16)
        values = proj_ref[:, value_lanes].astype(BF16)
        grad = grad_ref[:, lanes]
        context = jnp.zeros((length, PAIR), F32)
        d_query = context
        d_keys_a = d_keys_b = d_values_a = d_values_b = jnp.zeros((half, PAIR), F32)
        for head in range(2):
            mine = first if head == 0 else jnp.logical_not(first)
            q, k, v, g = (
                jnp.where(mine, item, jnp.zeros_like(item)) for item in (query, keys, values, grad)
            )
            qa, qb, ga, gb = q[:half], q[half:], g[:half], g[half:]
            s_aa = jnp.where(keep, rows_by_rows(keys[:half], qa), MASK_FILL)
            s_ab = rows_by_rows(keys[:half], qb)
            s_bb = jnp.where(keep, rows_by_rows(keys[half:], qb), MASK_FILL)
            max_a = over_keys(jnp.max, s_aa)
            max_b = jnp.maximum(over_keys(jnp.max, s_ab), over_keys(jnp.max, s_bb))
            e_aa, e_ab, e_bb = jnp.exp(s_aa - max_a), jnp.exp(s_ab - max_b), jnp.exp(s_bb - max_b)
            inv_a = 1.0 / over_keys(jnp.sum, e_aa)
            inv_b = 1.0 / (over_keys(jnp.sum, e_ab) + over_keys(jnp.sum, e_bb))
            p_aa, p_ab, p_bb = e_aa * inv_a, e_ab * inv_b, e_bb * inv_b
            r_aa, r_ab, r_bb = p_aa.astype(BF16), p_ab.astype(BF16), p_bb.astype(BF16)
            d_aa = rows_by_rows(values[:half], ga)
            d_ab = rows_by_rows(values[:half], gb)
            d_bb = rows_by_rows(values[half:], gb)
            centre_a = over_keys(jnp.sum, d_aa * p_aa)
            centre_b = over_keys(jnp.sum, d_ab * p_ab) + over_keys(jnp.sum, d_bb * p_bb)
            t_aa = (p_aa * (d_aa - centre_a)).astype(BF16)
            t_ab = (p_ab * (d_ab - centre_b)).astype(BF16)
            t_bb = (p_bb * (d_bb - centre_b)).astype(BF16)
            context += jnp.concatenate(
                [turned(r_aa, v[:half]), turned(r_ab, v[:half]) + turned(r_bb, v[half:])]
            )
            d_query += jnp.concatenate(
                [turned(t_aa, k[:half]), turned(t_ab, k[:half]) + turned(t_bb, k[half:])]
            )
            d_keys_a += plain(t_aa, qa) + plain(t_ab, qb)
            d_keys_b += plain(t_bb, qb)
            d_values_a += plain(r_aa, ga) + plain(r_ab, gb)
            d_values_b += plain(r_bb, gb)
        context_ref[:, lanes] = context.astype(BF16)
        d_proj_ref[:, lanes] = turn(d_query * SCALE, -1.0).astype(BF16)
        d_keys = jnp.concatenate([d_keys_a, d_keys_b])
        d_proj_ref[:, key_lanes] = turn(d_keys, -1.0).astype(BF16)
        d_proj_ref[:, value_lanes] = jnp.concatenate([d_values_a, d_values_b]).astype(BF16)


def dot_nn(a, b):
    return lax.dot_general(a, b, (((1,), (0,)), ((), ())), preferred_element_type=F32)


def dot_nt(a, b):
    return lax.dot_general(a, b, (((1,), (1,)), ((), ())), preferred_element_type=F32)


def dot_tn(a, b):
    return lax.dot_general(a, b, (((0,), (0,)), ((), ())), preferred_element_type=F32)


def rows_of(block, width):
    return pl.BlockSpec((block, width), lambda s: (s, 0))


def whole(shape):
    return pl.BlockSpec(shape, lambda s: (0, 0), pipeline_mode=pl.Buffered(1))


ANYWHERE = pl.BlockSpec(memory_space=pl.ANY)
PARAMS = pltpu.CompilerParams(vmem_limit_bytes=58 << 20)


def fetch(piece_refs, into_ref, sem_ref, start=0):
    width = into_ref.shape[1]

    @pl.when(pl.program_id(0) == 0)
    def _():
        copies = []
        for i, piece in enumerate(piece_refs):
            rows = piece.shape[0]
            copies.append(
                pltpu.make_async_copy(
                    piece.at[:, pl.ds(start, width)],
                    into_ref.at[pl.ds(i * rows, rows), :],
                    sem_ref.at[i],
                )
            )
        for copy in copies:
            copy.start()
        for copy in copies:
            copy.wait()


def add_and_flush(total_ref, part_refs, addends):
    step = pl.program_id(0)

    @pl.when(step == 0)
    def _():
        total_ref[...] = jnp.zeros_like(total_ref)

    for lanes, addend in addends:
        total_ref[:, lanes] += addend()

    @pl.when(step == pl.num_programs(0) - 1)
    def _():
        rows = part_refs[0].shape[0]
        for i, part_ref in enumerate(part_refs):
            part_ref[...] = total_ref[i * rows : (i + 1) * rows, :].astype(BF16)


def attention_step(table_ref, gain_ref, bias_ref, cos_ref, low_ref, high_ref, *refs, permute):
    x_pieces, g_pieces, pieces, refs = refs[:8], refs[8:16], refs[16:-12], refs[-12:]
    context_ref, d_proj_ref, hidden_ref, cotan_ref, cols_ref, proj_ref, grad_ref = refs[:7]
    x_buffer, g_buffer, x_sems, g_sems, sems = refs[7:]
    step = pl.program_id(0)
    length, features = hidden_ref.shape
    half = length // 2
    blocks = table_ref.shape[0] - 1 if permute else 1
    size = features // blocks

    def start(sequence):
        slot = sequence % 2
        for i in range(2):
            side = table_ref[0] if i == 0 else 1 - table_ref[0]
            rows = pl.ds(pl.multiple_of(side * half, half), half)

            def block(j, carry, i=i, rows=rows):
                entry = table_ref[1 + j] if permute else 0
                of = pl.ds(pl.multiple_of(entry * size, size), size)
                to = pl.ds(pl.multiple_of(j * size, size), size)
                for sources, buffer, buffer_sems in (
                    (x_pieces, x_buffer, x_sems),
                    (g_pieces, g_buffer, g_sems),
                ):
                    pltpu.make_async_copy(
                        sources[2 * sequence + i].at[:, of],
                        buffer.at[slot, rows, to],
                        buffer_sems.at[slot],
                    ).start()
                return carry

            lax.fori_loop(0, blocks, block, 0)

    pl.when(step == 0)(lambda: start(0))
    for sequence in range(1, 4):
        pl.when(step == sequence - 1)(lambda sequence=sequence: start(sequence))
    fetch(pieces, cols_ref, sems)
    slot = lax.rem(step, 2)
    for buffer, buffer_sems in ((x_buffer, x_sems), (g_buffer, g_sems)):
        pltpu.make_async_copy(buffer.at[slot], buffer.at[slot], buffer_sems.at[slot]).wait()
    chunk = min(128, length)

    def normalize(i, carry):
        at = pl.ds(pl.multiple_of(i * chunk, chunk), chunk)
        rows = x_buffer[slot, at, :].astype(F32)
        centred = rows - jnp.mean(rows, axis=1, keepdims=True)
        inv_std = lax.rsqrt(jnp.mean(centred * centred, axis=1, keepdims=True) + EPS_NORM)
        hidden_ref[at, :] = (centred * inv_std * gain_ref[...] + bias_ref[...]).astype(BF16)
        return carry

    lax.fori_loop(0, length // chunk, normalize, 0)
    cotan_ref[...] = g_buffer[slot]
    width = grad_ref.shape[1]
    proj_ref[...] = dot_nn(hidden_ref[...], cols_ref[:, : 3 * width])
    grad_ref[...] = dot_nn(cotan_ref[...], cols_ref[:, 3 * width :]).astype(BF16)
    attention_body(proj_ref, grad_ref, cos_ref, low_ref, high_ref, context_ref, d_proj_ref)


def attention(table, x_pieces, g_pieces, gain, bias, pieces):
    half, features = x_pieces[0].shape
    length, tokens = 2 * half, 8 * half
    width = pieces[0].shape[1] // 4
    permute = features // (table.shape[0] - 1) % 128 == 0
    if not permute:
        x_pieces = [relative(piece, table) for piece in x_pieces]
        g_pieces = [relative(piece, table) for piece in g_pieces]

    def rows(columns):
        return pl.BlockSpec((length, columns), lambda s, h: (s, 0))

    def fixed(shape):
        return pl.BlockSpec(shape, lambda s, h: (0, 0), pipeline_mode=pl.Buffered(1))

    widths = (width, 3 * width, features, features)
    return pl.pallas_call(
        functools.partial(attention_step, permute=permute),
        grid_spec=pltpu.PrefetchScalarGridSpec(
            num_scalar_prefetch=1,
            grid=(4,),
            in_specs=[fixed((1, features))] * 2
            + [fixed((length, PAIR))] * 3
            + [ANYWHERE] * (16 + len(pieces)),
            out_specs=[rows(columns) for columns in widths],
            scratch_shapes=[
                pltpu.VMEM((features, 4 * width), BF16),
                pltpu.VMEM((length, 3 * width), F32),
                pltpu.VMEM((length, width), BF16),
                pltpu.VMEM((2, length, features), BF16),
                pltpu.VMEM((2, length, features), BF16),
                pltpu.SemaphoreType.DMA((2,)),
                pltpu.SemaphoreType.DMA((2,)),
                pltpu.SemaphoreType.DMA((len(pieces),)),
            ],
        ),
        out_shape=[jax.ShapeDtypeStruct((tokens, columns), BF16) for columns in widths],
        compiler_params=PARAMS,
        name="attention",
    )(table, gain, bias, *lane_tables(length), *x_pieces, *g_pieces, *pieces)


def parts_of(count, features, width):
    rows = features // count
    shapes = [jax.ShapeDtypeStruct((rows, width), BF16)] * count
    return [whole((rows, width))] * count, shapes, [pltpu.VMEM((features, width), F32)]


def attention_grads_step(hidden_ref, cotan_ref, d_proj_ref, context_ref, *refs):
    wide = d_proj_ref.shape[1]
    add_and_flush(
        refs[-1],
        refs[:-1],
        [
            (pl.ds(0, wide), lambda: dot_tn(hidden_ref[...], d_proj_ref[...])),
            (pl.ds(wide, wide // 3), lambda: dot_tn(cotan_ref[...], context_ref[...])),
        ],
    )


def attention_grads(hidden, cotan, d_proj, context, block, count):
    tokens, features = hidden.shape
    width = context.shape[1]
    specs, shapes, scratch = parts_of(count, features, 4 * width)
    return pl.pallas_call(
        attention_grads_step,
        grid=(tokens // block,),
        in_specs=[rows_of(block, features)] * 2 + [rows_of(block, 3 * width), rows_of(block, width)],
        out_specs=specs,
        out_shape=shapes,
        scratch_shapes=scratch,
        compiler_params=PARAMS,
        name="attention_grads",
    )(hidden, cotan, d_proj, context)


def fc1_step(hidden_ref, cotan_ref, *refs, count):
    pieces, (act_ref, slope_ref), parts = refs[:count], refs[count : count + 2], refs[count + 2 : -3]
    cols_ref, total_ref, sems = refs[-3:]
    fetch(pieces, cols_ref, sems)
    pre = dot_nn(hidden_ref[...], cols_ref[...])
    square = pre * pre
    tanh = jnp.tanh(GELU_ROOT * (pre + GELU_CUBE * (pre * square)))
    half = 0.5 * (1.0 + tanh)
    slope = 0.5 * GELU_ROOT * pre * (1.0 - tanh * tanh) * (1.0 + 3.0 * GELU_CUBE * square)
    act_ref[...] = (pre * half).astype(BF16)
    slope_ref[...] = half + slope
    every = pl.ds(0, total_ref.shape[1])
    add_and_flush(total_ref, parts, [(every, lambda: dot_tn(cotan_ref[...], act_ref[...]))])


def fc1_pass(hidden, cotan, pieces, block):
    tokens, features = hidden.shape
    count, width = len(pieces), pieces[0].shape[1]
    specs, shapes, scratch = parts_of(count, features, width)
    act, slope, *parts = pl.pallas_call(
        functools.partial(fc1_step, count=count),
        grid=(tokens // block,),
        in_specs=[rows_of(block, features)] * 2 + [ANYWHERE] * count,
        out_specs=[rows_of(block, width)] * 2 + specs,
        out_shape=[
            jax.ShapeDtypeStruct((tokens, width), BF16),
            jax.ShapeDtypeStruct((tokens, width), F32),
            *shapes,
        ],
        scratch_shapes=[
            pltpu.VMEM((features, width), BF16),
            *scratch,
            pltpu.SemaphoreType.DMA((count,)),
        ],
        compiler_params=PARAMS,
        name="fc1_pass",
    )(hidden, cotan, *pieces)
    return act, slope, parts


def fc2_step(hidden_ref, cotan_ref, slope_ref, *refs, count):
    pieces, d_pre_ref, parts = refs[:count], refs[count], refs[count + 1 : -3]
    cols_ref, total_ref, sems = refs[-3:]
    fetch(pieces, cols_ref, sems)
    d_pre_ref[...] = (dot_nn(cotan_ref[...], cols_ref[...]) * slope_ref[...]).astype(BF16)
    every = pl.ds(0, total_ref.shape[1])
    add_and_flush(total_ref, parts, [(every, lambda: dot_tn(hidden_ref[...], d_pre_ref[...]))])


def fc2_pass(hidden, cotan, pieces, slope, block):
    tokens, features = hidden.shape
    count, width = len(pieces), pieces[0].shape[1]
    specs, shapes, scratch = parts_of(count, features, width)
    d_pre, *parts = pl.pallas_call(
        functools.partial(fc2_step, count=count),
        grid=(tokens // block,),
        in_specs=[rows_of(block, features)] * 2 + [rows_of(block, width)] + [ANYWHERE] * count,
        out_specs=[rows_of(block, width)] + specs,
        out_shape=[jax.ShapeDtypeStruct((tokens, width), BF16), *shapes],
        scratch_shapes=[
            pltpu.VMEM((features, width), BF16),
            *scratch,
            pltpu.SemaphoreType.DMA((count,)),
        ],
        compiler_params=PARAMS,
        name="fc2_pass",
    )(hidden, cotan, slope, *pieces)
    return d_pre, parts


def back_step(table_ref, first_ref, second_ref, *refs, count, start, permute):
    attn_pieces, fc_pieces, (mine_ref, other_ref) = refs[:count], refs[count:-6], refs[-6:-4]
    attn_ref, fc_ref, attn_sems, fc_sems = refs[-4:]
    fetch(attn_pieces, attn_ref, attn_sems, start)
    fetch(fc_pieces, fc_ref, fc_sems)
    out = dot_nt(first_ref[...], attn_ref[...]) + dot_nt(second_ref[...], fc_ref[...])
    out = out.astype(BF16)
    middle = pl.num_programs(0) // 2
    blocks = table_ref.shape[0] - 1
    size = out.shape[1] // blocks

    def store(out_ref):
        if not permute:
            out_ref[...] = out
            return
        for j in range(blocks):
            lanes = pl.ds(pl.multiple_of(table_ref[1 + j] * size, size), size)
            out_ref[:, lanes] = out[:, j * size : (j + 1) * size]

    pl.when(pl.program_id(0) < middle)(lambda: store(mine_ref))
    pl.when(pl.program_id(0) >= middle)(lambda: store(other_ref))


def back_product(table, first, second, attn_pieces, fc_pieces, start, block):
    (tokens, size), width = first.shape, second.shape[1]
    count = len(attn_pieces)
    features = count * attn_pieces[0].shape[0]
    blocks = table.shape[0] - 1
    permute = features // blocks % 128 == 0
    middle = tokens // block // 2
    outs = pl.pallas_call(
        functools.partial(back_step, count=count, start=start, permute=permute),
        grid_spec=pltpu.PrefetchScalarGridSpec(
            num_scalar_prefetch=1,
            grid=(tokens // block,),
            in_specs=[
                pl.BlockSpec((block, size), lambda s, h: (s, 0)),
                pl.BlockSpec((block, width), lambda s, h: (s, 0)),
            ]
            + [ANYWHERE] * (2 * count),
            out_specs=(
                pl.BlockSpec((block, features), lambda s, h: (jnp.minimum(s, middle - 1), 0)),
                pl.BlockSpec((block, features), lambda s, h: (jnp.maximum(s - middle, 0), 0)),
            ),
            scratch_shapes=[
                pltpu.VMEM((features, size), BF16),
                pltpu.VMEM((features, width), BF16),
                pltpu.SemaphoreType.DMA((count,)),
                pltpu.SemaphoreType.DMA((count,)),
            ],
        ),
        out_shape=(jax.ShapeDtypeStruct((tokens // 2, features), BF16),) * 2,
        compiler_params=PARAMS,
        name="back_product",
    )(table, first, second, *attn_pieces, *fc_pieces)
    if not permute:
        order = jnp.argsort(table[1:])
        cut = [out.reshape(tokens // 2, blocks, features // blocks) for out in outs]
        outs = [jnp.take(out, order, axis=1).reshape(tokens // 2, features) for out in cut]
    return outs


def adamw(weight, gradient, moment, second):
    new_m = BETA_ONE * moment + (1.0 - BETA_ONE) * gradient
    new_v = BETA_TWO * second + (1.0 - BETA_TWO) * gradient * gradient
    m_hat = new_m / (1.0 - BETA_ONE**STEP_COUNT)
    v_hat = new_v / (1.0 - BETA_TWO**STEP_COUNT)
    update = -RATE * (m_hat / (jnp.sqrt(v_hat) + ADAM_EPS) + DECAY * weight.astype(F32))
    return (gradient, update, new_m, new_v)


def shards(
    inputs,
    ln_gain,
    ln_bias,
    qkv_weight,
    out_weight,
    fc1_weight,
    fc2_weight,
    cotangent,
    m_gain,
    v_gain,
    m_bias,
    v_bias,
    m_qkv,
    v_qkv,
    m_out,
    v_out,
    m_fc1,
    v_fc1,
    m_fc2,
    v_fc2,
):
    length = 2 * inputs.shape[0]
    block = length // 2
    count = 2 * lax.axis_size("h")
    table = feature_table()

    first = exchange(
        cut(
            lambda j: jnp.concatenate(
                [attention_block(qkv_weight, out_weight, j), column_block(fc1_weight, j)], axis=1
            )
        )
    )
    fc2_cut = cut(functools.partial(column_block, fc2_weight))
    x, g = [inputs, swap(inputs, "t"), swap(inputs, "w")], [cotangent]
    vectors = place_vectors(jnp.stack([ln_gain, ln_bias]))
    vectors = vectors + swap(vectors, "y")
    vectors = vectors + swap(vectors, "c")
    first, x, g, fc2_cut, vectors = close(first, x, g, fc2_cut, vectors)
    split = 4 * (qkv_weight.shape[2] // 4)
    attn = Gather(jnp.concatenate([piece[:, :split] for piece in first]))
    attn.over_h()
    attn.over_y_first()
    others = shifted(vectors)
    x_other = [swap(piece, "c") for piece in x]
    x.append(swap(x[2], "t"))
    g += [swap(g[0], "t"), swap(g[0], "w")]
    fc1 = Gather(jnp.concatenate([piece[:, split:] for piece in first]))
    others, x_other, x, g, fc2_cut, vectors = close(
        others, x_other, attn, x, g, fc2_cut, fc1, vectors
    )
    vectors = sum(others, vectors)
    fc2 = Gather(jnp.concatenate(exchange(fc2_cut)))
    fc1.over_h()
    attn.over_y_rest()
    fc1.over_y_first()
    g.append(swap(g[2], "t"))
    x_late = swap(x[3], "c")
    g_other = [swap(piece, "c") for piece in g]
    g, x, x_other, x_late, g_other, vectors = close(
        fc1, attn, g, fc2, x, x_other, x_late, g_other, vectors
    )
    x_other.append(x_late)
    fc2.over_h()
    fc2.over_y_first()
    fc1.over_y_rest()
    affine = relative(vectors, table).astype(F32)
    context, d_proj, hidden, cotan = attention(
        table, x + x_other, g + g_other, affine[:1], affine[1:], attn.pieces()
    )
    attn_parts = attention_grads(hidden, cotan, d_proj, context, block, count)
    hidden, cotan, context, d_proj, attn_parts = close(
        attn, fc1, fc2, hidden, cotan, context, d_proj, attn_parts
    )
    fc2.over_y_rest()
    attn_sum = Reduce(attn_parts)
    attn_sum.over_y_rest()
    act, slope, fc2_parts = fc1_pass(hidden, cotan, fc1.pieces(), block)
    hidden, cotan, context, d_proj, act, slope, fc2_parts = close(attn, fc1, fc2, attn_sum, hidden, cotan, context, d_proj, act, slope, fc2_parts)
    attn_sum.over_h()
    attn_sum.over_y_first()
    fc2_sum = Reduce(fc2_parts)
    fc2_sum.over_y_rest()
    start = d_proj.shape[1]
    d_pre, fc1_parts = fc2_pass(hidden, cotan, fc2.pieces(), slope, block)
    d_hidden = GroupSum(back_product(table, d_proj, d_pre, attn.pieces(), fc1.pieces(), 0, block))
    context, act, fc1_parts = close(attn, fc2, attn_sum, fc2_sum, d_hidden, context, act, fc1_parts)
    fc2_sum.over_h()
    fc2_sum.over_y_first()
    fc1_sum = Reduce(fc1_parts)
    fc1_sum.over_y_rest()
    d_hidden.over_c()
    d_hidden.corner()
    branch = GroupSum(back_product(table, context, act, attn.pieces(), fc2.pieces(), start, block))
    attn_pieces = collect(attn_sum.total())
    (attn_pieces,) = close(fc1_sum, fc2_sum, d_hidden, branch, attn_pieces)
    fc1_sum.over_h()
    fc1_sum.over_y_first()
    d_hidden.edges()
    branch.over_c()
    branch.corner()
    qkv_grad, out_grad = join_attention(attn_pieces)
    qkv_res = adamw(qkv_weight, qkv_grad, m_qkv, v_qkv)
    out_res = adamw(out_weight, out_grad, m_out, v_out)
    fc2_total = fc2_sum.total()
    (fc2_total,) = close(fc1_sum, d_hidden, branch, fc2_total)
    fc1_pieces, fc2_pieces = collect(fc1_sum.total()), collect(fc2_total)
    d_hidden = d_hidden.total()
    own_rows = inputs.astype(F32)
    centred = own_rows - jnp.mean(own_rows, axis=1, keepdims=True)
    inv_std = lax.rsqrt(jnp.mean(centred * centred, axis=1, keepdims=True) + EPS_NORM)
    normed = centred * inv_std
    sums = jnp.stack([jnp.sum(d_hidden * normed, axis=0), jnp.sum(d_hidden, axis=0)])
    for axis in "cyt":
        sums = sums + swap(sums, axis)
    scaled_grad = d_hidden * vectors[:1].astype(F32)
    input_grad = cotangent.astype(F32) + inv_std * (
        scaled_grad
        - jnp.mean(scaled_grad, axis=1, keepdims=True)
        - normed * jnp.mean(scaled_grad * normed, axis=1, keepdims=True)
    )
    fc1_pieces, fc2_pieces, sums, input_grad = close(fc1_pieces, fc2_pieces, branch, sums, input_grad)
    others = shifted(sums)
    branch.edges()
    fc1_res = adamw(fc1_weight, join_columns(fc1_pieces), m_fc1, v_fc1)
    fc2_res = adamw(fc2_weight, join_columns(fc2_pieces), m_fc2, v_fc2)
    others, fc1_res, fc2_res, sums = close(others, branch, fc1_res, fc2_res, sums)
    output = (own_rows + branch.total()).astype(BF16)
    sums = own_part(sum(others, sums))
    gain_res = adamw(ln_gain, sums[0], m_gain, v_gain)
    bias_res = adamw(ln_bias, sums[1], m_bias, v_bias)
    return (
        output,
        input_grad,
        *gain_res,
        *bias_res,
        *qkv_res,
        *out_res,
        *fc1_res,
        *fc2_res,
    )


def solution(mesh):
    dp, tensor = mesh.devices.shape
    inner = Mesh(mesh.devices.reshape(dp // 8, 2, 2, 2, tensor), ("h", "w", "y", "c", "t"))
    rows = P(("h", "w", "y", "c", "t"), None)
    vector = P(("h", "w", "y", "c"))
    stack = P(None, ("h", "w", "y", "c"), "t")
    matrix = P(("h", "w", "y", "c"), "t")
    return jax.shard_map(
        shards,
        mesh=inner,
        in_specs=(rows, vector, vector, stack, matrix, matrix, matrix, rows)
        + (vector,) * 4
        + (stack,) * 2
        + (matrix,) * 6,
        out_specs=(rows, rows) + (vector,) * 8 + (stack,) * 4 + (matrix,) * 12,
        check_vma=False,
    )
```

```python
import functools
import math

import jax
import jax.numpy as jnp
import numpy as np
from jax import lax
from jax.experimental import pallas as pl
from jax.experimental.pallas import tpu as pltpu
from jax.sharding import Mesh
from jax.sharding import PartitionSpec as P

HEAD = 64
ROT = 32
PAIR = 2 * HEAD
SCALE = HEAD ** (-0.5)

EPS_NORM = 1e-05
MASK_FILL = -1e30
BETA_ONE = 0.9
BETA_TWO = 0.95
ADAM_EPS = 1e-08
RATE = 0.02
DECAY = 0.1
STEP_COUNT = 10
GELU_ROOT = math.sqrt(2.0 / math.pi)
GELU_CUBE = 0.044715

BF16 = jnp.bfloat16
F32 = jnp.float32


def swap(value, axis):
    return lax.ppermute(value, axis, [(0, 1), (1, 0)])


def ring(value):
    n = lax.axis_size("h")
    return lax.ppermute(value, "h", [(i, (i + 1) % n) for i in range(n)])


def inner_index():
    return 2 * lax.axis_index("w") + lax.axis_index("c")


def dp_index():
    outer = 2 * lax.axis_index("h") + lax.axis_index("w")
    return 4 * outer + 2 * lax.axis_index("y") + lax.axis_index("c")


def feature_table():
    n = lax.axis_size("h")
    h, w, y, c = (lax.axis_index(axis) for axis in "hwyc")
    entries = [lax.axis_index("t")]
    for flip_y in range(2):
        for back in range(n):
            for flip in range(4):
                outer = 2 * lax.rem(h + n - back, n) + (w ^ (flip >> 1))
                entries.append(4 * outer + 2 * (y ^ flip_y) + (c ^ (flip & 1)))
    return jnp.stack(entries).astype(jnp.int32)


def column_block(weight, j):
    width = weight.shape[-1] // 4
    return lax.dynamic_slice_in_dim(weight, j * width, width, weight.ndim - 1)


def attention_block(qkv_weight, out_weight, j):
    qkv = column_block(qkv_weight, j)
    return jnp.concatenate([qkv[0], qkv[1], qkv[2], column_block(out_weight, j)], axis=1)


def cut(piece_of):
    r = inner_index()
    return [piece_of(r), piece_of(r ^ 1), jnp.concatenate([piece_of(r ^ 2), piece_of(r ^ 3)])]


def exchange(blocks):
    own, beside, across = blocks
    rows = own.shape[0]
    across = swap(across, "w")
    both = swap(jnp.concatenate([beside, across[rows:]]), "c")
    return [own, both[:rows], across[:rows], both[rows:]]


def exchange_directly(pieces):
    out = pieces[:1]
    for flip in range(1, 4):
        out.append(lax.ppermute(pieces[flip], ("w", "c"), [(i, i ^ flip) for i in range(4)]))
    return out


def collect(total):
    r = inner_index()
    rows = total.shape[0] // 4
    pieces = exchange([total[:rows], total[rows : 2 * rows], total[2 * rows :]])
    return [(r ^ flip, piece) for flip, piece in enumerate(pieces)]


def join_columns(pieces):
    rows, width = pieces[0][1].shape
    out = jnp.zeros((rows, 4 * width), BF16)
    for j, piece in pieces:
        out = lax.dynamic_update_slice(out, piece, (0, j * width))
    return out.astype(F32)


def join_attention(pieces):
    rows, width = pieces[0][1].shape[0], pieces[0][1].shape[1] // 4
    parts = []
    for i in range(4):
        parts.append(join_columns([(j, piece[:, i * width : (i + 1) * width]) for j, piece in pieces]))
    return jnp.stack(parts[:3]), parts[3]


class Gather:
    def __init__(self, own):
        self.beside = [own]
        self.far = []

    def over_h(self):
        for _ in range(lax.axis_size("h") - 1):
            self.beside.append(ring(self.beside[-1]))

    def over_y_first(self):
        self.far.append(swap(self.beside[0], "y"))

    def over_y_rest(self):
        self.far += [swap(piece, "y") for piece in self.beside[1:]]

    def pieces(self):
        return self.beside + self.far


class Reduce:
    def __init__(self, parts):
        n = len(parts) // 2
        self.own, self.beside, self.own_far, self.far = parts[0], parts[1:n], parts[n], parts[n + 1 :]

    def over_y_rest(self):
        self.beside = [near + swap(far, "y") for near, far in zip(self.beside, self.far)]
        self.far = []

    def over_h(self):
        moving = None
        for near in self.beside:
            moving = ring(near if moving is None else near + moving)
        self.beside = [] if moving is None else [moving]

    def over_y_first(self):
        self.own_far = swap(self.own_far, "y")

    def total(self):
        total = self.own.astype(F32) + self.own_far.astype(F32)
        return sum((near.astype(F32) for near in self.beside), total).astype(BF16)


class GroupSum:
    def __init__(self, parts):
        self.mine, self.other = parts

    def over_c(self):
        self.other = swap(self.other, "c")

    def block(self, sequence, half):
        rows = self.mine.shape[0] // 4
        start = ((2 * sequence + half) * rows, 0)
        size = (rows, self.mine.shape[1])
        return lax.dynamic_slice(self.mine, start, size) + lax.dynamic_slice(self.other, start, size)

    def corner(self):
        t = lax.axis_index("t")
        self.moving = swap(self.block(1, 1 - t), "t")
        self.across, self.beside, own = self.block(1, t), self.block(0, 1 - t), self.block(0, t)
        self.mine, self.other = own, None

    def edges(self):
        self.across = swap(self.across + self.moving, "w")
        self.beside = swap(self.beside, "t")
        self.moving = None

    def total(self):
        return self.mine.astype(F32) + self.across.astype(F32) + self.beside.astype(F32)


def close(*items):
    holders = [vars(item) if isinstance(item, (Gather, Reduce, GroupSum)) else item for item in items]
    held = lax.optimization_barrier(holders)
    out = []
    for item, value in zip(items, held):
        if isinstance(item, (Gather, Reduce, GroupSum)):
            vars(item).update(value)
        else:
            out.append(value)
    return out


def shifted(value):
    n = 2 * lax.axis_size("h")
    return [
        lax.ppermute(value, ("h", "w"), [(i, (i + k) % n) for i in range(n)]) for k in range(1, n)
    ]


def place_vectors(pair):
    out = jnp.zeros((2, 8 * lax.axis_size("h") * pair.shape[1]), pair.dtype)
    return lax.dynamic_update_slice(out, pair, (0, dp_index() * pair.shape[1]))


def relative(vectors, table):
    rows, features = vectors.shape
    blocks = table.shape[0] - 1
    parts = jnp.take(vectors.reshape(rows, blocks, features // blocks), table[1:], axis=1)
    return parts.reshape(rows, features)


def own_part(sums):
    width = sums.shape[1] // (8 * lax.axis_size("h"))
    return lax.dynamic_slice(sums, (0, dp_index() * width), (2, width))


def lane_tables(length):
    position = np.arange(length, dtype=np.float32)[:, None]
    inverse = 10000.0 ** (-(np.arange(ROT // 2, dtype=np.float32) * 2.0 / ROT))
    angles = (position * inverse.astype(np.float32)[None, :]).astype(np.float64)
    cosine = jnp.asarray(np.cos(angles).astype(np.float32))
    sine = jnp.asarray(np.sin(angles).astype(np.float32))
    none = jnp.zeros_like(sine)
    rest = jnp.zeros((length, HEAD - ROT), F32)
    tables = (
        jnp.concatenate([cosine, cosine, rest + 1.0], axis=1),
        jnp.concatenate([sine, none, rest], axis=1),
        jnp.concatenate([none, sine, rest], axis=1),
    )
    return tuple(jnp.concatenate([table, table], axis=1) for table in tables)


def attention_body(proj_ref, grad_ref, cos_ref, low_ref, high_ref, context_ref, d_proj_ref):
    length, width = grad_ref.shape
    half = length // 2
    cosine, low, high = cos_ref[...], low_ref[...], high_ref[...]
    first = lax.broadcasted_iota(jnp.int32, (length, PAIR), 1) < HEAD
    row = lax.broadcasted_iota(jnp.int32, (half, half), 0)
    col = lax.broadcasted_iota(jnp.int32, (half, half), 1)
    keep = row <= col

    def turn(value, sign):
        ahead = pltpu.roll(value, PAIR - ROT // 2, 1)
        behind = pltpu.roll(value, ROT // 2, 1)
        return value * cosine - sign * ahead * low + sign * behind * high

    def rows_by_rows(a, b):
        return lax.dot_general(a, b, (((1,), (1,)), ((), ())), preferred_element_type=F32)

    def turned(a, b):
        return lax.dot_general(a, b, (((0,), (0,)), ((), ())), preferred_element_type=F32)

    def plain(a, b):
        return lax.dot_general(a, b, (((1,), (0,)), ((), ())), preferred_element_type=F32)

    def over_keys(function, value):
        return function(value, axis=0, keepdims=True)

    for pair in range(width // PAIR):
        lanes = pl.ds(pair * PAIR, PAIR)
        key_lanes = pl.ds(width + pair * PAIR, PAIR)
        value_lanes = pl.ds(2 * width + pair * PAIR, PAIR)
        query = (turn(proj_ref[:, lanes], 1.0).astype(BF16).astype(F32) * SCALE).astype(BF16)
        keys = turn(proj_ref[:, key_lanes], 1.0).astype(BF16)
        values = proj_ref[:, value_lanes].astype(BF16)
        grad = grad_ref[:, lanes]
        context = jnp.zeros((length, PAIR), F32)
        d_query = context
        d_keys_a = d_keys_b = d_values_a = d_values_b = jnp.zeros((half, PAIR), F32)
        for head in range(2):
            mine = first if head == 0 else jnp.logical_not(first)
            q, k, v, g = (
                jnp.where(mine, item, jnp.zeros_like(item)) for item in (query, keys, values, grad)
            )
            qa, qb, ga, gb = q[:half], q[half:], g[:half], g[half:]
            s_aa = jnp.where(keep, rows_by_rows(keys[:half], qa), MASK_FILL)
            s_ab = rows_by_rows(keys[:half], qb)
            s_bb = jnp.where(keep, rows_by_rows(keys[half:], qb), MASK_FILL)
            max_a = over_keys(jnp.max, s_aa)
            max_b = jnp.maximum(over_keys(jnp.max, s_ab), over_keys(jnp.max, s_bb))
            e_aa, e_ab, e_bb = jnp.exp(s_aa - max_a), jnp.exp(s_ab - max_b), jnp.exp(s_bb - max_b)
            inv_a = 1.0 / over_keys(jnp.sum, e_aa)
            inv_b = 1.0 / (over_keys(jnp.sum, e_ab) + over_keys(jnp.sum, e_bb))
            p_aa, p_ab, p_bb = e_aa * inv_a, e_ab * inv_b, e_bb * inv_b
            r_aa, r_ab, r_bb = p_aa.astype(BF16), p_ab.astype(BF16), p_bb.astype(BF16)
            d_aa = rows_by_rows(values[:half], ga)
            d_ab = rows_by_rows(values[:half], gb)
            d_bb = rows_by_rows(values[half:], gb)
            centre_a = over_keys(jnp.sum, d_aa * p_aa)
            centre_b = over_keys(jnp.sum, d_ab * p_ab) + over_keys(jnp.sum, d_bb * p_bb)
            t_aa = (p_aa * (d_aa - centre_a)).astype(BF16)
            t_ab = (p_ab * (d_ab - centre_b)).astype(BF16)
            t_bb = (p_bb * (d_bb - centre_b)).astype(BF16)
            context += jnp.concatenate(
                [turned(r_aa, v[:half]), turned(r_ab, v[:half]) + turned(r_bb, v[half:])]
            )
            d_query += jnp.concatenate(
                [turned(t_aa, k[:half]), turned(t_ab, k[:half]) + turned(t_bb, k[half:])]
            )
            d_keys_a += plain(t_aa, qa) + plain(t_ab, qb)
            d_keys_b += plain(t_bb, qb)
            d_values_a += plain(r_aa, ga) + plain(r_ab, gb)
            d_values_b += plain(r_bb, gb)
        context_ref[:, lanes] = context.astype(BF16)
        d_proj_ref[:, lanes] = turn(d_query * SCALE, -1.0).astype(BF16)
        d_keys = jnp.concatenate([d_keys_a, d_keys_b])
        d_proj_ref[:, key_lanes] = turn(d_keys, -1.0).astype(BF16)
        d_proj_ref[:, value_lanes] = jnp.concatenate([d_values_a, d_values_b]).astype(BF16)


def dot_nn(a, b):
    return lax.dot_general(a, b, (((1,), (0,)), ((), ())), preferred_element_type=F32)


def dot_nt(a, b):
    return lax.dot_general(a, b, (((1,), (1,)), ((), ())), preferred_element_type=F32)


def dot_tn(a, b):
    return lax.dot_general(a, b, (((0,), (0,)), ((), ())), preferred_element_type=F32)


def rows_of(block, width):
    return pl.BlockSpec((block, width), lambda s: (s, 0))


def whole(shape):
    return pl.BlockSpec(shape, lambda s: (0, 0), pipeline_mode=pl.Buffered(1))


ANYWHERE = pl.BlockSpec(memory_space=pl.ANY)
PARAMS = pltpu.CompilerParams(vmem_limit_bytes=58 << 20)


def fetches(piece_refs, into_ref, sem_ref, start=0, to=0, width=None):
    width = into_ref.shape[1] if width is None else width
    copies = []
    for i, piece in enumerate(piece_refs):
        rows = piece.shape[0]
        copies.append(
            pltpu.make_async_copy(
                piece.at[:, pl.ds(start, width)],
                into_ref.at[pl.ds(i * rows, rows), pl.ds(to, width)],
                sem_ref.at[i],
            )
        )
    return copies


def at_first(*copies, start=True, wait=True):
    @pl.when(pl.program_id(0) == 0)
    def _():
        if start:
            for copy in copies:
                copy.start()
        if wait:
            for copy in copies:
                copy.wait()


def add_and_flush(total_ref, part_refs, addends):
    step = pl.program_id(0)

    @pl.when(step == 0)
    def _():
        total_ref[...] = jnp.zeros_like(total_ref)

    for lanes, addend in addends:
        total_ref[:, lanes] += addend()

    @pl.when(step == pl.num_programs(0) - 1)
    def _():
        rows = part_refs[0].shape[0]
        for i, part_ref in enumerate(part_refs):
            part_ref[...] = total_ref[i * rows : (i + 1) * rows, :].astype(BF16)


def attention_step(table_ref, gain_ref, bias_ref, cos_ref, low_ref, high_ref, *refs, permute):
    x_pieces, g_pieces, pieces, refs = refs[:8], refs[8:16], refs[16:-12], refs[-12:]
    context_ref, d_proj_ref, hidden_ref, cotan_ref, cols_ref, proj_ref, grad_ref = refs[:7]
    x_buffer, g_buffer, x_sems, g_sems, sems = refs[7:]
    step = pl.program_id(0)
    length, features = hidden_ref.shape
    half = length // 2
    blocks = table_ref.shape[0] - 1 if permute else 1
    size = features // blocks

    def start(sequence):
        slot = sequence % 2
        for i in range(2):
            side = table_ref[0] if i == 0 else 1 - table_ref[0]
            rows = pl.ds(pl.multiple_of(side * half, half), half)

            def block(j, carry, i=i, rows=rows):
                entry = table_ref[1 + j] if permute else 0
                of = pl.ds(pl.multiple_of(entry * size, size), size)
                to = pl.ds(pl.multiple_of(j * size, size), size)
                for sources, buffer, buffer_sems in (
                    (x_pieces, x_buffer, x_sems),
                    (g_pieces, g_buffer, g_sems),
                ):
                    pltpu.make_async_copy(
                        sources[2 * sequence + i].at[:, of],
                        buffer.at[slot, rows, to],
                        buffer_sems.at[slot],
                    ).start()
                return carry

            lax.fori_loop(0, blocks, block, 0)

    pl.when(step == 0)(lambda: start(0))
    for sequence in range(1, 4):
        pl.when(step == sequence - 1)(lambda sequence=sequence: start(sequence))
    columns = fetches(pieces, cols_ref, sems)
    at_first(*columns, wait=False)
    slot = lax.rem(step, 2)
    for buffer, buffer_sems in ((x_buffer, x_sems), (g_buffer, g_sems)):
        pltpu.make_async_copy(buffer.at[slot], buffer.at[slot], buffer_sems.at[slot]).wait()
    chunk = min(128, length)

    def normalize(i, carry):
        at = pl.ds(pl.multiple_of(i * chunk, chunk), chunk)
        rows = x_buffer[slot, at, :].astype(F32)
        centred = rows - jnp.mean(rows, axis=1, keepdims=True)
        inv_std = lax.rsqrt(jnp.mean(centred * centred, axis=1, keepdims=True) + EPS_NORM)
        hidden_ref[at, :] = (centred * inv_std * gain_ref[...] + bias_ref[...]).astype(BF16)
        return carry

    lax.fori_loop(0, length // chunk, normalize, 0)
    cotan_ref[...] = g_buffer[slot]
    at_first(*columns, start=False)
    width = grad_ref.shape[1]
    proj_ref[...] = dot_nn(hidden_ref[...], cols_ref[:, : 3 * width])
    grad_ref[...] = dot_nn(cotan_ref[...], cols_ref[:, 3 * width :]).astype(BF16)
    attention_body(proj_ref, grad_ref, cos_ref, low_ref, high_ref, context_ref, d_proj_ref)


def attention(table, x_pieces, g_pieces, gain, bias, pieces):
    half, features = x_pieces[0].shape
    length, tokens = 2 * half, 8 * half
    width = pieces[0].shape[1] // 4
    permute = features // (table.shape[0] - 1) % 128 == 0
    if not permute:
        x_pieces = [relative(piece, table) for piece in x_pieces]
        g_pieces = [relative(piece, table) for piece in g_pieces]

    def rows(columns):
        return pl.BlockSpec((length, columns), lambda s, h: (s, 0))

    def fixed(shape):
        return pl.BlockSpec(shape, lambda s, h: (0, 0), pipeline_mode=pl.Buffered(1))

    widths = (width, 3 * width, features, features)
    return pl.pallas_call(
        functools.partial(attention_step, permute=permute),
        grid_spec=pltpu.PrefetchScalarGridSpec(
            num_scalar_prefetch=1,
            grid=(4,),
            in_specs=[fixed((1, features))] * 2
            + [fixed((length, PAIR))] * 3
            + [ANYWHERE] * (16 + len(pieces)),
            out_specs=[rows(columns) for columns in widths],
            scratch_shapes=[
                pltpu.VMEM((features, 4 * width), BF16),
                pltpu.VMEM((length, 3 * width), F32),
                pltpu.VMEM((length, width), BF16),
                pltpu.VMEM((2, length, features), BF16),
                pltpu.VMEM((2, length, features), BF16),
                pltpu.SemaphoreType.DMA((2,)),
                pltpu.SemaphoreType.DMA((2,)),
                pltpu.SemaphoreType.DMA((len(pieces),)),
            ],
        ),
        out_shape=[jax.ShapeDtypeStruct((tokens, columns), BF16) for columns in widths],
        compiler_params=PARAMS,
        name="attention",
    )(table, gain, bias, *lane_tables(length), *x_pieces, *g_pieces, *pieces)


def parts_of(count, features, width):
    rows = features // count
    shapes = [jax.ShapeDtypeStruct((rows, width), BF16)] * count
    return [whole((rows, width))] * count, shapes, [pltpu.VMEM((features, width), F32)]


def attention_grads_step(hidden_ref, cotan_ref, d_proj_ref, context_ref, *refs):
    wide = d_proj_ref.shape[1]
    add_and_flush(
        refs[-1],
        refs[:-1],
        [
            (pl.ds(0, wide), lambda: dot_tn(hidden_ref[...], d_proj_ref[...])),
            (pl.ds(wide, wide // 3), lambda: dot_tn(cotan_ref[...], context_ref[...])),
        ],
    )


def attention_grads(hidden, cotan, d_proj, context, block, count):
    tokens, features = hidden.shape
    width = context.shape[1]
    specs, shapes, scratch = parts_of(count, features, 4 * width)
    return pl.pallas_call(
        attention_grads_step,
        grid=(tokens // block,),
        in_specs=[rows_of(block, features)] * 2 + [rows_of(block, 3 * width), rows_of(block, width)],
        out_specs=specs,
        out_shape=shapes,
        scratch_shapes=scratch,
        compiler_params=PARAMS,
        name="attention_grads",
    )(hidden, cotan, d_proj, context)


def fc1_step(hidden_ref, cotan_ref, *refs, count):
    pieces, (act_ref, slope_ref), parts = refs[:count], refs[count : count + 2], refs[count + 2 : -3]
    cols_ref, total_ref, sems = refs[-3:]
    at_first(*fetches(pieces, cols_ref, sems))
    pre = dot_nn(hidden_ref[...], cols_ref[...])
    square = pre * pre
    tanh = jnp.tanh(pre * (GELU_ROOT + GELU_ROOT * GELU_CUBE * square))
    half = 0.5 + 0.5 * tanh
    steep = pre * (GELU_ROOT + 3.0 * GELU_ROOT * GELU_CUBE * square)
    act_ref[...] = (pre * half).astype(BF16)
    slope_ref[...] = half + half * (steep * (1.0 - tanh))
    every = pl.ds(0, total_ref.shape[1])
    add_and_flush(total_ref, parts, [(every, lambda: dot_tn(cotan_ref[...], act_ref[...]))])


def fc1_pass(hidden, cotan, pieces, block):
    tokens, features = hidden.shape
    count, width = len(pieces), pieces[0].shape[1]
    specs, shapes, scratch = parts_of(count, features, width)
    act, slope, *parts = pl.pallas_call(
        functools.partial(fc1_step, count=count),
        grid=(tokens // block,),
        in_specs=[rows_of(block, features)] * 2 + [ANYWHERE] * count,
        out_specs=[rows_of(block, width)] * 2 + specs,
        out_shape=[
            jax.ShapeDtypeStruct((tokens, width), BF16),
            jax.ShapeDtypeStruct((tokens, width), F32),
            *shapes,
        ],
        scratch_shapes=[
            pltpu.VMEM((features, width), BF16),
            *scratch,
            pltpu.SemaphoreType.DMA((count,)),
        ],
        compiler_params=PARAMS,
        name="fc1_pass",
    )(hidden, cotan, *pieces)
    return act, slope, parts


def fc2_step(hidden_ref, cotan_ref, slope_ref, *refs, count):
    pieces, d_pre_ref, parts = refs[:count], refs[count], refs[count + 1 : -3]
    cols_ref, total_ref, sems = refs[-3:]
    at_first(*fetches(pieces, cols_ref, sems))
    d_pre_ref[...] = (dot_nn(cotan_ref[...], cols_ref[...]) * slope_ref[...]).astype(BF16)
    every = pl.ds(0, total_ref.shape[1])
    add_and_flush(total_ref, parts, [(every, lambda: dot_tn(hidden_ref[...], d_pre_ref[...]))])


def fc2_pass(hidden, cotan, pieces, slope, block):
    tokens, features = hidden.shape
    count, width = len(pieces), pieces[0].shape[1]
    specs, shapes, scratch = parts_of(count, features, width)
    d_pre, *parts = pl.pallas_call(
        functools.partial(fc2_step, count=count),
        grid=(tokens // block,),
        in_specs=[rows_of(block, features)] * 2 + [rows_of(block, width)] + [ANYWHERE] * count,
        out_specs=[rows_of(block, width)] + specs,
        out_shape=[jax.ShapeDtypeStruct((tokens, width), BF16), *shapes],
        scratch_shapes=[
            pltpu.VMEM((features, width), BF16),
            *scratch,
            pltpu.SemaphoreType.DMA((count,)),
        ],
        compiler_params=PARAMS,
        name="fc2_pass",
    )(hidden, cotan, slope, *pieces)
    return d_pre, parts


def back_step(table_ref, first_ref, second_ref, *refs, count, start, permute):
    attn_pieces, fc_pieces, (mine_ref, other_ref) = refs[:count], refs[count:-6], refs[-6:-4]
    rows_ref, cols_ref, attn_sems, fc_sems = refs[-4:]
    size, width = first_ref.shape[1], second_ref.shape[1]
    at_first(
        *fetches(attn_pieces, cols_ref, attn_sems, start, 0, size),
        *fetches(fc_pieces, cols_ref, fc_sems, 0, size, width),
    )
    rows_ref[:, :size] = first_ref[...]
    rows_ref[:, size:] = second_ref[...]
    out = dot_nt(rows_ref[...], cols_ref[...])
    out = out.astype(BF16)
    middle = pl.num_programs(0) // 2
    blocks = table_ref.shape[0] - 1
    size = out.shape[1] // blocks

    def store(out_ref):
        if not permute:
            out_ref[...] = out
            return
        for j in range(blocks):
            lanes = pl.ds(pl.multiple_of(table_ref[1 + j] * size, size), size)
            out_ref[:, lanes] = out[:, j * size : (j + 1) * size]

    pl.when(pl.program_id(0) < middle)(lambda: store(mine_ref))
    pl.when(pl.program_id(0) >= middle)(lambda: store(other_ref))


def back_product(table, first, second, attn_pieces, fc_pieces, start, block):
    (tokens, size), width = first.shape, second.shape[1]
    count = len(attn_pieces)
    features = count * attn_pieces[0].shape[0]
    blocks = table.shape[0] - 1
    permute = features // blocks % 128 == 0
    middle = tokens // block // 2
    outs = pl.pallas_call(
        functools.partial(back_step, count=count, start=start, permute=permute),
        grid_spec=pltpu.PrefetchScalarGridSpec(
            num_scalar_prefetch=1,
            grid=(tokens // block,),
            in_specs=[
                pl.BlockSpec((block, size), lambda s, h: (s, 0)),
                pl.BlockSpec((block, width), lambda s, h: (s, 0)),
            ]
            + [ANYWHERE] * (2 * count),
            out_specs=(
                pl.BlockSpec((block, features), lambda s, h: (jnp.minimum(s, middle - 1), 0)),
                pl.BlockSpec((block, features), lambda s, h: (jnp.maximum(s - middle, 0), 0)),
            ),
            scratch_shapes=[
                pltpu.VMEM((block, size + width), BF16),
                pltpu.VMEM((features, size + width), BF16),
                pltpu.SemaphoreType.DMA((count,)),
                pltpu.SemaphoreType.DMA((count,)),
            ],
        ),
        out_shape=(jax.ShapeDtypeStruct((tokens // 2, features), BF16),) * 2,
        compiler_params=PARAMS,
        name="back_product",
    )(table, first, second, *attn_pieces, *fc_pieces)
    if not permute:
        order = jnp.argsort(table[1:])
        cut = [out.reshape(tokens // 2, blocks, features // blocks) for out in outs]
        outs = [jnp.take(out, order, axis=1).reshape(tokens // 2, features) for out in cut]
    return outs


def adamw(weight, gradient, moment, second):
    new_m = BETA_ONE * moment + (1.0 - BETA_ONE) * gradient
    new_v = BETA_TWO * second + (1.0 - BETA_TWO) * gradient * gradient
    m_hat = new_m / (1.0 - BETA_ONE**STEP_COUNT)
    v_hat = new_v / (1.0 - BETA_TWO**STEP_COUNT)
    update = -RATE * (m_hat / (jnp.sqrt(v_hat) + ADAM_EPS) + DECAY * weight.astype(F32))
    return (gradient, update, new_m, new_v)


def shards(
    inputs,
    ln_gain,
    ln_bias,
    qkv_weight,
    out_weight,
    fc1_weight,
    fc2_weight,
    cotangent,
    m_gain,
    v_gain,
    m_bias,
    v_bias,
    m_qkv,
    v_qkv,
    m_out,
    v_out,
    m_fc1,
    v_fc1,
    m_fc2,
    v_fc2,
):
    length = 2 * inputs.shape[0]
    block = length // 2
    count = 2 * lax.axis_size("h")
    table = feature_table()

    r = inner_index()
    vectors = place_vectors(jnp.stack([ln_gain, ln_bias]))
    for axis in "yc":
        vectors = vectors + swap(vectors, axis)
    first = [
        jnp.concatenate(
            [attention_block(qkv_weight, out_weight, r ^ flip), column_block(fc1_weight, r ^ flip)],
            axis=1,
        )
        for flip in range(4)
    ]
    first = exchange_directly(first)
    fc2_cut = cut(functools.partial(column_block, fc2_weight))
    x, g = [inputs, swap(inputs, "t"), swap(inputs, "w")], [cotangent]
    x[2], vectors = lax.optimization_barrier((x[2], vectors))
    others = shifted(vectors)
    first, x, g, fc2_cut, vectors, others = close(first, x, g, fc2_cut, vectors, others)
    split = 4 * (qkv_weight.shape[2] // 4)
    attn = Gather(jnp.concatenate([piece[:, :split] for piece in first]))
    attn.over_h()
    attn.over_y_first()
    vectors = sum(others, vectors)
    x_other = [swap(piece, "c") for piece in x]
    x.append(swap(x[2], "t"))
    g += [swap(g[0], "t"), swap(g[0], "w")]
    fc1 = Gather(jnp.concatenate([piece[:, split:] for piece in first]))
    x_other, x, g, fc2_cut, vectors = close(x_other, attn, x, g, fc2_cut, fc1, vectors)
    fc2 = Gather(jnp.concatenate(exchange(fc2_cut)))
    fc1.over_h()
    attn.over_y_rest()
    fc1.over_y_first()
    g.append(swap(g[2], "t"))
    x_late = swap(x[3], "c")
    g_other = [swap(piece, "c") for piece in g]
    g, x, x_other, x_late, g_other, vectors = close(
        fc1, attn, g, fc2, x, x_other, x_late, g_other, vectors
    )
    x_other.append(x_late)
    fc2.over_h()
    fc2.over_y_first()
    fc1.over_y_rest()
    affine = relative(vectors, table).astype(F32)
    context, d_proj, hidden, cotan = attention(
        table, x + x_other, g + g_other, affine[:1], affine[1:], attn.pieces()
    )
    attn_parts = attention_grads(hidden, cotan, d_proj, context, block, count)
    hidden, cotan, context, d_proj, attn_parts = close(
        attn, fc1, fc2, hidden, cotan, context, d_proj, attn_parts
    )
    fc2.over_y_rest()
    attn_sum = Reduce(attn_parts)
    attn_sum.over_y_rest()
    act, slope, fc2_parts = fc1_pass(hidden, cotan, fc1.pieces(), block)
    hidden, cotan, context, d_proj, act, slope, fc2_parts = close(attn, fc1, fc2, attn_sum, hidden, cotan, context, d_proj, act, slope, fc2_parts)
    attn_sum.over_h()
    attn_sum.over_y_first()
    fc2_sum = Reduce(fc2_parts)
    fc2_sum.over_y_rest()
    start = d_proj.shape[1]
    d_pre, fc1_parts = fc2_pass(hidden, cotan, fc2.pieces(), slope, block)
    d_hidden = GroupSum(back_product(table, d_proj, d_pre, attn.pieces(), fc1.pieces(), 0, block))
    context, act, fc1_parts = close(attn, fc2, attn_sum, fc2_sum, d_hidden, context, act, fc1_parts)
    fc2_sum.over_h()
    fc2_sum.over_y_first()
    fc1_sum = Reduce(fc1_parts)
    fc1_sum.over_y_rest()
    d_hidden.over_c()
    d_hidden.corner()
    branch = GroupSum(back_product(table, context, act, attn.pieces(), fc2.pieces(), start, block))
    attn_pieces = collect(attn_sum.total())
    (attn_pieces,) = close(attn_pieces, fc1_sum, fc2_sum, d_hidden, branch)
    fc1_sum.over_h()
    fc1_sum.over_y_first()
    d_hidden.edges()
    branch.over_c()
    branch.corner()
    qkv_grad, out_grad = join_attention(attn_pieces)
    qkv_res = adamw(qkv_weight, qkv_grad, m_qkv, v_qkv)
    out_res = adamw(out_weight, out_grad, m_out, v_out)
    fc2_total = fc2_sum.total()
    (fc2_total,) = close(fc1_sum, d_hidden, branch, fc2_total)
    fc1_pieces, fc2_pieces = collect(fc1_sum.total()), collect(fc2_total)
    d_hidden = d_hidden.total()
    own_rows = inputs.astype(F32)
    centred = own_rows - jnp.mean(own_rows, axis=1, keepdims=True)
    inv_std = lax.rsqrt(jnp.mean(centred * centred, axis=1, keepdims=True) + EPS_NORM)
    normed = centred * inv_std
    sums = jnp.stack([jnp.sum(d_hidden * normed, axis=0), jnp.sum(d_hidden, axis=0)])
    for axis in "cyt":
        sums = sums + swap(sums, axis)
    scaled_grad = d_hidden * vectors[:1].astype(F32)
    input_grad = cotangent.astype(F32) + inv_std * (
        scaled_grad
        - jnp.mean(scaled_grad, axis=1, keepdims=True)
        - normed * jnp.mean(scaled_grad * normed, axis=1, keepdims=True)
    )
    fc1_pieces, fc2_pieces, sums, input_grad = close(fc1_pieces, fc2_pieces, branch, sums, input_grad)
    branch.edges()
    fc1_res = adamw(fc1_weight, join_columns(fc1_pieces), m_fc1, v_fc1)
    fc2_res = adamw(fc2_weight, join_columns(fc2_pieces), m_fc2, v_fc2)
    fc1_res, fc2_res, sums = lax.optimization_barrier((fc1_res, fc2_res, sums))
    (others,) = close(branch, shifted(sums))
    output = (own_rows + branch.total()).astype(BF16)
    sums = own_part(sum(others, sums))
    gain_res = adamw(ln_gain, sums[0], m_gain, v_gain)
    bias_res = adamw(ln_bias, sums[1], m_bias, v_bias)
    return (
        output,
        input_grad,
        *gain_res,
        *bias_res,
        *qkv_res,
        *out_res,
        *fc1_res,
        *fc2_res,
    )


def solution(mesh):
    dp, tensor = mesh.devices.shape
    inner = Mesh(mesh.devices.reshape(dp // 8, 2, 2, 2, tensor), ("h", "w", "y", "c", "t"))
    rows = P(("h", "w", "y", "c", "t"), None)
    vector = P(("h", "w", "y", "c"))
    stack = P(None, ("h", "w", "y", "c"), "t")
    matrix = P(("h", "w", "y", "c"), "t")
    return jax.shard_map(
        shards,
        mesh=inner,
        in_specs=(rows, vector, vector, stack, matrix, matrix, matrix, rows)
        + (vector,) * 4
        + (stack,) * 2
        + (matrix,) * 6,
        out_specs=(rows, rows) + (vector,) * 8 + (stack,) * 4 + (matrix,) * 12,
        check_vma=False,
    )
```

```python
import functools
import math

import jax
import jax.numpy as jnp
import numpy as np
from jax import lax
from jax.experimental import pallas as pl
from jax.experimental.pallas import tpu as pltpu
from jax.sharding import Mesh
from jax.sharding import PartitionSpec as P

HEAD = 64
ROT = 32
PAIR = 2 * HEAD
SCALE = HEAD ** (-0.5)

EPS_NORM = 1e-05
MASK_FILL = -1e30
BETA_ONE = 0.9
BETA_TWO = 0.95
ADAM_EPS = 1e-08
RATE = 0.02
DECAY = 0.1
STEP_COUNT = 10
GELU_ROOT = math.sqrt(2.0 / math.pi)
GELU_CUBE = 0.044715

BF16 = jnp.bfloat16
F32 = jnp.float32


def swap(value, axis):
    return lax.ppermute(value, axis, [(0, 1), (1, 0)])


def ring(value):
    n = lax.axis_size("h")
    return lax.ppermute(value, "h", [(i, (i + 1) % n) for i in range(n)])


def inner_index():
    return 2 * lax.axis_index("w") + lax.axis_index("c")


def dp_index():
    outer = 2 * lax.axis_index("h") + lax.axis_index("w")
    return 4 * outer + 2 * lax.axis_index("y") + lax.axis_index("c")


def feature_table():
    n = lax.axis_size("h")
    h, w, y, c = (lax.axis_index(axis) for axis in "hwyc")
    entries = [lax.axis_index("t")]
    for flip_y in range(2):
        for back in range(n):
            for flip in range(4):
                outer = 2 * lax.rem(h + n - back, n) + (w ^ (flip >> 1))
                entries.append(4 * outer + 2 * (y ^ flip_y) + (c ^ (flip & 1)))
    return jnp.stack(entries).astype(jnp.int32)


def column_block(weight, j):
    width = weight.shape[-1] // 4
    return lax.dynamic_slice_in_dim(weight, j * width, width, weight.ndim - 1)


def attention_block(qkv_weight, out_weight, j):
    qkv = column_block(qkv_weight, j)
    return jnp.concatenate([qkv[0], qkv[1], qkv[2], column_block(out_weight, j)], axis=1)


def cut(piece_of):
    r = inner_index()
    return [piece_of(r), piece_of(r ^ 1), jnp.concatenate([piece_of(r ^ 2), piece_of(r ^ 3)])]


def exchange(blocks):
    own, beside, across = blocks
    rows = own.shape[0]
    across = swap(across, "w")
    both = swap(jnp.concatenate([beside, across[rows:]]), "c")
    return [own, both[:rows], across[:rows], both[rows:]]


def exchange_directly(pieces):
    out = pieces[:1]
    for flip in range(1, 4):
        out.append(lax.ppermute(pieces[flip], ("w", "c"), [(i, i ^ flip) for i in range(4)]))
    return out


def collect(total):
    r = inner_index()
    rows = total.shape[0] // 4
    pieces = exchange([total[:rows], total[rows : 2 * rows], total[2 * rows :]])
    return [(r ^ flip, piece) for flip, piece in enumerate(pieces)]


def join_columns(pieces):
    rows, width = pieces[0][1].shape
    out = jnp.zeros((rows, 4 * width), BF16)
    for j, piece in pieces:
        out = lax.dynamic_update_slice(out, piece, (0, j * width))
    return out.astype(F32)


def join_attention(pieces):
    rows, width = pieces[0][1].shape[0], pieces[0][1].shape[1] // 4
    parts = []
    for i in range(4):
        parts.append(join_columns([(j, piece[:, i * width : (i + 1) * width]) for j, piece in pieces]))
    return jnp.stack(parts[:3]), parts[3]


class Gather:
    def __init__(self, own):
        self.beside = [own]
        self.far = []

    def over_h(self):
        for _ in range(lax.axis_size("h") - 1):
            self.beside.append(ring(self.beside[-1]))

    def over_y_first(self):
        self.far.append(swap(self.beside[0], "y"))

    def over_y_rest(self):
        self.far += [swap(piece, "y") for piece in self.beside[1:]]

    def pieces(self):
        return self.beside + self.far


class Reduce:
    def __init__(self, parts):
        n = len(parts) // 2
        self.own, self.beside, self.own_far, self.far = parts[0], parts[1:n], parts[n], parts[n + 1 :]

    def over_y_rest(self):
        self.beside = [near + swap(far, "y") for near, far in zip(self.beside, self.far)]
        self.far = []

    def over_h(self):
        moving = None
        for near in self.beside:
            moving = ring(near if moving is None else near + moving)
        self.beside = [] if moving is None else [moving]

    def over_y_first(self):
        self.own_far = swap(self.own_far, "y")

    def total(self):
        total = self.own.astype(F32) + self.own_far.astype(F32)
        return sum((near.astype(F32) for near in self.beside), total).astype(BF16)


class GroupSum:
    def __init__(self, parts):
        self.mine, self.other = parts

    def over_c(self):
        self.other = swap(self.other, "c")

    def block(self, sequence, half):
        rows = self.mine.shape[0] // 4
        start = ((2 * sequence + half) * rows, 0)
        size = (rows, self.mine.shape[1])
        return lax.dynamic_slice(self.mine, start, size) + lax.dynamic_slice(self.other, start, size)

    def corner(self):
        t = lax.axis_index("t")
        self.moving = swap(self.block(1, 1 - t), "t")
        self.across, self.beside, own = self.block(1, t), self.block(0, 1 - t), self.block(0, t)
        self.mine, self.other = own, None

    def edges(self):
        self.across = swap(self.across + self.moving, "w")
        self.beside = swap(self.beside, "t")
        self.moving = None

    def total(self):
        return self.mine.astype(F32) + self.across.astype(F32) + self.beside.astype(F32)


def close(*items):
    holders = [vars(item) if isinstance(item, (Gather, Reduce, GroupSum)) else item for item in items]
    held = lax.optimization_barrier(holders)
    out = []
    for item, value in zip(items, held):
        if isinstance(item, (Gather, Reduce, GroupSum)):
            vars(item).update(value)
        else:
            out.append(value)
    return out


def shifted(value):
    n = 2 * lax.axis_size("h")
    return [
        lax.ppermute(value, ("h", "w"), [(i, (i + k) % n) for i in range(n)]) for k in range(1, n)
    ]


def place_vectors(pair):
    out = jnp.zeros((2, 8 * lax.axis_size("h") * pair.shape[1]), pair.dtype)
    return lax.dynamic_update_slice(out, pair, (0, dp_index() * pair.shape[1]))


def relative(vectors, table):
    rows, features = vectors.shape
    blocks = table.shape[0] - 1
    parts = jnp.take(vectors.reshape(rows, blocks, features // blocks), table[1:], axis=1)
    return parts.reshape(rows, features)


def own_part(sums):
    width = sums.shape[1] // (8 * lax.axis_size("h"))
    return lax.dynamic_slice(sums, (0, dp_index() * width), (2, width))


def lane_tables(length):
    position = np.arange(length, dtype=np.float32)[:, None]
    inverse = 10000.0 ** (-(np.arange(ROT // 2, dtype=np.float32) * 2.0 / ROT))
    angles = (position * inverse.astype(np.float32)[None, :]).astype(np.float64)
    cosine = jnp.asarray(np.cos(angles).astype(np.float32))
    sine = jnp.asarray(np.sin(angles).astype(np.float32))
    none = jnp.zeros_like(sine)
    rest = jnp.zeros((length, HEAD - ROT), F32)
    tables = (
        jnp.concatenate([cosine, cosine, rest + 1.0], axis=1),
        jnp.concatenate([sine, none, rest], axis=1),
        jnp.concatenate([none, sine, rest], axis=1),
    )
    return tuple(jnp.concatenate([table, table], axis=1) for table in tables)


def attention_body(proj_ref, grad_ref, cos_ref, low_ref, high_ref, context_ref, d_proj_ref):
    length, width = grad_ref.shape
    half = length // 2
    cosine, low, high = cos_ref[...], low_ref[...], high_ref[...]
    first = lax.broadcasted_iota(jnp.int32, (length, PAIR), 1) < HEAD
    row = lax.broadcasted_iota(jnp.int32, (half, half), 0)
    col = lax.broadcasted_iota(jnp.int32, (half, half), 1)
    keep = row <= col

    def turn(value, sign):
        ahead = pltpu.roll(value, PAIR - ROT // 2, 1)
        behind = pltpu.roll(value, ROT // 2, 1)
        return value * cosine - sign * ahead * low + sign * behind * high

    def rows_by_rows(a, b):
        return lax.dot_general(a, b, (((1,), (1,)), ((), ())), preferred_element_type=F32)

    def turned(a, b):
        return lax.dot_general(a, b, (((0,), (0,)), ((), ())), preferred_element_type=F32)

    def plain(a, b):
        return lax.dot_general(a, b, (((1,), (0,)), ((), ())), preferred_element_type=F32)

    def over_keys(function, value):
        return function(value, axis=0, keepdims=True)

    for pair in range(width // PAIR):
        lanes = pl.ds(pair * PAIR, PAIR)
        key_lanes = pl.ds(width + pair * PAIR, PAIR)
        value_lanes = pl.ds(2 * width + pair * PAIR, PAIR)
        query = (turn(proj_ref[:, lanes], 1.0).astype(BF16).astype(F32) * SCALE).astype(BF16)
        keys = turn(proj_ref[:, key_lanes], 1.0).astype(BF16)
        values = proj_ref[:, value_lanes].astype(BF16)
        grad = grad_ref[:, lanes]
        context = jnp.zeros((length, PAIR), F32)
        d_query = context
        d_keys_a = d_keys_b = d_values_a = d_values_b = jnp.zeros((half, PAIR), F32)
        for head in range(2):
            mine = first if head == 0 else jnp.logical_not(first)
            q, k, v, g = (
                jnp.where(mine, item, jnp.zeros_like(item)) for item in (query, keys, values, grad)
            )
            qa, qb, ga, gb = q[:half], q[half:], g[:half], g[half:]
            s_aa = jnp.where(keep, rows_by_rows(keys[:half], qa), MASK_FILL)
            s_ab = rows_by_rows(keys[:half], qb)
            s_bb = jnp.where(keep, rows_by_rows(keys[half:], qb), MASK_FILL)
            max_a = over_keys(jnp.max, s_aa)
            max_b = jnp.maximum(over_keys(jnp.max, s_ab), over_keys(jnp.max, s_bb))
            e_aa, e_ab, e_bb = jnp.exp(s_aa - max_a), jnp.exp(s_ab - max_b), jnp.exp(s_bb - max_b)
            inv_a = 1.0 / over_keys(jnp.sum, e_aa)
            inv_b = 1.0 / (over_keys(jnp.sum, e_ab) + over_keys(jnp.sum, e_bb))
            p_aa, p_ab, p_bb = e_aa * inv_a, e_ab * inv_b, e_bb * inv_b
            r_aa, r_ab, r_bb = p_aa.astype(BF16), p_ab.astype(BF16), p_bb.astype(BF16)
            d_aa = rows_by_rows(values[:half], ga)
            d_ab = rows_by_rows(values[:half], gb)
            d_bb = rows_by_rows(values[half:], gb)
            centre_a = over_keys(jnp.sum, d_aa * p_aa)
            centre_b = over_keys(jnp.sum, d_ab * p_ab) + over_keys(jnp.sum, d_bb * p_bb)
            t_aa = (p_aa * (d_aa - centre_a)).astype(BF16)
            t_ab = (p_ab * (d_ab - centre_b)).astype(BF16)
            t_bb = (p_bb * (d_bb - centre_b)).astype(BF16)
            context += jnp.concatenate(
                [turned(r_aa, v[:half]), turned(r_ab, v[:half]) + turned(r_bb, v[half:])]
            )
            d_query += jnp.concatenate(
                [turned(t_aa, k[:half]), turned(t_ab, k[:half]) + turned(t_bb, k[half:])]
            )
            d_keys_a += plain(t_aa, qa) + plain(t_ab, qb)
            d_keys_b += plain(t_bb, qb)
            d_values_a += plain(r_aa, ga) + plain(r_ab, gb)
            d_values_b += plain(r_bb, gb)
        context_ref[:, lanes] = context.astype(BF16)
        d_proj_ref[:, lanes] = turn(d_query * SCALE, -1.0).astype(BF16)
        d_keys = jnp.concatenate([d_keys_a, d_keys_b])
        d_proj_ref[:, key_lanes] = turn(d_keys, -1.0).astype(BF16)
        d_proj_ref[:, value_lanes] = jnp.concatenate([d_values_a, d_values_b]).astype(BF16)


def dot_nn(a, b):
    return lax.dot_general(a, b, (((1,), (0,)), ((), ())), preferred_element_type=F32)


def dot_nt(a, b):
    return lax.dot_general(a, b, (((1,), (1,)), ((), ())), preferred_element_type=F32)


def dot_tn(a, b):
    return lax.dot_general(a, b, (((0,), (0,)), ((), ())), preferred_element_type=F32)


def rows_of(block, width):
    return pl.BlockSpec((block, width), lambda s: (s, 0))


def whole(shape):
    return pl.BlockSpec(shape, lambda s: (0, 0), pipeline_mode=pl.Buffered(1))


ANYWHERE = pl.BlockSpec(memory_space=pl.ANY)
PARAMS = pltpu.CompilerParams(vmem_limit_bytes=58 << 20)


def fetches(piece_refs, into_ref, sem_ref, start=0, to=0, width=None):
    width = into_ref.shape[1] if width is None else width
    copies = []
    for i, piece in enumerate(piece_refs):
        rows = piece.shape[0]
        copies.append(
            pltpu.make_async_copy(
                piece.at[:, pl.ds(start, width)],
                into_ref.at[pl.ds(i * rows, rows), pl.ds(to, width)],
                sem_ref.at[i],
            )
        )
    return copies


def at_first(*copies, start=True, wait=True):
    @pl.when(pl.program_id(0) == 0)
    def _():
        if start:
            for copy in copies:
                copy.start()
        if wait:
            for copy in copies:
                copy.wait()


def add_and_flush(total_ref, part_refs, addends):
    step = pl.program_id(0)

    @pl.when(step == 0)
    def _():
        total_ref[...] = jnp.zeros_like(total_ref)

    for lanes, addend in addends:
        total_ref[:, lanes] += addend()

    @pl.when(step == pl.num_programs(0) - 1)
    def _():
        rows = part_refs[0].shape[0]
        for i, part_ref in enumerate(part_refs):
            part_ref[...] = total_ref[i * rows : (i + 1) * rows, :].astype(BF16)


def attention_step(table_ref, gain_ref, bias_ref, cos_ref, low_ref, high_ref, *refs, permute):
    x_pieces, g_pieces, pieces, refs = refs[:8], refs[8:16], refs[16:-12], refs[-12:]
    context_ref, d_proj_ref, hidden_ref, cotan_ref, cols_ref, proj_ref, grad_ref = refs[:7]
    x_buffer, g_buffer, x_sems, g_sems, sems = refs[7:]
    step = pl.program_id(0)
    length, features = hidden_ref.shape
    half = length // 2
    blocks = table_ref.shape[0] - 1 if permute else 1
    size = features // blocks

    def start(sequence):
        slot = sequence % 2
        for i in range(2):
            side = table_ref[0] if i == 0 else 1 - table_ref[0]
            rows = pl.ds(pl.multiple_of(side * half, half), half)

            def block(j, carry, i=i, rows=rows):
                entry = table_ref[1 + j] if permute else 0
                of = pl.ds(pl.multiple_of(entry * size, size), size)
                to = pl.ds(pl.multiple_of(j * size, size), size)
                for sources, buffer, buffer_sems in (
                    (x_pieces, x_buffer, x_sems),
                    (g_pieces, g_buffer, g_sems),
                ):
                    pltpu.make_async_copy(
                        sources[2 * sequence + i].at[:, of],
                        buffer.at[slot, rows, to],
                        buffer_sems.at[slot],
                    ).start()
                return carry

            lax.fori_loop(0, blocks, block, 0)

    pl.when(step == 0)(lambda: start(0))
    for sequence in range(1, 4):
        pl.when(step == sequence - 1)(lambda sequence=sequence: start(sequence))
    columns = fetches(pieces, cols_ref, sems)
    at_first(*columns, wait=False)
    slot = lax.rem(step, 2)
    for buffer, buffer_sems in ((x_buffer, x_sems), (g_buffer, g_sems)):
        pltpu.make_async_copy(buffer.at[slot], buffer.at[slot], buffer_sems.at[slot]).wait()
    chunk = min(128, length)

    def normalize(i, carry):
        at = pl.ds(pl.multiple_of(i * chunk, chunk), chunk)
        rows = x_buffer[slot, at, :].astype(F32)
        centred = rows - jnp.mean(rows, axis=1, keepdims=True)
        inv_std = lax.rsqrt(jnp.mean(centred * centred, axis=1, keepdims=True) + EPS_NORM)
        hidden_ref[at, :] = (centred * inv_std * gain_ref[...] + bias_ref[...]).astype(BF16)
        return carry

    lax.fori_loop(0, length // chunk, normalize, 0)
    cotan_ref[...] = g_buffer[slot]
    at_first(*columns, start=False)
    width = grad_ref.shape[1]
    proj_ref[...] = dot_nn(hidden_ref[...], cols_ref[:, : 3 * width])
    grad_ref[...] = dot_nn(cotan_ref[...], cols_ref[:, 3 * width :]).astype(BF16)
    attention_body(proj_ref, grad_ref, cos_ref, low_ref, high_ref, context_ref, d_proj_ref)


def attention(table, x_pieces, g_pieces, gain, bias, pieces):
    half, features = x_pieces[0].shape
    length, tokens = 2 * half, 8 * half
    width = pieces[0].shape[1] // 4
    permute = features // (table.shape[0] - 1) % 128 == 0
    if not permute:
        x_pieces = [relative(piece, table) for piece in x_pieces]
        g_pieces = [relative(piece, table) for piece in g_pieces]

    def rows(columns):
        return pl.BlockSpec((length, columns), lambda s, h: (s, 0))

    def fixed(shape):
        return pl.BlockSpec(shape, lambda s, h: (0, 0), pipeline_mode=pl.Buffered(1))

    widths = (width, 3 * width, features, features)
    return pl.pallas_call(
        functools.partial(attention_step, permute=permute),
        grid_spec=pltpu.PrefetchScalarGridSpec(
            num_scalar_prefetch=1,
            grid=(4,),
            in_specs=[fixed((1, features))] * 2
            + [fixed((length, PAIR))] * 3
            + [ANYWHERE] * (16 + len(pieces)),
            out_specs=[rows(columns) for columns in widths],
            scratch_shapes=[
                pltpu.VMEM((features, 4 * width), BF16),
                pltpu.VMEM((length, 3 * width), F32),
                pltpu.VMEM((length, width), BF16),
                pltpu.VMEM((2, length, features), BF16),
                pltpu.VMEM((2, length, features), BF16),
                pltpu.SemaphoreType.DMA((2,)),
                pltpu.SemaphoreType.DMA((2,)),
                pltpu.SemaphoreType.DMA((len(pieces),)),
            ],
        ),
        out_shape=[jax.ShapeDtypeStruct((tokens, columns), BF16) for columns in widths],
        compiler_params=PARAMS,
        name="attention",
    )(table, gain, bias, *lane_tables(length), *x_pieces, *g_pieces, *pieces)


def parts_of(count, features, width):
    rows = features // count
    shapes = [jax.ShapeDtypeStruct((rows, width), BF16)] * count
    return [whole((rows, width))] * count, shapes, [pltpu.VMEM((features, width), F32)]


def attention_grads_step(hidden_ref, cotan_ref, d_proj_ref, context_ref, *refs):
    wide = d_proj_ref.shape[1]
    add_and_flush(
        refs[-1],
        refs[:-1],
        [
            (pl.ds(0, wide), lambda: dot_tn(hidden_ref[...], d_proj_ref[...])),
            (pl.ds(wide, wide // 3), lambda: dot_tn(cotan_ref[...], context_ref[...])),
        ],
    )


def attention_grads(hidden, cotan, d_proj, context, block, count):
    tokens, features = hidden.shape
    width = context.shape[1]
    specs, shapes, scratch = parts_of(count, features, 4 * width)
    return pl.pallas_call(
        attention_grads_step,
        grid=(tokens // block,),
        in_specs=[rows_of(block, features)] * 2 + [rows_of(block, 3 * width), rows_of(block, width)],
        out_specs=specs,
        out_shape=shapes,
        scratch_shapes=scratch,
        compiler_params=PARAMS,
        name="attention_grads",
    )(hidden, cotan, d_proj, context)


def fc1_step(hidden_ref, cotan_ref, *refs, count):
    pieces, (act_ref, slope_ref), parts = refs[:count], refs[count : count + 2], refs[count + 2 : -3]
    cols_ref, total_ref, sems = refs[-3:]
    at_first(*fetches(pieces, cols_ref, sems))
    pre = dot_nn(hidden_ref[...], cols_ref[...])
    square = pre * pre
    tanh = jnp.tanh(pre * (GELU_ROOT + GELU_ROOT * GELU_CUBE * square))
    half = 0.5 + 0.5 * tanh
    steep = pre * (GELU_ROOT + 3.0 * GELU_ROOT * GELU_CUBE * square)
    act_ref[...] = (pre * half).astype(BF16)
    slope_ref[...] = half + half * (steep * (1.0 - tanh))
    every = pl.ds(0, total_ref.shape[1])
    add_and_flush(total_ref, parts, [(every, lambda: dot_tn(cotan_ref[...], act_ref[...]))])


def fc1_pass(hidden, cotan, pieces, block):
    tokens, features = hidden.shape
    count, width = len(pieces), pieces[0].shape[1]
    specs, shapes, scratch = parts_of(count, features, width)
    act, slope, *parts = pl.pallas_call(
        functools.partial(fc1_step, count=count),
        grid=(tokens // block,),
        in_specs=[rows_of(block, features)] * 2 + [ANYWHERE] * count,
        out_specs=[rows_of(block, width)] * 2 + specs,
        out_shape=[
            jax.ShapeDtypeStruct((tokens, width), BF16),
            jax.ShapeDtypeStruct((tokens, width), F32),
            *shapes,
        ],
        scratch_shapes=[
            pltpu.VMEM((features, width), BF16),
            *scratch,
            pltpu.SemaphoreType.DMA((count,)),
        ],
        compiler_params=PARAMS,
        name="fc1_pass",
    )(hidden, cotan, *pieces)
    return act, slope, parts


def fc2_step(hidden_ref, cotan_ref, slope_ref, *refs, count):
    pieces, d_pre_ref, parts = refs[:count], refs[count], refs[count + 1 : -3]
    cols_ref, total_ref, sems = refs[-3:]
    at_first(*fetches(pieces, cols_ref, sems))
    d_pre_ref[...] = (dot_nn(cotan_ref[...], cols_ref[...]) * slope_ref[...]).astype(BF16)
    every = pl.ds(0, total_ref.shape[1])
    add_and_flush(total_ref, parts, [(every, lambda: dot_tn(hidden_ref[...], d_pre_ref[...]))])


def fc2_pass(hidden, cotan, pieces, slope, block):
    tokens, features = hidden.shape
    count, width = len(pieces), pieces[0].shape[1]
    specs, shapes, scratch = parts_of(count, features, width)
    d_pre, *parts = pl.pallas_call(
        functools.partial(fc2_step, count=count),
        grid=(tokens // block,),
        in_specs=[rows_of(block, features)] * 2 + [rows_of(block, width)] + [ANYWHERE] * count,
        out_specs=[rows_of(block, width)] + specs,
        out_shape=[jax.ShapeDtypeStruct((tokens, width), BF16), *shapes],
        scratch_shapes=[
            pltpu.VMEM((features, width), BF16),
            *scratch,
            pltpu.SemaphoreType.DMA((count,)),
        ],
        compiler_params=PARAMS,
        name="fc2_pass",
    )(hidden, cotan, slope, *pieces)
    return d_pre, parts


def back_step(table_ref, first_ref, second_ref, *refs, count, start, permute):
    attn_pieces, fc_pieces, (mine_ref, other_ref) = refs[:count], refs[count:-6], refs[-6:-4]
    rows_ref, cols_ref, attn_sems, fc_sems = refs[-4:]
    size, width = first_ref.shape[1], second_ref.shape[1]
    at_first(
        *fetches(attn_pieces, cols_ref, attn_sems, start, 0, size),
        *fetches(fc_pieces, cols_ref, fc_sems, 0, size, width),
    )
    rows_ref[:, :size] = first_ref[...]
    rows_ref[:, size:] = second_ref[...]
    out = dot_nt(rows_ref[...], cols_ref[...])
    out = out.astype(BF16)
    middle = pl.num_programs(0) // 2
    blocks = table_ref.shape[0] - 1
    size = out.shape[1] // blocks

    def store(out_ref):
        if not permute:
            out_ref[...] = out
            return
        for j in range(blocks):
            lanes = pl.ds(pl.multiple_of(table_ref[1 + j] * size, size), size)
            out_ref[:, lanes] = out[:, j * size : (j + 1) * size]

    pl.when(pl.program_id(0) < middle)(lambda: store(mine_ref))
    pl.when(pl.program_id(0) >= middle)(lambda: store(other_ref))


def back_product(table, first, second, attn_pieces, fc_pieces, start, block):
    (tokens, size), width = first.shape, second.shape[1]
    count = len(attn_pieces)
    features = count * attn_pieces[0].shape[0]
    blocks = table.shape[0] - 1
    permute = features // blocks % 128 == 0
    middle = tokens // block // 2
    outs = pl.pallas_call(
        functools.partial(back_step, count=count, start=start, permute=permute),
        grid_spec=pltpu.PrefetchScalarGridSpec(
            num_scalar_prefetch=1,
            grid=(tokens // block,),
            in_specs=[
                pl.BlockSpec((block, size), lambda s, h: (s, 0)),
                pl.BlockSpec((block, width), lambda s, h: (s, 0)),
            ]
            + [ANYWHERE] * (2 * count),
            out_specs=(
                pl.BlockSpec((block, features), lambda s, h: (jnp.minimum(s, middle - 1), 0)),
                pl.BlockSpec((block, features), lambda s, h: (jnp.maximum(s - middle, 0), 0)),
            ),
            scratch_shapes=[
                pltpu.VMEM((block, size + width), BF16),
                pltpu.VMEM((features, size + width), BF16),
                pltpu.SemaphoreType.DMA((count,)),
                pltpu.SemaphoreType.DMA((count,)),
            ],
        ),
        out_shape=(jax.ShapeDtypeStruct((tokens // 2, features), BF16),) * 2,
        compiler_params=PARAMS,
        name="back_product",
    )(table, first, second, *attn_pieces, *fc_pieces)
    if not permute:
        order = jnp.argsort(table[1:])
        cut = [out.reshape(tokens // 2, blocks, features // blocks) for out in outs]
        outs = [jnp.take(out, order, axis=1).reshape(tokens // 2, features) for out in cut]
    return outs


def adamw(weight, gradient, moment, second):
    new_m = BETA_ONE * moment + (1.0 - BETA_ONE) * gradient
    new_v = BETA_TWO * second + (1.0 - BETA_TWO) * gradient * gradient
    m_hat = new_m / (1.0 - BETA_ONE**STEP_COUNT)
    v_hat = new_v / (1.0 - BETA_TWO**STEP_COUNT)
    update = -RATE * (m_hat / (jnp.sqrt(v_hat) + ADAM_EPS) + DECAY * weight.astype(F32))
    return (gradient, update, new_m, new_v)


def shards(
    inputs,
    ln_gain,
    ln_bias,
    qkv_weight,
    out_weight,
    fc1_weight,
    fc2_weight,
    cotangent,
    m_gain,
    v_gain,
    m_bias,
    v_bias,
    m_qkv,
    v_qkv,
    m_out,
    v_out,
    m_fc1,
    v_fc1,
    m_fc2,
    v_fc2,
):
    length = 2 * inputs.shape[0]
    block = length // 2
    count = 2 * lax.axis_size("h")
    table = feature_table()

    r = inner_index()
    vectors = place_vectors(jnp.stack([ln_gain, ln_bias]))
    for axis in "yc":
        vectors = vectors + swap(vectors, axis)
    first = [
        jnp.concatenate(
            [attention_block(qkv_weight, out_weight, r ^ flip), column_block(fc1_weight, r ^ flip)],
            axis=1,
        )
        for flip in range(4)
    ]
    first = exchange_directly(first)
    fc2_cut = cut(functools.partial(column_block, fc2_weight))
    x, g = [inputs, swap(inputs, "t"), swap(inputs, "w")], [cotangent]
    x[2], vectors = lax.optimization_barrier((x[2], vectors))
    others = shifted(vectors)
    early = [swap(inputs, "c"), swap(cotangent, "c")]
    first, x, g, fc2_cut, vectors, others, early = close(
        first, x, g, fc2_cut, vectors, others, early
    )
    split = 4 * (qkv_weight.shape[2] // 4)
    attn = Gather(jnp.concatenate([piece[:, :split] for piece in first]))
    attn.over_h()
    attn.over_y_first()
    vectors = sum(others, vectors)
    x.append(swap(x[2], "t"))
    g += [swap(g[0], "t"), swap(g[0], "w")]
    fc1 = Gather(jnp.concatenate([piece[:, split:] for piece in first]))
    x, g, fc2_cut, vectors = close(attn, x, g, fc2_cut, fc1, vectors)
    fc2 = Gather(jnp.concatenate(exchange(fc2_cut)))
    fc1.over_h()
    attn.over_y_rest()
    fc1.over_y_first()
    g.append(swap(g[2], "t"))
    late = [swap(piece, "c") for piece in (*x[1:], *g[1:])]
    g, x, late, vectors = close(fc1, attn, g, fc2, x, late, vectors)
    x_other, g_other = [early[0], *late[:3]], [early[1], *late[3:]]
    fc2.over_h()
    fc2.over_y_first()
    fc1.over_y_rest()
    affine = relative(vectors, table).astype(F32)
    context, d_proj, hidden, cotan = attention(
        table, x + x_other, g + g_other, affine[:1], affine[1:], attn.pieces()
    )
    attn_parts = attention_grads(hidden, cotan, d_proj, context, block, count)
    hidden, cotan, context, d_proj, attn_parts = close(
        attn, fc1, fc2, hidden, cotan, context, d_proj, attn_parts
    )
    fc2.over_y_rest()
    attn_sum = Reduce(attn_parts)
    attn_sum.over_y_rest()
    act, slope, fc2_parts = fc1_pass(hidden, cotan, fc1.pieces(), block)
    hidden, cotan, context, d_proj, act, slope, fc2_parts = close(attn, fc1, fc2, attn_sum, hidden, cotan, context, d_proj, act, slope, fc2_parts)
    attn_sum.over_h()
    attn_sum.over_y_first()
    fc2_sum = Reduce(fc2_parts)
    fc2_sum.over_y_rest()
    start = d_proj.shape[1]
    d_pre, fc1_parts = fc2_pass(hidden, cotan, fc2.pieces(), slope, block)
    d_hidden = GroupSum(back_product(table, d_proj, d_pre, attn.pieces(), fc1.pieces(), 0, block))
    context, act, fc1_parts = close(attn, fc2, attn_sum, fc2_sum, d_hidden, context, act, fc1_parts)
    fc2_sum.over_h()
    fc2_sum.over_y_first()
    fc1_sum = Reduce(fc1_parts)
    fc1_sum.over_y_rest()
    d_hidden.over_c()
    d_hidden.corner()
    branch = GroupSum(back_product(table, context, act, attn.pieces(), fc2.pieces(), start, block))
    attn_pieces = collect(attn_sum.total())
    (attn_pieces,) = close(attn_pieces, fc1_sum, fc2_sum, d_hidden, branch)
    fc1_sum.over_h()
    fc1_sum.over_y_first()
    d_hidden.edges()
    branch.over_c()
    branch.corner()
    qkv_grad, out_grad = join_attention(attn_pieces)
    qkv_res = adamw(qkv_weight, qkv_grad, m_qkv, v_qkv)
    out_res = adamw(out_weight, out_grad, m_out, v_out)
    fc2_total = fc2_sum.total()
    (fc2_total,) = close(fc1_sum, d_hidden, branch, fc2_total)
    d_hidden = d_hidden.total()
    own_rows = inputs.astype(F32)
    centred = own_rows - jnp.mean(own_rows, axis=1, keepdims=True)
    inv_std = lax.rsqrt(jnp.mean(centred * centred, axis=1, keepdims=True) + EPS_NORM)
    normed = centred * inv_std
    sums = jnp.stack([jnp.sum(d_hidden * normed, axis=0), jnp.sum(d_hidden, axis=0)])
    scaled_grad = d_hidden * vectors[:1].astype(F32)
    input_grad = cotangent.astype(F32) + inv_std * (
        scaled_grad
        - jnp.mean(scaled_grad, axis=1, keepdims=True)
        - normed * jnp.mean(scaled_grad * normed, axis=1, keepdims=True)
    )
    fc1_pieces, fc2_pieces = collect(fc1_sum.total()), collect(fc2_total)
    for axis in "cyt":
        sums = sums + swap(sums, axis)
    sums, branch.across, branch.beside, input_grad = lax.optimization_barrier(
        (sums, branch.across, branch.beside, input_grad)
    )
    branch.edges()
    fc1_res = adamw(fc1_weight, join_columns(fc1_pieces), m_fc1, v_fc1)
    fc2_res = adamw(fc2_weight, join_columns(fc2_pieces), m_fc2, v_fc2)
    fc1_res, sums = lax.optimization_barrier((fc1_res, sums))
    others = shifted(sums)
    fc1_res, fc2_res, others, input_grad = close(
        fc1_res, fc2_res, branch, others, input_grad
    )
    output = (own_rows + branch.total()).astype(BF16)
    sums = own_part(sum(others, sums))
    gain_res = adamw(ln_gain, sums[0], m_gain, v_gain)
    bias_res = adamw(ln_bias, sums[1], m_bias, v_bias)
    return (
        output,
        input_grad,
        *gain_res,
        *bias_res,
        *qkv_res,
        *out_res,
        *fc1_res,
        *fc2_res,
    )


def solution(mesh):
    dp, tensor = mesh.devices.shape
    inner = Mesh(mesh.devices.reshape(dp // 8, 2, 2, 2, tensor), ("h", "w", "y", "c", "t"))
    rows = P(("h", "w", "y", "c", "t"), None)
    vector = P(("h", "w", "y", "c"))
    stack = P(None, ("h", "w", "y", "c"), "t")
    matrix = P(("h", "w", "y", "c"), "t")
    return jax.shard_map(
        shards,
        mesh=inner,
        in_specs=(rows, vector, vector, stack, matrix, matrix, matrix, rows)
        + (vector,) * 4
        + (stack,) * 2
        + (matrix,) * 6,
        out_specs=(rows, rows) + (vector,) * 8 + (stack,) * 4 + (matrix,) * 12,
        check_vma=False,
    )
```

```python
import functools
import math

import jax
import jax.numpy as jnp
import numpy as np
from jax import lax
from jax.experimental import pallas as pl
from jax.experimental.pallas import tpu as pltpu
from jax.sharding import Mesh
from jax.sharding import PartitionSpec as P

HEAD = 64
ROT = 32
PAIR = 2 * HEAD
SCALE = HEAD ** (-0.5)

EPS_NORM = 1e-05
MASK_FILL = -1e30
BETA_ONE = 0.9
BETA_TWO = 0.95
ADAM_EPS = 1e-08
RATE = 0.02
DECAY = 0.1
STEP_COUNT = 10
GELU_ROOT = math.sqrt(2.0 / math.pi)
GELU_CUBE = 0.044715

BF16 = jnp.bfloat16
F32 = jnp.float32


def swap(value, axis):
    return lax.ppermute(value, axis, [(0, 1), (1, 0)])


def ring(value):
    n = lax.axis_size("h")
    return lax.ppermute(value, "h", [(i, (i + 1) % n) for i in range(n)])


def inner_index():
    return 2 * lax.axis_index("w") + lax.axis_index("c")


def dp_index():
    outer = 2 * lax.axis_index("h") + lax.axis_index("w")
    return 4 * outer + 2 * lax.axis_index("y") + lax.axis_index("c")


def feature_table():
    n = lax.axis_size("h")
    h, w, y, c = (lax.axis_index(axis) for axis in "hwyc")
    entries = [lax.axis_index("t")]
    for flip_y in range(2):
        for back in range(n):
            for flip in range(4):
                outer = 2 * lax.rem(h + n - back, n) + (w ^ (flip >> 1))
                entries.append(4 * outer + 2 * (y ^ flip_y) + (c ^ (flip & 1)))
    return jnp.stack(entries).astype(jnp.int32)


def column_block(weight, j):
    width = weight.shape[-1] // 4
    return lax.dynamic_slice_in_dim(weight, j * width, width, weight.ndim - 1)


def attention_block(qkv_weight, out_weight, j):
    qkv = column_block(qkv_weight, j)
    return jnp.concatenate([qkv[0], qkv[1], qkv[2], column_block(out_weight, j)], axis=1)


def cut(piece_of):
    r = inner_index()
    return [piece_of(r), piece_of(r ^ 1), jnp.concatenate([piece_of(r ^ 2), piece_of(r ^ 3)])]


def exchange(blocks):
    own, beside, across = blocks
    rows = own.shape[0]
    across = swap(across, "w")
    both = swap(jnp.concatenate([beside, across[rows:]]), "c")
    return [own, both[:rows], across[:rows], both[rows:]]


def exchange_directly(pieces):
    out = pieces[:1]
    for flip in range(1, 4):
        out.append(lax.ppermute(pieces[flip], ("w", "c"), [(i, i ^ flip) for i in range(4)]))
    return out


def collect(total):
    r = inner_index()
    rows = total.shape[0] // 4
    pieces = exchange([total[:rows], total[rows : 2 * rows], total[2 * rows :]])
    return [(r ^ flip, piece) for flip, piece in enumerate(pieces)]


def join_columns(pieces):
    rows, width = pieces[0][1].shape
    out = jnp.zeros((rows, 4 * width), BF16)
    for j, piece in pieces:
        out = lax.dynamic_update_slice(out, piece, (0, j * width))
    return out.astype(F32)


def join_attention(pieces):
    rows, width = pieces[0][1].shape[0], pieces[0][1].shape[1] // 4
    parts = []
    for i in range(4):
        parts.append(join_columns([(j, piece[:, i * width : (i + 1) * width]) for j, piece in pieces]))
    return jnp.stack(parts[:3]), parts[3]


class Gather:
    def __init__(self, own):
        self.beside = [own]
        self.far = []

    def over_h(self):
        for _ in range(lax.axis_size("h") - 1):
            self.beside.append(ring(self.beside[-1]))

    def over_y_first(self):
        self.far.append(swap(self.beside[0], "y"))

    def over_y_rest(self):
        self.far += [swap(piece, "y") for piece in self.beside[1:]]

    def pieces(self):
        return self.beside + self.far


class Reduce:
    def __init__(self, parts):
        n = len(parts) // 2
        self.own, self.beside, self.own_far, self.far = parts[0], parts[1:n], parts[n], parts[n + 1 :]

    def over_y_rest(self):
        self.beside = [near + swap(far, "y") for near, far in zip(self.beside, self.far)]
        self.far = []

    def over_h(self):
        moving = None
        for near in self.beside:
            moving = ring(near if moving is None else near + moving)
        self.beside = [] if moving is None else [moving]

    def over_y_first(self):
        self.own_far = swap(self.own_far, "y")

    def total(self):
        total = self.own.astype(F32) + self.own_far.astype(F32)
        return sum((near.astype(F32) for near in self.beside), total).astype(BF16)


class GroupSum:
    def __init__(self, parts):
        self.mine, self.other = parts

    def over_c(self):
        self.other = swap(self.other, "c")

    def block(self, sequence, half):
        rows = self.mine.shape[0] // 4
        start = ((2 * sequence + half) * rows, 0)
        size = (rows, self.mine.shape[1])
        return lax.dynamic_slice(self.mine, start, size) + lax.dynamic_slice(self.other, start, size)

    def corner(self):
        t = lax.axis_index("t")
        self.moving = swap(self.block(1, 1 - t), "t")
        self.across, self.beside, own = self.block(1, t), self.block(0, 1 - t), self.block(0, t)
        self.mine, self.other = own, None

    def edges(self):
        self.across = swap(self.across + self.moving, "w")
        self.beside = swap(self.beside, "t")
        self.moving = None

    def total(self):
        return self.mine.astype(F32) + self.across.astype(F32) + self.beside.astype(F32)


def close(*items):
    holders = [vars(item) if isinstance(item, (Gather, Reduce, GroupSum)) else item for item in items]
    held = lax.optimization_barrier(holders)
    out = []
    for item, value in zip(items, held):
        if isinstance(item, (Gather, Reduce, GroupSum)):
            vars(item).update(value)
        else:
            out.append(value)
    return out


def shifted(value):
    n = 2 * lax.axis_size("h")
    return [
        lax.ppermute(value, ("h", "w"), [(i, (i + k) % n) for i in range(n)]) for k in range(1, n)
    ]


def place_vectors(pair):
    out = jnp.zeros((2, 8 * lax.axis_size("h") * pair.shape[1]), pair.dtype)
    return lax.dynamic_update_slice(out, pair, (0, dp_index() * pair.shape[1]))


def relative(vectors, table):
    rows, features = vectors.shape
    blocks = table.shape[0] - 1
    parts = jnp.take(vectors.reshape(rows, blocks, features // blocks), table[1:], axis=1)
    return parts.reshape(rows, features)


def own_part(sums):
    width = sums.shape[1] // (8 * lax.axis_size("h"))
    return lax.dynamic_slice(sums, (0, dp_index() * width), (2, width))


def lane_tables(length):
    position = np.arange(length, dtype=np.float32)[:, None]
    inverse = 10000.0 ** (-(np.arange(ROT // 2, dtype=np.float32) * 2.0 / ROT))
    angles = (position * inverse.astype(np.float32)[None, :]).astype(np.float64)
    cosine = jnp.asarray(np.cos(angles).astype(np.float32))
    sine = jnp.asarray(np.sin(angles).astype(np.float32))
    none = jnp.zeros_like(sine)
    rest = jnp.zeros((length, HEAD - ROT), F32)
    tables = (
        jnp.concatenate([cosine, cosine, rest + 1.0], axis=1),
        jnp.concatenate([sine, none, rest], axis=1),
        jnp.concatenate([none, sine, rest], axis=1),
    )
    return tuple(jnp.concatenate([table, table], axis=1) for table in tables)


def attention_body(proj_ref, grad_ref, cos_ref, low_ref, high_ref, context_ref, d_proj_ref):
    length, width = grad_ref.shape
    half = length // 2
    cosine, low, high = cos_ref[...], low_ref[...], high_ref[...]
    first = lax.broadcasted_iota(jnp.int32, (length, PAIR), 1) < HEAD
    row = lax.broadcasted_iota(jnp.int32, (half, half), 0)
    col = lax.broadcasted_iota(jnp.int32, (half, half), 1)
    keep = row <= col

    def turn(value, sign):
        ahead = pltpu.roll(value, PAIR - ROT // 2, 1)
        behind = pltpu.roll(value, ROT // 2, 1)
        return value * cosine - sign * ahead * low + sign * behind * high

    def rows_by_rows(a, b):
        return lax.dot_general(a, b, (((1,), (1,)), ((), ())), preferred_element_type=F32)

    def turned(a, b):
        return lax.dot_general(a, b, (((0,), (0,)), ((), ())), preferred_element_type=F32)

    def plain(a, b):
        return lax.dot_general(a, b, (((1,), (0,)), ((), ())), preferred_element_type=F32)

    def over_keys(function, value):
        return function(value, axis=0, keepdims=True)

    for pair in range(width // PAIR):
        lanes = pl.ds(pair * PAIR, PAIR)
        key_lanes = pl.ds(width + pair * PAIR, PAIR)
        value_lanes = pl.ds(2 * width + pair * PAIR, PAIR)
        query = (turn(proj_ref[:, lanes], 1.0).astype(BF16).astype(F32) * SCALE).astype(BF16)
        keys = turn(proj_ref[:, key_lanes], 1.0).astype(BF16)
        values = proj_ref[:, value_lanes].astype(BF16)
        grad = grad_ref[:, lanes]
        context = jnp.zeros((length, PAIR), F32)
        d_query = context
        d_keys_a = d_keys_b = d_values_a = d_values_b = jnp.zeros((half, PAIR), F32)
        for head in range(2):
            mine = first if head == 0 else jnp.logical_not(first)
            q, k, v, g = (
                jnp.where(mine, item, jnp.zeros_like(item)) for item in (query, keys, values, grad)
            )
            qa, qb, ga, gb = q[:half], q[half:], g[:half], g[half:]
            s_aa = jnp.where(keep, rows_by_rows(keys[:half], qa), MASK_FILL)
            s_ab = rows_by_rows(keys[:half], qb)
            s_bb = jnp.where(keep, rows_by_rows(keys[half:], qb), MASK_FILL)
            max_a = over_keys(jnp.max, s_aa)
            max_b = jnp.maximum(over_keys(jnp.max, s_ab), over_keys(jnp.max, s_bb))
            e_aa, e_ab, e_bb = jnp.exp(s_aa - max_a), jnp.exp(s_ab - max_b), jnp.exp(s_bb - max_b)
            inv_a = 1.0 / over_keys(jnp.sum, e_aa)
            inv_b = 1.0 / (over_keys(jnp.sum, e_ab) + over_keys(jnp.sum, e_bb))
            p_aa, p_ab, p_bb = e_aa * inv_a, e_ab * inv_b, e_bb * inv_b
            r_aa, r_ab, r_bb = p_aa.astype(BF16), p_ab.astype(BF16), p_bb.astype(BF16)
            d_aa = rows_by_rows(values[:half], ga)
            d_ab = rows_by_rows(values[:half], gb)
            d_bb = rows_by_rows(values[half:], gb)
            centre_a = over_keys(jnp.sum, d_aa * p_aa)
            centre_b = over_keys(jnp.sum, d_ab * p_ab) + over_keys(jnp.sum, d_bb * p_bb)
            t_aa = (p_aa * (d_aa - centre_a)).astype(BF16)
            t_ab = (p_ab * (d_ab - centre_b)).astype(BF16)
            t_bb = (p_bb * (d_bb - centre_b)).astype(BF16)
            context += jnp.concatenate(
                [turned(r_aa, v[:half]), turned(r_ab, v[:half]) + turned(r_bb, v[half:])]
            )
            d_query += jnp.concatenate(
                [turned(t_aa, k[:half]), turned(t_ab, k[:half]) + turned(t_bb, k[half:])]
            )
            d_keys_a += plain(t_aa, qa) + plain(t_ab, qb)
            d_keys_b += plain(t_bb, qb)
            d_values_a += plain(r_aa, ga) + plain(r_ab, gb)
            d_values_b += plain(r_bb, gb)
        context_ref[:, lanes] = context.astype(BF16)
        d_proj_ref[:, lanes] = turn(d_query * SCALE, -1.0).astype(BF16)
        d_keys = jnp.concatenate([d_keys_a, d_keys_b])
        d_proj_ref[:, key_lanes] = turn(d_keys, -1.0).astype(BF16)
        d_proj_ref[:, value_lanes] = jnp.concatenate([d_values_a, d_values_b]).astype(BF16)


def dot_nn(a, b):
    return lax.dot_general(a, b, (((1,), (0,)), ((), ())), preferred_element_type=F32)


def dot_nt(a, b):
    return lax.dot_general(a, b, (((1,), (1,)), ((), ())), preferred_element_type=F32)


def dot_tn(a, b):
    return lax.dot_general(a, b, (((0,), (0,)), ((), ())), preferred_element_type=F32)


def rows_of(block, width):
    return pl.BlockSpec((block, width), lambda s: (s, 0))


def whole(shape):
    return pl.BlockSpec(shape, lambda s: (0, 0), pipeline_mode=pl.Buffered(1))


ANYWHERE = pl.BlockSpec(memory_space=pl.ANY)
PARAMS = pltpu.CompilerParams(vmem_limit_bytes=58 << 20)


def fetches(piece_refs, into_ref, sem_ref, start=0, to=0, width=None):
    width = into_ref.shape[1] if width is None else width
    copies = []
    for i, piece in enumerate(piece_refs):
        rows = piece.shape[0]
        copies.append(
            pltpu.make_async_copy(
                piece.at[:, pl.ds(start, width)],
                into_ref.at[pl.ds(i * rows, rows), pl.ds(to, width)],
                sem_ref.at[i],
            )
        )
    return copies


def at_first(*copies, start=True, wait=True):
    @pl.when(pl.program_id(0) == 0)
    def _():
        if start:
            for copy in copies:
                copy.start()
        if wait:
            for copy in copies:
                copy.wait()


def add_and_flush(total_ref, part_refs, addends):
    step = pl.program_id(0)

    @pl.when(step == 0)
    def _():
        total_ref[...] = jnp.zeros_like(total_ref)

    for lanes, addend in addends:
        total_ref[:, lanes] += addend()

    @pl.when(step == pl.num_programs(0) - 1)
    def _():
        rows = part_refs[0].shape[0]
        for i, part_ref in enumerate(part_refs):
            part_ref[...] = total_ref[i * rows : (i + 1) * rows, :].astype(BF16)


def attention_step(table_ref, gain_ref, bias_ref, cos_ref, low_ref, high_ref, *refs, permute):
    x_pieces, g_pieces, pieces, refs = refs[:8], refs[8:16], refs[16:-12], refs[-12:]
    context_ref, d_proj_ref, hidden_ref, cotan_ref, cols_ref, proj_ref, grad_ref = refs[:7]
    x_buffer, g_buffer, x_sems, g_sems, sems = refs[7:]
    step = pl.program_id(0)
    length, features = hidden_ref.shape
    half = length // 2
    blocks = table_ref.shape[0] - 1 if permute else 1
    size = features // blocks

    def start(sequence):
        slot = sequence % 2
        for i in range(2):
            side = table_ref[0] if i == 0 else 1 - table_ref[0]
            rows = pl.ds(pl.multiple_of(side * half, half), half)

            def block(j, carry, i=i, rows=rows):
                entry = table_ref[1 + j] if permute else 0
                of = pl.ds(pl.multiple_of(entry * size, size), size)
                to = pl.ds(pl.multiple_of(j * size, size), size)
                for sources, buffer, buffer_sems in (
                    (x_pieces, x_buffer, x_sems),
                    (g_pieces, g_buffer, g_sems),
                ):
                    pltpu.make_async_copy(
                        sources[2 * sequence + i].at[:, of],
                        buffer.at[slot, rows, to],
                        buffer_sems.at[slot],
                    ).start()
                return carry

            lax.fori_loop(0, blocks, block, 0)

    pl.when(step == 0)(lambda: start(0))
    for sequence in range(1, 4):
        pl.when(step == sequence - 1)(lambda sequence=sequence: start(sequence))
    columns = fetches(pieces, cols_ref, sems)
    at_first(*columns, wait=False)
    slot = lax.rem(step, 2)
    for buffer, buffer_sems in ((x_buffer, x_sems), (g_buffer, g_sems)):
        pltpu.make_async_copy(buffer.at[slot], buffer.at[slot], buffer_sems.at[slot]).wait()
    chunk = min(128, length)

    def normalize(i, carry):
        at = pl.ds(pl.multiple_of(i * chunk, chunk), chunk)
        rows = x_buffer[slot, at, :].astype(F32)
        centred = rows - jnp.mean(rows, axis=1, keepdims=True)
        inv_std = lax.rsqrt(jnp.mean(centred * centred, axis=1, keepdims=True) + EPS_NORM)
        hidden_ref[at, :] = (centred * inv_std * gain_ref[...] + bias_ref[...]).astype(BF16)
        return carry

    lax.fori_loop(0, length // chunk, normalize, 0)
    cotan_ref[...] = g_buffer[slot]
    at_first(*columns, start=False)
    width = grad_ref.shape[1]
    proj_ref[...] = dot_nn(hidden_ref[...], cols_ref[:, : 3 * width])
    grad_ref[...] = dot_nn(cotan_ref[...], cols_ref[:, 3 * width :]).astype(BF16)
    attention_body(proj_ref, grad_ref, cos_ref, low_ref, high_ref, context_ref, d_proj_ref)


def attention(table, x_pieces, g_pieces, gain, bias, pieces):
    half, features = x_pieces[0].shape
    length, tokens = 2 * half, 8 * half
    width = pieces[0].shape[1] // 4
    permute = features // (table.shape[0] - 1) % 128 == 0
    if not permute:
        x_pieces = [relative(piece, table) for piece in x_pieces]
        g_pieces = [relative(piece, table) for piece in g_pieces]

    def rows(columns):
        return pl.BlockSpec((length, columns), lambda s, h: (s, 0))

    def fixed(shape):
        return pl.BlockSpec(shape, lambda s, h: (0, 0), pipeline_mode=pl.Buffered(1))

    widths = (width, 3 * width, features, features)
    return pl.pallas_call(
        functools.partial(attention_step, permute=permute),
        grid_spec=pltpu.PrefetchScalarGridSpec(
            num_scalar_prefetch=1,
            grid=(4,),
            in_specs=[fixed((1, features))] * 2
            + [fixed((length, PAIR))] * 3
            + [ANYWHERE] * (16 + len(pieces)),
            out_specs=[rows(columns) for columns in widths],
            scratch_shapes=[
                pltpu.VMEM((features, 4 * width), BF16),
                pltpu.VMEM((length, 3 * width), F32),
                pltpu.VMEM((length, width), BF16),
                pltpu.VMEM((2, length, features), BF16),
                pltpu.VMEM((2, length, features), BF16),
                pltpu.SemaphoreType.DMA((2,)),
                pltpu.SemaphoreType.DMA((2,)),
                pltpu.SemaphoreType.DMA((len(pieces),)),
            ],
        ),
        out_shape=[jax.ShapeDtypeStruct((tokens, columns), BF16) for columns in widths],
        compiler_params=PARAMS,
        name="attention",
    )(table, gain, bias, *lane_tables(length), *x_pieces, *g_pieces, *pieces)


def parts_of(count, features, width):
    rows = features // count
    shapes = [jax.ShapeDtypeStruct((rows, width), BF16)] * count
    return [whole((rows, width))] * count, shapes, [pltpu.VMEM((features, width), F32)]


def attention_grads_step(hidden_ref, cotan_ref, d_proj_ref, context_ref, *refs):
    wide = d_proj_ref.shape[1]
    add_and_flush(
        refs[-1],
        refs[:-1],
        [
            (pl.ds(0, wide), lambda: dot_tn(hidden_ref[...], d_proj_ref[...])),
            (pl.ds(wide, wide // 3), lambda: dot_tn(cotan_ref[...], context_ref[...])),
        ],
    )


def attention_grads(hidden, cotan, d_proj, context, block, count):
    tokens, features = hidden.shape
    width = context.shape[1]
    specs, shapes, scratch = parts_of(count, features, 4 * width)
    return pl.pallas_call(
        attention_grads_step,
        grid=(tokens // block,),
        in_specs=[rows_of(block, features)] * 2 + [rows_of(block, 3 * width), rows_of(block, width)],
        out_specs=specs,
        out_shape=shapes,
        scratch_shapes=scratch,
        compiler_params=PARAMS,
        name="attention_grads",
    )(hidden, cotan, d_proj, context)


def fc1_step(hidden_ref, cotan_ref, *refs, count):
    pieces, (act_ref, slope_ref), parts = refs[:count], refs[count : count + 2], refs[count + 2 : -3]
    cols_ref, total_ref, sems = refs[-3:]
    at_first(*fetches(pieces, cols_ref, sems))
    pre = dot_nn(hidden_ref[...], cols_ref[...])
    square = pre * pre
    tanh = jnp.tanh(pre * (GELU_ROOT + GELU_ROOT * GELU_CUBE * square))
    half = 0.5 + 0.5 * tanh
    steep = pre * (GELU_ROOT + 3.0 * GELU_ROOT * GELU_CUBE * square)
    act_ref[...] = (pre * half).astype(BF16)
    slope_ref[...] = half + half * (steep * (1.0 - tanh))
    every = pl.ds(0, total_ref.shape[1])
    add_and_flush(total_ref, parts, [(every, lambda: dot_tn(cotan_ref[...], act_ref[...]))])


def fc1_pass(hidden, cotan, pieces, block):
    tokens, features = hidden.shape
    count, width = len(pieces), pieces[0].shape[1]
    specs, shapes, scratch = parts_of(count, features, width)
    act, slope, *parts = pl.pallas_call(
        functools.partial(fc1_step, count=count),
        grid=(tokens // block,),
        in_specs=[rows_of(block, features)] * 2 + [ANYWHERE] * count,
        out_specs=[rows_of(block, width)] * 2 + specs,
        out_shape=[
            jax.ShapeDtypeStruct((tokens, width), BF16),
            jax.ShapeDtypeStruct((tokens, width), F32),
            *shapes,
        ],
        scratch_shapes=[
            pltpu.VMEM((features, width), BF16),
            *scratch,
            pltpu.SemaphoreType.DMA((count,)),
        ],
        compiler_params=PARAMS,
        name="fc1_pass",
    )(hidden, cotan, *pieces)
    return act, slope, parts


def fc2_step(hidden_ref, cotan_ref, slope_ref, *refs, count):
    pieces, d_pre_ref, parts = refs[:count], refs[count], refs[count + 1 : -3]
    cols_ref, total_ref, sems = refs[-3:]
    at_first(*fetches(pieces, cols_ref, sems))
    d_pre_ref[...] = (dot_nn(cotan_ref[...], cols_ref[...]) * slope_ref[...]).astype(BF16)
    every = pl.ds(0, total_ref.shape[1])
    add_and_flush(total_ref, parts, [(every, lambda: dot_tn(hidden_ref[...], d_pre_ref[...]))])


def fc2_pass(hidden, cotan, pieces, slope, block):
    tokens, features = hidden.shape
    count, width = len(pieces), pieces[0].shape[1]
    specs, shapes, scratch = parts_of(count, features, width)
    d_pre, *parts = pl.pallas_call(
        functools.partial(fc2_step, count=count),
        grid=(tokens // block,),
        in_specs=[rows_of(block, features)] * 2 + [rows_of(block, width)] + [ANYWHERE] * count,
        out_specs=[rows_of(block, width)] + specs,
        out_shape=[jax.ShapeDtypeStruct((tokens, width), BF16), *shapes],
        scratch_shapes=[
            pltpu.VMEM((features, width), BF16),
            *scratch,
            pltpu.SemaphoreType.DMA((count,)),
        ],
        compiler_params=PARAMS,
        name="fc2_pass",
    )(hidden, cotan, slope, *pieces)
    return d_pre, parts


def back_step(table_ref, first_ref, second_ref, *refs, count, start, permute):
    attn_pieces, fc_pieces, (mine_ref, other_ref) = refs[:count], refs[count:-6], refs[-6:-4]
    rows_ref, cols_ref, attn_sems, fc_sems = refs[-4:]
    size, width = first_ref.shape[1], second_ref.shape[1]
    at_first(
        *fetches(attn_pieces, cols_ref, attn_sems, start, 0, size),
        *fetches(fc_pieces, cols_ref, fc_sems, 0, size, width),
    )
    rows_ref[:, :size] = first_ref[...]
    rows_ref[:, size:] = second_ref[...]
    out = dot_nt(rows_ref[...], cols_ref[...])
    out = out.astype(BF16)
    middle = pl.num_programs(0) // 2
    blocks = table_ref.shape[0] - 1
    size = out.shape[1] // blocks

    def store(out_ref):
        if not permute:
            out_ref[...] = out
            return
        for j in range(blocks):
            lanes = pl.ds(pl.multiple_of(table_ref[1 + j] * size, size), size)
            out_ref[:, lanes] = out[:, j * size : (j + 1) * size]

    pl.when(pl.program_id(0) < middle)(lambda: store(mine_ref))
    pl.when(pl.program_id(0) >= middle)(lambda: store(other_ref))


def back_product(table, first, second, attn_pieces, fc_pieces, start, block):
    (tokens, size), width = first.shape, second.shape[1]
    count = len(attn_pieces)
    features = count * attn_pieces[0].shape[0]
    blocks = table.shape[0] - 1
    permute = features // blocks % 128 == 0
    middle = tokens // block // 2
    outs = pl.pallas_call(
        functools.partial(back_step, count=count, start=start, permute=permute),
        grid_spec=pltpu.PrefetchScalarGridSpec(
            num_scalar_prefetch=1,
            grid=(tokens // block,),
            in_specs=[
                pl.BlockSpec((block, size), lambda s, h: (s, 0)),
                pl.BlockSpec((block, width), lambda s, h: (s, 0)),
            ]
            + [ANYWHERE] * (2 * count),
            out_specs=(
                pl.BlockSpec((block, features), lambda s, h: (jnp.minimum(s, middle - 1), 0)),
                pl.BlockSpec((block, features), lambda s, h: (jnp.maximum(s - middle, 0), 0)),
            ),
            scratch_shapes=[
                pltpu.VMEM((block, size + width), BF16),
                pltpu.VMEM((features, size + width), BF16),
                pltpu.SemaphoreType.DMA((count,)),
                pltpu.SemaphoreType.DMA((count,)),
            ],
        ),
        out_shape=(jax.ShapeDtypeStruct((tokens // 2, features), BF16),) * 2,
        compiler_params=PARAMS,
        name="back_product",
    )(table, first, second, *attn_pieces, *fc_pieces)
    if not permute:
        order = jnp.argsort(table[1:])
        cut = [out.reshape(tokens // 2, blocks, features // blocks) for out in outs]
        outs = [jnp.take(out, order, axis=1).reshape(tokens // 2, features) for out in cut]
    return outs


def adamw(weight, gradient, moment, second):
    new_m = BETA_ONE * moment + (1.0 - BETA_ONE) * gradient
    new_v = BETA_TWO * second + (1.0 - BETA_TWO) * gradient * gradient
    m_hat = new_m / (1.0 - BETA_ONE**STEP_COUNT)
    v_hat = new_v / (1.0 - BETA_TWO**STEP_COUNT)
    update = -RATE * (m_hat / (jnp.sqrt(v_hat) + ADAM_EPS) + DECAY * weight.astype(F32))
    return (gradient, update, new_m, new_v)


def shards(
    inputs,
    ln_gain,
    ln_bias,
    qkv_weight,
    out_weight,
    fc1_weight,
    fc2_weight,
    cotangent,
    m_gain,
    v_gain,
    m_bias,
    v_bias,
    m_qkv,
    v_qkv,
    m_out,
    v_out,
    m_fc1,
    v_fc1,
    m_fc2,
    v_fc2,
):
    length = 2 * inputs.shape[0]
    block = length // 2
    count = 2 * lax.axis_size("h")
    table = feature_table()

    r = inner_index()
    vectors = place_vectors(jnp.stack([ln_gain, ln_bias]))
    for axis in "yc":
        vectors = vectors + swap(vectors, axis)
    first = [
        jnp.concatenate(
            [attention_block(qkv_weight, out_weight, r ^ flip), column_block(fc1_weight, r ^ flip)],
            axis=1,
        )
        for flip in range(4)
    ]
    first = exchange_directly(first)
    fc2_cut = cut(functools.partial(column_block, fc2_weight))
    x, g = [inputs, swap(inputs, "t"), swap(inputs, "w")], [cotangent]
    x[2], vectors = lax.optimization_barrier((x[2], vectors))
    others = shifted(vectors)
    early = [swap(inputs, "c"), swap(cotangent, "c")]
    early, x, first, g, fc2_cut, vectors, others = close(
        early, x, first, g, fc2_cut, vectors, others
    )
    split = 4 * (qkv_weight.shape[2] // 4)
    attn = Gather(jnp.concatenate([piece[:, :split] for piece in first]))
    attn.over_h()
    attn.over_y_first()
    vectors = sum(others, vectors)
    x.append(swap(x[2], "t"))
    g += [swap(g[0], "t"), swap(g[0], "w")]
    fc1 = Gather(jnp.concatenate([piece[:, split:] for piece in first]))
    x, g, fc2_cut, vectors = close(attn, x, g, fc2_cut, fc1, vectors)
    fc2 = Gather(jnp.concatenate(exchange(fc2_cut)))
    fc1.over_h()
    attn.over_y_rest()
    fc1.over_y_first()
    g.append(swap(g[2], "t"))
    late = [swap(piece, "c") for piece in (*x[1:], *g[1:])]
    g, x, late, vectors = close(fc1, attn, g, fc2, x, late, vectors)
    x_other, g_other = [early[0], *late[:3]], [early[1], *late[3:]]
    fc2.over_h()
    fc2.over_y_first()
    fc1.over_y_rest()
    affine = relative(vectors, table).astype(F32)
    context, d_proj, hidden, cotan = attention(
        table, x + x_other, g + g_other, affine[:1], affine[1:], attn.pieces()
    )
    attn_parts = attention_grads(hidden, cotan, d_proj, context, block, count)
    hidden, cotan, context, d_proj, attn_parts = close(
        attn, fc1, fc2, hidden, cotan, context, d_proj, attn_parts
    )
    fc2.over_y_rest()
    attn_sum = Reduce(attn_parts)
    attn_sum.over_y_rest()
    act, slope, fc2_parts = fc1_pass(hidden, cotan, fc1.pieces(), block)
    hidden, cotan, context, d_proj, act, slope, fc2_parts = close(attn, fc1, fc2, attn_sum, hidden, cotan, context, d_proj, act, slope, fc2_parts)
    attn_sum.over_h()
    attn_sum.over_y_first()
    fc2_sum = Reduce(fc2_parts)
    fc2_sum.over_y_rest()
    start = d_proj.shape[1]
    d_pre, fc1_parts = fc2_pass(hidden, cotan, fc2.pieces(), slope, block)
    d_hidden = GroupSum(back_product(table, d_proj, d_pre, attn.pieces(), fc1.pieces(), 0, block))
    context, act, fc1_parts = close(attn, fc2, attn_sum, fc2_sum, d_hidden, context, act, fc1_parts)
    fc2_sum.over_h()
    fc2_sum.over_y_first()
    fc1_sum = Reduce(fc1_parts)
    fc1_sum.over_y_rest()
    d_hidden.over_c()
    d_hidden.corner()
    branch = GroupSum(back_product(table, context, act, attn.pieces(), fc2.pieces(), start, block))
    attn_pieces = collect(attn_sum.total())
    (attn_pieces,) = close(attn_pieces, fc1_sum, fc2_sum, d_hidden, branch)
    fc1_sum.over_h()
    fc1_sum.over_y_first()
    d_hidden.edges()
    branch.over_c()
    branch.corner()
    qkv_grad, out_grad = join_attention(attn_pieces)
    qkv_res = adamw(qkv_weight, qkv_grad, m_qkv, v_qkv)
    out_res = adamw(out_weight, out_grad, m_out, v_out)
    fc2_total = fc2_sum.total()
    (fc2_total,) = close(fc1_sum, d_hidden, branch, fc2_total)
    d_hidden = d_hidden.total()
    own_rows = inputs.astype(F32)
    centred = own_rows - jnp.mean(own_rows, axis=1, keepdims=True)
    inv_std = lax.rsqrt(jnp.mean(centred * centred, axis=1, keepdims=True) + EPS_NORM)
    normed = centred * inv_std
    sums = jnp.stack([jnp.sum(d_hidden * normed, axis=0), jnp.sum(d_hidden, axis=0)])
    scaled_grad = d_hidden * vectors[:1].astype(F32)
    input_grad = cotangent.astype(F32) + inv_std * (
        scaled_grad
        - jnp.mean(scaled_grad, axis=1, keepdims=True)
        - normed * jnp.mean(scaled_grad * normed, axis=1, keepdims=True)
    )
    fc1_pieces, fc2_pieces = collect(fc1_sum.total()), collect(fc2_total)
    for axis in "cyt":
        sums = sums + swap(sums, axis)
    sums, branch.across, branch.beside, input_grad = lax.optimization_barrier(
        (sums, branch.across, branch.beside, input_grad)
    )
    branch.edges()
    fc1_res = adamw(fc1_weight, join_columns(fc1_pieces), m_fc1, v_fc1)
    fc2_res = adamw(fc2_weight, join_columns(fc2_pieces), m_fc2, v_fc2)
    fc1_res, sums = lax.optimization_barrier((fc1_res, sums))
    others = shifted(sums)
    fc1_res, fc2_res, others, input_grad = close(
        fc1_res, fc2_res, branch, others, input_grad
    )
    output = (own_rows + branch.total()).astype(BF16)
    sums = own_part(sum(others, sums))
    gain_res = adamw(ln_gain, sums[0], m_gain, v_gain)
    bias_res = adamw(ln_bias, sums[1], m_bias, v_bias)
    return (
        output,
        input_grad,
        *gain_res,
        *bias_res,
        *qkv_res,
        *out_res,
        *fc1_res,
        *fc2_res,
    )


def solution(mesh):
    dp, tensor = mesh.devices.shape
    inner = Mesh(mesh.devices.reshape(dp // 8, 2, 2, 2, tensor), ("h", "w", "y", "c", "t"))
    rows = P(("h", "w", "y", "c", "t"), None)
    vector = P(("h", "w", "y", "c"))
    stack = P(None, ("h", "w", "y", "c"), "t")
    matrix = P(("h", "w", "y", "c"), "t")
    return jax.shard_map(
        shards,
        mesh=inner,
        in_specs=(rows, vector, vector, stack, matrix, matrix, matrix, rows)
        + (vector,) * 4
        + (stack,) * 2
        + (matrix,) * 6,
        out_specs=(rows, rows) + (vector,) * 8 + (stack,) * 4 + (matrix,) * 12,
        check_vma=False,
    )
```
